512 devices in a mesh: seq: 32 (over z, core), head: 16 (over x, y).
Axes of the slice: x: 4, y: 4, z: 16, core: 2. Of those that a mesh axis runs over, the one named last changes fastest.
Arguments:
- queries: bfloat16 [65536, 2048], P(('seq', 'head')), may hold values from -6 to 6
- keys: bfloat16 [65536, 2048], P(('seq', 'head')), may hold values from -6 to 6
- values: bfloat16 [65536, 4096], P(('seq', 'head')), may hold values from -6 to 6
- input_pre: float32 [65536, 8], P(('seq', 'head')), may hold values from -4 to 97
- forget_pre: float32 [65536, 8], P(('seq', 'head')), may hold values from 0 to 16
Outputs:
- cell_output: bfloat16 [65536, 4096], P('seq', 'head')
The draws below stay inside these ranges and needn't reach their ends.
All inputs are finite; a program needn't handle non-finite values.
Results may differ from the reference program's by a relative error of at most 0.0028.
Values may be sent and summed in bfloat16 or wider, within the bound.
No kernel may reach another device: no remote copies, remote signals or barrier semaphores. Data moves between devices by JAX's collectives and lax.ppermute only.
A program may use at most 64 MiB of HBM per device.

```python
import math
import jax
import jax.numpy as jnp
from jax import lax

HEAD_TOTAL = 8
DQK = 256
DV = 512
GROUP = 64
TOK_SEQ = 2048
SEQUENCE_TOKENS = 65536


def draw_forget_pre(key, part):
    every_key_row = jax.random.split(jax.random.fold_in(key, 11), 5)
    head_order = jax.random.permutation(every_key_row[0], HEAD_TOTAL)
    fast_heads = HEAD_TOTAL // 2
    is_fast = head_order < fast_heads
    base_rate = jnp.where(is_fast, 1.0 / 40.0, 0.4 / SEQUENCE_TOKENS).astype(jnp.float32)
    shard_blocks = SEQUENCE_TOKENS // TOK_SEQ
    shard_factor = jnp.exp(jax.random.uniform(every_key_row[1], (shard_blocks, HEAD_TOTAL), jnp.float32, math.log(0.5), math.log(2.0)))
    shard_factor = jnp.repeat(shard_factor, TOK_SEQ, axis=0)
    roughness = jax.random.uniform(every_key_row[2], (SEQUENCE_TOKENS, HEAD_TOTAL), jnp.float32, 0.5, 1.5)
    step_rate = base_rate[None, :] * shard_factor * roughness
    forget_gate_logit = -jnp.log(jnp.expm1(step_rate))
    surge_location = jax.random.randint(every_key_row[3], (2, HEAD_TOTAL), 0, SEQUENCE_TOKENS)
    surge_retain = jax.random.uniform(every_key_row[4], (2, HEAD_TOTAL), jnp.float32, 0.5, 0.8)
    surge_logit_value = jnp.log(surge_retain / (1.0 - surge_retain))
    token_position = jnp.arange(SEQUENCE_TOKENS)[:, None]
    for surge_index in range(2):
        forget_gate_logit = jnp.where(token_position == surge_location[surge_index][None, :], surge_logit_value[surge_index][None, :], forget_gate_logit)
    return forget_gate_logit.astype(jnp.float32)


def draw_input_pre(key, part):
    every_key_row = jax.random.split(jax.random.fold_in(key, 23), 1)
    jitter = jax.random.uniform(every_key_row[0], (SEQUENCE_TOKENS, HEAD_TOTAL), jnp.float32, -4.0, 4.0)
    gate_value = jitter
    return gate_value.astype(jnp.float32)


def level_of(key, extent, pieces, least, high):
    def one(axis_at, parts):
        heights = jax.random.uniform(jax.random.fold_in(jax.random.fold_in(key, 6), axis_at), (parts,), jnp.float32, least / len(pieces), high / len(pieces))
        return jnp.repeat(jnp.exp(heights), extent[axis_at] // parts).reshape((-1,) + (1,) * (len(extent) - axis_at - 1))

    gain = one(*pieces[0])
    for cut in pieces[1:]:
        gain = gain * one(*cut)
    return gain


def gaussian(key, dims, deviation, limit, pieces=(), kind=jnp.bfloat16):
    drawn = deviation * jax.random.normal(key, dims, jnp.float32)
    if pieces:
        drawn = drawn * level_of(key, dims, pieces, -0.22, 0.18)
    return jnp.clip(drawn, -limit, limit).astype(kind)


def setup_inputs(seed: int = 0) -> dict:
    splits = jax.random.split(jax.random.key(seed), 6)
    queries = gaussian(splits[0], (SEQUENCE_TOKENS, HEAD_TOTAL * DQK), 1.0, 6.0, ((0, 512),))
    keys = gaussian(splits[1], (SEQUENCE_TOKENS, HEAD_TOTAL * DQK), 1.0, 6.0, ((0, 512),))
    values = gaussian(splits[2], (SEQUENCE_TOKENS, HEAD_TOTAL * DV), 1.0, 6.0, ((0, 512),))
    input_pre = draw_input_pre(jax.random.fold_in(splits[5], 71), 0)
    forget_pre = draw_forget_pre(jax.random.fold_in(splits[5], 71), 0)
    return {"queries": queries, "keys": keys, "values": values, "input_pre": input_pre, "forget_pre": forget_pre}


VERY_NEGATIVE = -1.0e30
HIGHEST = lax.Precision.HIGHEST


def combine(earlier, latter):
    carry_c, carry_n, carry_m, carry_f = earlier
    fresh_c, fresh_n, fresh_m, fresh_f = latter
    joined_m = jnp.maximum(carry_m + fresh_f, fresh_m)
    keep_old = jnp.exp(carry_m + fresh_f - joined_m)
    keep_new = jnp.exp(fresh_m - joined_m)
    return (keep_old[..., None, None] * carry_c + keep_new[..., None, None] * fresh_c,
            keep_old[..., None] * carry_n + keep_new[..., None] * fresh_n,
            joined_m, carry_f + fresh_f)


def group_parts(piece_block):
    query_rows, key_rows, value_rows, gate_in, log_forget = piece_block
    group_width = query_rows.shape[0]
    cumulated = jnp.cumsum(log_forget, axis=0)
    overall = cumulated[-1]
    places = jnp.arange(group_width)
    causal = (places[:, None] >= places[None, :])[:, :, None]
    gap_table = jnp.where(causal, cumulated[:, None, :] - cumulated[None, :, :] + gate_in[None, :, :], VERY_NEGATIVE)
    tail_gap = overall[None, :] - cumulated + gate_in
    return cumulated, overall, gap_table, tail_gap


def group_summary(piece_block):
    query_rows, key_rows, value_rows, gate_in, log_forget = piece_block
    cumulated, overall, gap_table, tail_gap = group_parts(piece_block)
    tail_top = jnp.max(tail_gap, axis=0)
    scaled_keys = key_rows.astype(jnp.float32) * jnp.exp(tail_gap - tail_top[None, :])[:, :, None]
    matrix = jnp.einsum("spd,spe->pde", scaled_keys, value_rows.astype(jnp.float32), precision=HIGHEST)
    return (matrix, jnp.sum(scaled_keys, axis=0), tail_top, overall)


def group_output(running_state, piece_block):
    query_rows, key_rows, value_rows, gate_in, log_forget = piece_block
    matrix, normal, stabilizer, unused_decay = running_state
    cumulated, overall, gap_table, tail_gap = group_parts(piece_block)
    factor = query_rows.shape[-1] ** -0.5
    carried = cumulated + stabilizer[None, :]
    running = jnp.maximum(carried, jnp.max(gap_table, axis=1))
    inside = jnp.exp(gap_table - running[:, None, :])
    outside = jnp.exp(carried - running)
    query_wide = query_rows.astype(jnp.float32)
    scores = jnp.einsum("tpd,spd->tsp", query_wide, key_rows.astype(jnp.float32), precision=HIGHEST) * factor
    weighted = inside * scores
    numerator = jnp.einsum("tsp,spe->tpe", weighted, value_rows.astype(jnp.float32), precision=HIGHEST)
    numerator = numerator + outside[:, :, None] * jnp.einsum("tpd,pde->tpe", query_wide, matrix, precision=HIGHEST) * factor
    denominator = jnp.sum(weighted, axis=1) + outside * jnp.einsum("tpd,pd->tp", query_wide, normal, precision=HIGHEST) * factor
    return (numerator / jnp.maximum(jnp.abs(denominator), 1.0)[:, :, None]).astype(jnp.bfloat16)


def reference(queries, keys, values, input_pre, forget_pre):
    tok_total = queries.shape[0]
    group_count = tok_total // GROUP
    blocks = (queries.reshape(group_count, GROUP, HEAD_TOTAL, DQK),
              keys.reshape(group_count, GROUP, HEAD_TOTAL, DQK),
              values.reshape(group_count, GROUP, HEAD_TOTAL, DV),
              input_pre.reshape(group_count, GROUP, HEAD_TOTAL),
              jax.nn.log_sigmoid(forget_pre).reshape(group_count, GROUP, HEAD_TOTAL))
    start_state = (jnp.zeros((HEAD_TOTAL, DQK, DV), jnp.float32), jnp.zeros((HEAD_TOTAL, DQK), jnp.float32),
                   jnp.full((HEAD_TOTAL,), VERY_NEGATIVE, jnp.float32), jnp.zeros((HEAD_TOTAL,), jnp.float32))

    def advance(running_state, piece_block):
        emitted = group_output(running_state, piece_block)
        return combine(running_state, group_summary(piece_block)), emitted

    unused_final, outputs = lax.scan(advance, start_state, blocks)
    return outputs.reshape(tok_total, HEAD_TOTAL * DV)
```

```python
import jax
import jax.numpy as jnp
from jax import lax
from jax.experimental import pallas as pl
from jax.experimental.pallas import tpu as pltpu
from jax.sharding import PartitionSpec as P

VERY_NEGATIVE = -1e30
CHUNK = 256
EXTRA = 128
GATE_ROWS = 8
F32 = jnp.float32
BF16 = jnp.bfloat16
F16 = jnp.float16


def dot(a, b, contract):
    return lax.dot_general(a, b, ((contract[:1], contract[1:]), ((), ())), preferred_element_type=F32)


def halves(x):
    top = x.astype(BF16)
    return top, (x - top.astype(F32)).astype(BF16)


def thirds(x, scale):
    first = x.astype(BF16).astype(F32)
    rest = (x - first) * scale
    second = rest.astype(BF16).astype(F32)
    third = ((rest - second) * scale).astype(BF16).astype(F32)
    return first, second, third


def iota(shape, dim):
    return lax.broadcasted_iota(jnp.int32, shape, dim)


def pack_kernel(k_ref, v_ref, gate_ref, forget_ref, out_ref, parts_ref):
    head = pl.program_id(0)
    rows, width = k_ref.shape

    @pl.when(head == 0)
    def _():
        decay = -jnp.log1p(jnp.exp(-forget_ref[...]))
        for n, x in enumerate((decay.T, gate_ref[...].T)):
            for p, part in enumerate(thirds(x, 1.0)):
                parts_ref[3 * n + p] = part

    row = iota((GATE_ROWS, rows), 0)
    block = []
    for n in range(2):
        area = jnp.zeros((GATE_ROWS, rows), F32)
        for p in range(3):
            area = jnp.where(row == p, parts_ref[3 * n + p, pl.ds(head, 1), :], area)
        block.append(area)
    gates = jnp.concatenate(block, axis=1).astype(BF16)
    for u in range(2):
        out_ref[u, 0:rows, 0:width] = k_ref[...]
        out_ref[u, 0:rows, width : 2 * width] = v_ref[:, u * width : (u + 1) * width]
        out_ref[u, rows : rows + GATE_ROWS, :] = jnp.zeros((GATE_ROWS, 2 * width), BF16)
        out_ref[u, rows : rows + GATE_ROWS, 0 : 2 * rows] = gates


def twice_kernel(q_ref, out_ref):
    for u in range(2):
        out_ref[u] = q_ref[...]


def state_kernel(r_ref, entry_top_ref, entry_low_ref, aux_ref, z_ref, c_ref, n_ref, m_ref, f_ref):
    step = pl.program_id(0)
    sources, rows = r_ref.shape[0], r_ref.shape[1] - GATE_ROWS
    width = c_ref.shape[0]

    @pl.when(step == 0)
    def _():
        c_ref[...] = jnp.zeros_like(c_ref)
        n_ref[...] = jnp.zeros_like(n_ref)
        m_ref[...] = jnp.full_like(m_ref, VERY_NEGATIVE)
        f_ref[...] = jnp.zeros_like(f_ref)

    entry_top, entry_low = halves(c_ref[...])
    entry_top_ref[0] = entry_top
    entry_low_ref[0] = entry_low

    gates = [r_ref[b, rows : rows + GATE_ROWS, 0 : 2 * rows] for b in range(sources)]
    decay = jnp.concatenate([g[:, 0:rows] for g in gates], axis=1)
    gate = jnp.concatenate([g[:, rows:] for g in gates], axis=1).astype(F32)
    gate = gate[0:1] + gate[1:2] + gate[2:3]
    upper = (iota((CHUNK, CHUNK), 0) <= iota((CHUNK, CHUNK), 1)).astype(BF16)
    cum = dot(decay, upper, (1, 0))
    cum = cum[0:1] + cum[1:2] + cum[2:3]
    total = cum[:, CHUNK - 1 : CHUNK]
    tail = total - cum + gate
    old_m = m_ref[0:1, 0:1]
    new_m = jnp.maximum(old_m + total, jnp.max(tail, axis=1, keepdims=True))
    keep = jnp.exp(old_m + total - new_m)
    weight = jnp.exp(tail - new_m)

    row = iota((8, CHUNK), 0)
    aux = jnp.where(row == 0, n_ref[0:1, :], 0.0)
    for p, x in ((1, old_m), (2, f_ref[0:1, 0:1]), (3, cum), (4, gate)):
        aux = jnp.where(row == p, x, aux)
    aux_ref[0] = aux

    column = jnp.where(row == 0, weight, 0.0).T[:, 0:1]
    keys = r_ref[:, 0:rows, 0:width].reshape(CHUNK, width).astype(F32) * column
    values = r_ref[:, 0:rows, width:].reshape(CHUNK, width)
    keys_top, keys_low = halves(keys)
    c_new = keep * c_ref[...] + dot(keys_top, values, (0, 0)) + dot(keys_low, values, (0, 0))
    n_new = keep * n_ref[0:1, :] + jnp.sum(keys, axis=0, keepdims=True)
    f_new = f_ref[0:1, 0:1] + total
    c_ref[...] = c_new
    n_ref[0:1, :] = n_new
    m_ref[...] = jnp.broadcast_to(new_m, m_ref.shape)
    f_ref[...] = jnp.broadcast_to(f_new, f_ref.shape)

    @pl.when(step == pl.num_programs(0) - 1)
    def _():
        count, slab = z_ref.shape[0], z_ref.shape[1]
        most = jnp.max(jnp.max(jnp.abs(c_new), axis=1, keepdims=True), axis=0, keepdims=True)
        scaled = c_new * jnp.where(most > 0.0, 1.0 / most, 0.0)
        z_ref[:, :, 0:width] = scaled.reshape(count, slab, width)
        place = iota((slab, EXTRA), 0)
        lane = iota((slab, EXTRA), 1)
        extra = jnp.zeros((slab, EXTRA), F32)
        for p, part in enumerate(thirds(n_new, 256.0)):
            for h in range(width // EXTRA):
                extra = jnp.where(place == 2 * p + h, part[:, h * EXTRA : (h + 1) * EXTRA], extra)
        for n, x in enumerate((new_m, f_new, most * 0.25)):
            for p, part in enumerate(thirds(x, 256.0)):
                extra = jnp.where((place == 6) & (lane == 3 * n + p), part, extra)
        z_ref[:, :, width:] = jnp.broadcast_to(extra[None], (count, slab, EXTRA))


def prefix_kernel(own_ref, z_ref, y_ref, nin_ref):
    slab, count, wide = z_ref.shape
    width = wide - EXTRA
    own = own_ref[0]

    def joined(a, b, c):
        return a + (b + c * (1.0 / 256.0)) * (1.0 / 256.0)

    scalars = z_ref[6, :, width:]
    m, f, most = (joined(*(scalars[:, 3 * n + p : 3 * n + p + 1] for p in range(3))) for n in range(3))
    most = most * 4.0
    shard = iota((count, EXTRA), 0)
    later = iota((count, EXTRA), 1)
    gap = jnp.zeros((count, EXTRA), F32)
    for j in range(count):
        gap = jnp.where((shard < j) & (later > j), gap + f[j : j + 1, :], gap)
    before = shard < later
    reach = jnp.where(before, m + gap, VERY_NEGATIVE)
    top = jnp.max(reach, axis=0, keepdims=True)
    weight = jnp.where(before, jnp.exp(reach - top), 0.0)
    heavy = weight * most
    bound = jnp.sum(heavy, axis=0, keepdims=True)
    heavy = heavy * jnp.where(bound > 0.0, 1.0 / bound, 0.0)
    heavy_top, heavy_low = halves(heavy)
    both = jnp.concatenate([heavy_top, heavy_low], axis=1)
    for r in range(slab):
        x_top, x_low = halves(z_ref[r, :, 0:width])
        y = dot(both, x_top, (0, 0))
        y = y[0:count] + y[EXTRA : EXTRA + count] + dot(heavy_top, x_low, (0, 0))[0:count]
        y_ref[r] = y

    mine = iota((1, EXTRA), 1) == own
    column = jnp.sum(jnp.where(mine, weight, 0.0), axis=1, keepdims=True)
    row = iota((8, EXTRA), 0)
    own_top = jnp.sum(jnp.where(mine, top, 0.0), axis=1, keepdims=True)
    own_bound = jnp.sum(jnp.where(mine, bound, 0.0), axis=1, keepdims=True)
    for h in range(width // EXTRA):
        n = joined(*(z_ref[2 * p + h, :, width:] for p in range(3)))
        n = jnp.sum(column * n, axis=0, keepdims=True)
        area = jnp.where(row == 0, n, jnp.where(row == 1, own_top, own_bound))
        nin_ref[:, h * EXTRA : (h + 1) * EXTRA] = area


def inside_kernel(q_ref, r_ref, entry_top_ref, entry_low_ref, aux_ref, num_ref, col_ref):
    rows = q_ref.shape[1]
    width = q_ref.shape[2]
    factor = width**-0.5
    queries = q_ref[...].reshape(CHUNK, width)
    keys = r_ref[:, 0:rows, 0:width].reshape(CHUNK, width)
    values = r_ref[:, 0:rows, width:].reshape(CHUNK, width)
    aux = aux_ref[0]
    turned = aux.T
    cum_column = turned[:, 3:4]
    old_m = aux[1:2, 0:1]
    start = aux[2:3, 0:1]
    score = dot(queries, keys, (1, 1))
    causal = iota((CHUNK, CHUNK), 0) >= iota((CHUNK, CHUNK), 1)
    gap = jnp.where(causal, cum_column + (aux[4:5] - aux[3:4]), VERY_NEGATIVE)
    carried = cum_column + old_m
    top = jnp.maximum(carried, jnp.max(gap, axis=1, keepdims=True))
    weighted = jnp.exp(gap - top) * (score * factor)
    outside = jnp.exp(carried - top) * factor
    weighted_top, weighted_low = halves(weighted)
    num = dot(weighted_top, values, (1, 0)) + dot(weighted_low, values, (1, 0))
    num = num + outside * (
        dot(queries, entry_top_ref[0], (1, 0)) + dot(queries, entry_low_ref[0], (1, 0))
    )
    reached = jnp.sum(queries.astype(F32) * aux[0:1], axis=1, keepdims=True)
    den = jnp.sum(weighted, axis=1, keepdims=True) + outside * reached
    num_ref[...] = num
    lane = iota((CHUNK, EXTRA), 1)
    col_ref[...] = jnp.where(lane == 0, top, jnp.where(lane == 1, den, cum_column + start))


def finish_kernel(q_ref, num_ref, col_ref, c_ref, nin_ref, out_ref, top_ref, low_ref):
    width = q_ref.shape[2]
    count = q_ref.shape[0] * q_ref.shape[1]
    factor = width**-0.5

    @pl.when(pl.program_id(0) == 0)
    def _():
        top, low = halves(c_ref[...])
        top_ref[...] = top
        low_ref[...] = low

    queries = q_ref[...].reshape(count, width)
    cols = col_ref[...]
    m, den, cum = cols[:, 0:1], cols[:, 1:2], cols[:, 2:3]
    before_m = nin_ref[1:2, 0:1]
    bound = nin_ref[2:3, 0:1]
    carried = cum + before_m
    new_m = jnp.maximum(m, carried)
    inside = jnp.exp(m - new_m)
    outside = jnp.exp(carried - new_m) * factor
    reached = jnp.sum(queries.astype(F32) * nin_ref[0:1, :], axis=1, keepdims=True)
    den = den * inside + outside * reached
    over = 1.0 / jnp.maximum(jnp.abs(den), 1.0)
    read = dot(queries, top_ref[...], (1, 0)) + dot(queries, low_ref[...], (1, 0))
    out_ref[...] = (num_ref[...] * (inside * over) + read * (outside * bound * over)).astype(BF16)


def whole(shape):
    return pl.BlockSpec(shape, lambda i: (0,) * len(shape))


def stepped(shape, at=0):
    return pl.BlockSpec(shape, lambda i: tuple(i if d == at else 0 for d in range(len(shape))))


def on_device(queries, keys, values, input_pre, forget_pre):
    rows = queries.shape[0]
    heads = input_pre.shape[1]
    pieces = lax.axis_size("head")
    shards = lax.axis_size("seq")
    width = queries.shape[1] // heads
    tokens = pieces * rows
    steps = tokens // CHUNK
    group = CHUNK // rows
    tall = rows + GATE_ROWS
    slab = width // shards

    packed = pl.pallas_call(
        pack_kernel,
        grid=(heads,),
        in_specs=[
            stepped((rows, width), 1),
            stepped((rows, 2 * width), 1),
            whole((rows, heads)),
            whole((rows, heads)),
        ],
        out_specs=stepped((2, tall, 2 * width)),
        out_shape=jax.ShapeDtypeStruct((pieces, tall, 2 * width), BF16),
        scratch_shapes=[pltpu.VMEM((6, heads, rows), F32)],
        name="pack",
    )(keys, values, input_pre, forget_pre)
    doubled = pl.pallas_call(
        twice_kernel,
        grid=(heads,),
        in_specs=[stepped((rows, width), 1)],
        out_specs=stepped((2, rows, width)),
        out_shape=jax.ShapeDtypeStruct((pieces, rows, width), BF16),
        name="twice",
    )(queries)

    with jax.named_scope("kv"):
        received = lax.all_to_all(packed, "head", split_axis=0, concat_axis=0, tiled=True)
    with jax.named_scope("q"):
        asked = lax.all_to_all(doubled, "head", split_axis=0, concat_axis=0, tiled=True)

    entry_top, entry_low, aux, summary = pl.pallas_call(
        state_kernel,
        grid=(steps,),
        in_specs=[stepped((group, tall, 2 * width))],
        out_specs=[
            stepped((1, width, width)),
            stepped((1, width, width)),
            stepped((1, 8, CHUNK)),
            whole((shards, slab, width + EXTRA)),
        ],
        out_shape=[
            jax.ShapeDtypeStruct((steps, width, width), BF16),
            jax.ShapeDtypeStruct((steps, width, width), BF16),
            jax.ShapeDtypeStruct((steps, 8, CHUNK), F32),
            jax.ShapeDtypeStruct((shards, slab, width + EXTRA), F32),
        ],
        scratch_shapes=[
            pltpu.VMEM((width, width), F32),
            pltpu.VMEM((8, width), F32),
            pltpu.VMEM((8, EXTRA), F32),
            pltpu.VMEM((8, EXTRA), F32),
        ],
        name="state",
    )(received)

    with jax.named_scope("spread"):
        spread = lax.all_to_all(summary.astype(F16), "seq", split_axis=0, concat_axis=0, tiled=True)

    own = lax.axis_index("seq").astype(jnp.int32).reshape(1)
    before, normal = pl.pallas_call(
        prefix_kernel,
        in_specs=[
            pl.BlockSpec(memory_space=pltpu.SMEM),
            pl.BlockSpec(memory_space=pltpu.VMEM),
        ],
        out_specs=[pl.BlockSpec(memory_space=pltpu.VMEM), pl.BlockSpec(memory_space=pltpu.VMEM)],
        out_shape=[
            jax.ShapeDtypeStruct((slab, shards, width), F32),
            jax.ShapeDtypeStruct((8, width), F32),
        ],
        name="prefix",
    )(own, jnp.swapaxes(spread, 0, 1).astype(F32))

    with jax.named_scope("back"):
        back = lax.all_to_all(
            jnp.swapaxes(before, 0, 1).astype(F16), "seq", split_axis=0, concat_axis=0, tiled=True
        )

    num, cols = pl.pallas_call(
        inside_kernel,
        grid=(steps,),
        in_specs=[
            stepped((group, rows, width)),
            stepped((group, tall, 2 * width)),
            stepped((1, width, width)),
            stepped((1, width, width)),
            stepped((1, 8, CHUNK)),
        ],
        out_specs=[stepped((CHUNK, width)), stepped((CHUNK, EXTRA))],
        out_shape=[
            jax.ShapeDtypeStruct((tokens, width), F32),
            jax.ShapeDtypeStruct((tokens, EXTRA), F32),
        ],
        name="inside",
    )(asked, received, entry_top, entry_low, aux)

    return pl.pallas_call(
        finish_kernel,
        grid=(steps // 2,),
        in_specs=[
            stepped((2 * group, rows, width)),
            stepped((2 * CHUNK, width)),
            stepped((2 * CHUNK, EXTRA)),
            whole((width, width)),
            whole((8, width)),
        ],
        out_specs=stepped((2 * CHUNK, width)),
        out_shape=jax.ShapeDtypeStruct((tokens, width), BF16),
        scratch_shapes=[pltpu.VMEM((width, width), BF16), pltpu.VMEM((width, width), BF16)],
        name="finish",
    )(asked, num, cols, back.reshape(width, width).astype(F32), normal)


def solution(mesh):
    spec = P(("seq", "head"), None)
    return jax.shard_map(
        on_device, mesh=mesh, in_specs=(spec,) * 5, out_specs=P("seq", "head"), check_vma=False
    )
```

```python
import jax
import jax.numpy as jnp
from jax import lax
from jax.experimental import pallas as pl
from jax.experimental.pallas import tpu as pltpu
from jax.sharding import PartitionSpec as P

VERY_NEGATIVE = -1e30
CHUNK = 256
PIECE = 256
PACK_STEPS = 4
EXTRA = 128
GATE_ROWS = 8
F32 = jnp.float32
BF16 = jnp.bfloat16
F16 = jnp.float16


def dot(a, b, contract):
    return lax.dot_general(a, b, ((contract[:1], contract[1:]), ((), ())), preferred_element_type=F32)


def halves(x):
    top = x.astype(BF16)
    return top, (x - top.astype(F32)).astype(BF16)


def thirds(x, scale):
    first = x.astype(BF16).astype(F32)
    rest = (x - first) * scale
    second = rest.astype(BF16).astype(F32)
    third = ((rest - second) * scale).astype(BF16).astype(F32)
    return first, second, third


def iota(shape, dim):
    return lax.broadcasted_iota(jnp.int32, shape, dim)


def pack_kernel(q_ref, k_ref, v_ref, gate_ref, forget_ref, out_ref, parts_ref):
    at = pl.program_id(0)
    rows = k_ref.shape[0]
    heads = k_ref.shape[1] // PIECE

    @pl.when(at == 0)
    def _():
        decay = -jnp.log1p(jnp.exp(-forget_ref[...]))
        for n, x in enumerate((decay, gate_ref[...])):
            for p, part in enumerate(thirds(x, 1.0)):
                parts_ref[3 * n + p] = part

    row = iota((GATE_ROWS, rows), 0)
    for h in range(heads):
        area = jnp.zeros((GATE_ROWS, rows), F32)
        for p in range(6):
            area = jnp.where(row == p, parts_ref[p, pl.ds(at * heads + h, 1), :], area)
        area = area.astype(BF16)
        turned = q_ref[:, h * PIECE : (h + 1) * PIECE].T
        for u in range(2):
            n = 2 * h + u
            out_ref[n, 0:PIECE, :] = turned
            out_ref[n, PIECE : 2 * PIECE, :] = v_ref[:, n * PIECE : (n + 1) * PIECE].T
            for c in range(PIECE // rows):
                out_ref[n, 2 * PIECE + c * rows : 2 * PIECE + (c + 1) * rows, :] = k_ref[
                    :, h * PIECE + c * rows : h * PIECE + (c + 1) * rows
                ]
            out_ref[n, 3 * PIECE : 3 * PIECE + GATE_ROWS, :] = area


def beside(ref, blocks=None):
    return jnp.concatenate([ref[b] for b in blocks or range(ref.shape[0])], axis=1)


def key_rows(ref, blocks=None):
    rows = ref.shape[2]
    return jnp.concatenate(
        [
            jnp.concatenate([ref[b, c : c + rows, :] for c in range(0, PIECE, rows)], axis=1)
            for b in blocks or range(ref.shape[0])
        ],
        axis=0,
    )


def weighted_values(turned, weight):
    top, low = halves(turned.astype(F32) * weight)
    first, second, third = thirds(weight, 1.0)
    row = iota((8, weight.shape[1]), 0)
    left = jnp.where(row == 0, first, jnp.where(row == 1, third, 0.0)).astype(BF16)
    right = jnp.where(row == 0, second, 0.0).astype(BF16)
    return jnp.concatenate(
        [jnp.concatenate([top, left], axis=0), jnp.concatenate([low, right], axis=0)], axis=1
    )


def summary_kernel(v_ref, k_ref, g_ref, z_ref):
    sources, rows = v_ref.shape[0], v_ref.shape[2]
    decay = [g_ref[:, p, :] for p in range(3)]
    gate = [g_ref[:, 3 + p, :].astype(F32) for p in range(3)]
    gate = gate[0] + gate[1] + gate[2]
    after = (iota((rows, rows), 0) > iota((rows, rows), 1)).astype(BF16)
    later = (iota((sources, sources), 1) > iota((sources, sources), 0)).astype(BF16)
    suffix = sum(dot(d, after, (1, 0)) for d in decay)
    rest = sum(dot(later, d, (1, 0)) for d in decay)
    total = sum(jnp.sum(d.astype(F32), axis=0, keepdims=True) for d in decay)
    total = jnp.sum(total, axis=1, keepdims=True)
    tail = suffix + jnp.sum(rest, axis=1, keepdims=True) + gate
    new_m = jnp.max(jnp.max(tail, axis=1, keepdims=True), axis=0, keepdims=True)
    weight = jnp.exp(tail - new_m)
    state = jnp.zeros((PIECE + 8, PIECE), F32)
    group = CHUNK // rows
    for g in range(sources // group):
        mine = range(g * group, (g + 1) * group)
        turned = beside(v_ref, mine)
        share = jnp.concatenate([weight[b : b + 1, :] for b in mine], axis=1)
        keys = key_rows(k_ref, mine)
        state = state + dot(
            weighted_values(turned, share), jnp.concatenate([keys, keys], axis=0), (1, 0)
        )
    c_new = state[0:PIECE]
    n_new = state[PIECE : PIECE + 1] + state[PIECE + 1 : PIECE + 2]

    count, slab = z_ref.shape[0], z_ref.shape[1]
    most = jnp.max(jnp.max(jnp.abs(c_new), axis=1, keepdims=True), axis=0, keepdims=True)
    scaled = c_new * jnp.where(most > 0.0, 1.0 / most, 0.0)
    z_ref[:, :, 0:PIECE] = scaled.reshape(count, slab, PIECE)
    place = iota((slab, EXTRA), 0)
    lane = iota((slab, EXTRA), 1)
    extra = jnp.zeros((slab, EXTRA), F32)
    for p, part in enumerate(thirds(n_new, 256.0)):
        for h in range(PIECE // EXTRA):
            extra = jnp.where(place == 2 * p + h, part[:, h * EXTRA : (h + 1) * EXTRA], extra)
    for n, x in enumerate((new_m, total, most * 0.25)):
        for p, part in enumerate(thirds(x, 256.0)):
            extra = jnp.where((place == 6) & (lane == 3 * n + p), part, extra)
    z_ref[:, :, PIECE:] = jnp.broadcast_to(extra[None], (count, slab, EXTRA))


def entries_kernel(v_ref, k_ref, g_ref, top_ref, low_ref, aux_ref, c_ref, n_ref, m_ref, f_ref):
    step = pl.program_id(0)

    @pl.when(step == 0)
    def _():
        c_ref[...] = jnp.zeros_like(c_ref)
        n_ref[...] = jnp.zeros_like(n_ref)
        m_ref[...] = jnp.full_like(m_ref, VERY_NEGATIVE)
        f_ref[...] = jnp.zeros_like(f_ref)

    old = c_ref[...]
    entry_top, entry_low = halves(old)
    top_ref[0] = entry_top
    low_ref[0] = entry_low

    gates = beside(g_ref)
    upper = (iota((CHUNK, CHUNK), 0) <= iota((CHUNK, CHUNK), 1)).astype(BF16)
    cum = dot(gates, upper, (1, 0))
    cum = cum[0:1] + cum[1:2] + cum[2:3]
    gate = gates.astype(F32)
    gate = gate[3:4] + gate[4:5] + gate[5:6]
    total = cum[:, CHUNK - 1 : CHUNK]
    tail = total - cum + gate
    old_m = m_ref[0:1, 0:1]
    new_m = jnp.maximum(old_m + total, jnp.max(tail, axis=1, keepdims=True))
    keep = jnp.exp(old_m + total - new_m)

    row = iota((8, CHUNK), 0)
    aux = jnp.where(row == 0, n_ref[0:1, :], 0.0)
    for p, x in ((1, old_m), (2, f_ref[0:1, 0:1]), (3, cum), (4, gate - cum)):
        aux = jnp.where(row == p, x, aux)
    aux_ref[0] = aux

    keys = key_rows(k_ref)
    fresh = dot(
        weighted_values(beside(v_ref), jnp.exp(tail - new_m)),
        jnp.concatenate([keys, keys], axis=0),
        (1, 0),
    )
    c_ref[...] = keep * old + fresh[0:PIECE]
    n_ref[0:1, :] = keep * n_ref[0:1, :] + fresh[PIECE : PIECE + 1] + fresh[PIECE + 1 : PIECE + 2]
    m_ref[...] = jnp.broadcast_to(new_m, m_ref.shape)
    f_ref[...] = jnp.broadcast_to(f_ref[0:1, 0:1] + total, f_ref.shape)


def prefix_kernel(own_ref, z_ref, y_ref, nin_ref):
    count, slab, _ = z_ref.shape
    own = own_ref[0]
    small = 1.0 / 256.0

    def joined(a, b, c):
        return a + (b + c * small) * small

    scalars = z_ref[:, 6, PIECE:]
    columns = [scalars[:, p : p + 1] for p in range(9)]
    m = joined(*columns[0:3])
    most = joined(*columns[6:9]) * 4.0
    shard = iota((count, EXTRA), 0)
    later = iota((count, EXTRA), 1)
    before = shard < later
    after = (iota((count, count), 1) > iota((count, count), 0)).astype(BF16)
    gap = joined(
        *(dot(after, jnp.where(before, c, 0.0).astype(BF16), (1, 0)) for c in columns[3:6])
    )
    reach = jnp.where(before, m + gap, VERY_NEGATIVE)
    top = jnp.max(reach, axis=0, keepdims=True)
    weight = jnp.where(before, jnp.exp(reach - top), 0.0)
    heavy = weight * most
    bound = jnp.sum(heavy, axis=0, keepdims=True)
    heavy = heavy * jnp.where(bound > 0.0, 1.0 / bound, 0.0)
    heavy_top, heavy_low = halves(heavy.T)
    heavy_top, heavy_low = heavy_top[0:count], heavy_low[0:count]
    spread = jnp.concatenate([heavy_top, heavy_low, heavy_top], axis=1)
    for r in range(slab):
        x_top, x_low = halves(z_ref[:, r, 0:PIECE])
        y_ref[:, r, :] = dot(spread, jnp.concatenate([x_top, x_top, x_low], axis=0), (1, 0))

    mine = iota((1, EXTRA), 1) == own
    column = jnp.sum(jnp.where(mine, weight, 0.0), axis=1, keepdims=True)
    row = iota((8, EXTRA), 0)
    own_top = jnp.sum(jnp.where(mine, top, 0.0), axis=1, keepdims=True)
    own_bound = jnp.sum(jnp.where(mine, bound, 0.0), axis=1, keepdims=True)
    for h in range(PIECE // EXTRA):
        n = joined(*(z_ref[:, 2 * p + h, PIECE:] for p in range(3)))
        n = jnp.sum(column * n, axis=0, keepdims=True)
        area = jnp.where(row == 3, own_top, jnp.where(row == 4, own_bound, 0.0))
        for p, part in enumerate(thirds(n, 1.0)):
            area = jnp.where(row == p, part, area)
        nin_ref[:, h * EXTRA : (h + 1) * EXTRA] = area


def inside_kernel(q_ref, v_ref, k_ref, top_ref, low_ref, aux_ref, num_ref, row_ref):
    factor = PIECE**-0.5
    asked = beside(q_ref)
    turned = beside(v_ref)
    keys = key_rows(k_ref)
    aux = aux_ref[0]
    cum = aux[3:4]
    carried = cum + aux[1:2]
    score = dot(keys, asked, (1, 0))
    causal = iota((CHUNK, CHUNK), 0) <= iota((CHUNK, CHUNK), 1)
    gap = jnp.where(causal, aux.T[:, 4:5] + cum, VERY_NEGATIVE)
    top = jnp.maximum(carried, jnp.max(gap, axis=0, keepdims=True))
    weighted = jnp.exp(gap - top) * score
    outside = jnp.exp(carried - top)
    row = iota((8, CHUNK), 0)
    normal = jnp.zeros((8, CHUNK), F32)
    for p, part in enumerate(thirds(aux[0:1], 1.0)):
        normal = jnp.where(row == p, part, normal)
    reached = jnp.sum(dot(normal.astype(BF16), asked, (1, 0)), axis=0, keepdims=True)
    den = jnp.sum(weighted, axis=0, keepdims=True) + outside * reached
    num = dot(
        jnp.concatenate([turned, turned], axis=1), jnp.concatenate(halves(weighted), axis=0), (1, 0)
    )
    read = dot(
        jnp.concatenate([top_ref[0], low_ref[0]], axis=1),
        jnp.concatenate([asked, asked], axis=0),
        (1, 0),
    )
    num_ref[0] = num + outside * read
    row_ref[0] = jnp.where(row == 0, top, jnp.where(row == 1, den * factor, cum + aux[2:3]))


def finish_kernel(q_ref, num_ref, row_ref, c_ref, nin_ref, out_ref, both_ref):
    factor = PIECE**-0.5

    @pl.when(pl.program_id(0) == 0)
    def _():
        both_ref[...] = jnp.concatenate(halves(c_ref[...]), axis=1)

    asked = beside(q_ref)
    chunks = num_ref.shape[0]
    rows = jnp.concatenate([row_ref[c] for c in range(chunks)], axis=1)
    num = jnp.concatenate([num_ref[c] for c in range(chunks)], axis=1)
    m, den, cum = rows[0:1], rows[1:2], rows[2:3]
    place = iota((8, PIECE), 0)
    normal = jnp.where(place < 3, nin_ref[...], 0.0).astype(BF16)
    reached = jnp.sum(dot(normal, asked, (1, 0)), axis=0, keepdims=True)
    carried = cum + nin_ref[3:4, 0:1]
    new_m = jnp.maximum(m, carried)
    inside = jnp.exp(m - new_m)
    outside = jnp.exp(carried - new_m) * factor
    den = den * inside + outside * reached
    over = 1.0 / jnp.maximum(jnp.abs(den), 1.0)
    read = dot(both_ref[...], jnp.concatenate([asked, asked], axis=0), (1, 0))
    out = num * (inside * over * factor) + read * (outside * nin_ref[4:5, 0:1] * over)
    out_ref[...] = out.astype(BF16).T


def whole(shape):
    return pl.BlockSpec(shape, lambda i: (0,) * len(shape))


def stepped(shape, at=0):
    return pl.BlockSpec(shape, lambda i: tuple(i if d == at else 0 for d in range(len(shape))))


def part(shape, n):
    return pl.BlockSpec(shape, lambda i: (i, n, 0))


def gates(blocks):
    return pl.BlockSpec((blocks, GATE_ROWS, 128), lambda i: (i, 3 * PIECE // GATE_ROWS, 0))


def on_device(queries, keys, values, input_pre, forget_pre):
    rows = queries.shape[0]
    heads = input_pre.shape[1]
    pieces = lax.axis_size("head")
    shards = lax.axis_size("seq")
    tokens = pieces * rows
    steps = tokens // CHUNK
    group = CHUNK // rows
    tall = 3 * PIECE + GATE_ROWS
    slab = PIECE // shards
    cut = heads // PACK_STEPS
    wide = PIECE + EXTRA

    packed = pl.pallas_call(
        pack_kernel,
        grid=(PACK_STEPS,),
        in_specs=[
            stepped((rows, cut * PIECE), 1),
            stepped((rows, cut * PIECE), 1),
            stepped((rows, cut * 2 * PIECE), 1),
            whole((heads, rows)),
            whole((heads, rows)),
        ],
        out_specs=stepped((2 * cut, tall, rows)),
        out_shape=jax.ShapeDtypeStruct((pieces, tall, rows), BF16),
        scratch_shapes=[pltpu.VMEM((6, heads, rows), F32)],
        name="pack",
    )(queries, keys, values, input_pre.T, forget_pre.T)
    received = lax.all_to_all(packed, "head", split_axis=0, concat_axis=0, tiled=True)

    summary = pl.pallas_call(
        summary_kernel,
        grid=(1,),
        in_specs=[part((pieces, PIECE, rows), 1), part((pieces, PIECE, rows), 2), gates(pieces)],
        out_specs=whole((shards, slab, wide)),
        out_shape=jax.ShapeDtypeStruct((shards, slab, wide), F32),
        name="summary",
    )(received, received, received)

    spread = lax.all_to_all(summary.astype(F16), "seq", split_axis=0, concat_axis=0, tiled=True)

    entry_top, entry_low, aux = pl.pallas_call(
        entries_kernel,
        grid=(steps,),
        in_specs=[part((group, PIECE, rows), 1), part((group, PIECE, rows), 2), gates(group)],
        out_specs=[
            stepped((1, PIECE, PIECE)),
            stepped((1, PIECE, PIECE)),
            stepped((1, 8, CHUNK)),
        ],
        out_shape=[
            jax.ShapeDtypeStruct((steps, PIECE, PIECE), BF16),
            jax.ShapeDtypeStruct((steps, PIECE, PIECE), BF16),
            jax.ShapeDtypeStruct((steps, 8, CHUNK), F32),
        ],
        scratch_shapes=[
            pltpu.VMEM((PIECE, PIECE), F32),
            pltpu.VMEM((8, PIECE), F32),
            pltpu.VMEM((8, EXTRA), F32),
            pltpu.VMEM((8, EXTRA), F32),
        ],
        name="entries",
    )(received, received, received)

    own = lax.axis_index("seq").astype(jnp.int32).reshape(1)
    before, normal = pl.pallas_call(
        prefix_kernel,
        in_specs=[
            pl.BlockSpec(memory_space=pltpu.SMEM),
            pl.BlockSpec(memory_space=pltpu.VMEM),
        ],
        out_specs=[pl.BlockSpec(memory_space=pltpu.VMEM), pl.BlockSpec(memory_space=pltpu.VMEM)],
        out_shape=[
            jax.ShapeDtypeStruct((shards, slab, PIECE), F32),
            jax.ShapeDtypeStruct((8, PIECE), F32),
        ],
        name="prefix",
    )(own, spread.astype(F32))

    back = lax.all_to_all(before.astype(F16), "seq", split_axis=0, concat_axis=0, tiled=True)

    num, line = pl.pallas_call(
        inside_kernel,
        grid=(steps,),
        in_specs=[
            part((group, PIECE, rows), 0),
            part((group, PIECE, rows), 1),
            part((group, PIECE, rows), 2),
            stepped((1, PIECE, PIECE)),
            stepped((1, PIECE, PIECE)),
            stepped((1, 8, CHUNK)),
        ],
        out_specs=[stepped((1, PIECE, CHUNK)), stepped((1, 8, CHUNK))],
        out_shape=[
            jax.ShapeDtypeStruct((steps, PIECE, CHUNK), F32),
            jax.ShapeDtypeStruct((steps, 8, CHUNK), F32),
        ],
        name="inside",
    )(received, received, received, entry_top, entry_low, aux)

    return pl.pallas_call(
        finish_kernel,
        grid=(steps // 2,),
        in_specs=[
            part((2 * group, PIECE, rows), 0),
            stepped((2, PIECE, CHUNK)),
            stepped((2, 8, CHUNK)),
            whole((PIECE, PIECE)),
            whole((8, PIECE)),
        ],
        out_specs=stepped((2 * CHUNK, PIECE)),
        out_shape=jax.ShapeDtypeStruct((tokens, PIECE), BF16),
        scratch_shapes=[pltpu.VMEM((PIECE, 2 * PIECE), BF16)],
        name="finish",
    )(received, num, line, back.reshape(PIECE, PIECE).astype(F32), normal)


def solution(mesh):
    spec = P(("seq", "head"), None)

    return jax.shard_map(
        on_device, mesh=mesh, in_specs=(spec,) * 5, out_specs=P("seq", "head"), check_vma=False
    )
```

```python
import jax
import jax.numpy as jnp
from jax import lax
from jax.experimental import pallas as pl
from jax.experimental.pallas import tpu as pltpu
from jax.sharding import PartitionSpec as P

VERY_NEGATIVE = -1e30
CHUNK = 256
PIECE = 256
FINISH_STEPS = 4
HALF = PIECE // 2
KEYS = PIECE
ASKED = 2 * PIECE
GATES = ASKED + HALF
VMEM_LIMIT = 24 << 20
EXTRA = 128
GATE_ROWS = 8
F32 = jnp.float32
BF16 = jnp.bfloat16
F16 = jnp.float16


def dot(a, b, contract):
    return lax.dot_general(a, b, ((contract[:1], contract[1:]), ((), ())), preferred_element_type=F32)


def halves(x):
    top = x.astype(BF16)
    return top, (x - top.astype(F32)).astype(BF16)


def thirds(x, scale):
    first = x.astype(BF16).astype(F32)
    rest = (x - first) * scale
    second = rest.astype(BF16).astype(F32)
    third = ((rest - second) * scale).astype(BF16).astype(F32)
    return first, second, third


def iota(shape, dim):
    return lax.broadcasted_iota(jnp.int32, shape, dim)


def pack_kernel(q_ref, k_ref, v_ref, gate_ref, forget_ref, out_ref):
    rows = k_ref.shape[0]
    parts = []
    for x in (-jnp.log1p(jnp.exp(-forget_ref[...])), gate_ref[...]):
        parts += thirds(x, 1.0)
    row = iota((GATE_ROWS, rows), 0)
    for h in range(k_ref.shape[1] // PIECE):
        area = jnp.zeros((GATE_ROWS, rows), F32)
        for p in range(6):
            area = jnp.where(row == p, parts[p][h : h + 1], area)
        area = area.astype(BF16)
        for u in range(2):
            n = 2 * h + u
            out_ref[n, 0:PIECE, :] = v_ref[:, n * PIECE : (n + 1) * PIECE].T
            for c in range(2):
                left = h * PIECE + (c ^ u) * HALF
                out_ref[n, KEYS + c * HALF : KEYS + (c + 1) * HALF, :] = k_ref[:, left : left + HALF]
            left = h * PIECE + u * HALF
            out_ref[n, ASKED:GATES, :] = q_ref[:, left : left + HALF].T
            out_ref[n, GATES : GATES + GATE_ROWS, :] = area


def beside(ref, blocks, low, high):
    return jnp.concatenate([ref[b, low:high, :] for b in blocks], axis=1)


def key_rows(ref, blocks):
    return jnp.concatenate(
        [
            jnp.concatenate([ref[b, KEYS + c * HALF : KEYS + (c + 1) * HALF, :] for c in range(2)], axis=1)
            for b in blocks
        ],
        axis=0,
    )


def asked_rows(ref, other_ref, blocks):
    return jnp.concatenate([beside(ref, blocks, ASKED, GATES), beside(other_ref, blocks, 0, HALF)], axis=0)


def chunk_blocks(ref, chunk):
    group = CHUNK // ref.shape[2]
    return range(chunk * group, (chunk + 1) * group)


def weighted_values(turned, weight):
    top, low = halves(turned.astype(F32) * weight)
    first, second, third = thirds(weight, 1.0)
    row = iota((8, weight.shape[1]), 0)
    left = jnp.where(row == 0, first, jnp.where(row == 1, third, 0.0)).astype(BF16)
    right = jnp.where(row == 0, second, 0.0).astype(BF16)
    return jnp.concatenate(
        [jnp.concatenate([top, left], axis=0), jnp.concatenate([low, right], axis=0)], axis=1
    )


def summary_kernel(r_ref, z_ref):
    sources, rows = r_ref.shape[0], r_ref.shape[2]
    decay = [r_ref[:, GATES + p, :] for p in range(3)]
    gate = [r_ref[:, GATES + 3 + p, :].astype(F32) for p in range(3)]
    gate = gate[0] + gate[1] + gate[2]
    after = (iota((rows, rows), 0) > iota((rows, rows), 1)).astype(BF16)
    later = (iota((sources, sources), 1) > iota((sources, sources), 0)).astype(BF16)
    suffix = sum(dot(d, after, (1, 0)) for d in decay)
    rest = sum(dot(later, d, (1, 0)) for d in decay)
    total = sum(jnp.sum(d.astype(F32), axis=0, keepdims=True) for d in decay)
    total = jnp.sum(total, axis=1, keepdims=True)
    tail = suffix + jnp.sum(rest, axis=1, keepdims=True) + gate
    new_m = jnp.max(jnp.max(tail, axis=1, keepdims=True), axis=0, keepdims=True)
    weight = jnp.exp(tail - new_m)
    state = jnp.zeros((PIECE + 8, PIECE), F32)
    for g in range(sources * rows // CHUNK):
        mine = chunk_blocks(r_ref, g)
        turned = beside(r_ref, mine, 0, PIECE)
        share = jnp.concatenate([weight[b : b + 1, :] for b in mine], axis=1)
        keys = key_rows(r_ref, mine)
        state = state + dot(
            weighted_values(turned, share), jnp.concatenate([keys, keys], axis=0), (1, 0)
        )
    c_new = state[0:PIECE]
    n_new = state[PIECE : PIECE + 1] + state[PIECE + 1 : PIECE + 2]

    count, slab = z_ref.shape[0], z_ref.shape[1]
    most = jnp.max(jnp.max(jnp.abs(c_new), axis=1, keepdims=True), axis=0, keepdims=True)
    scaled = c_new * jnp.where(most > 0.0, 1.0 / most, 0.0)
    z_ref[:, :, 0:PIECE] = scaled.reshape(count, slab, PIECE)
    place = iota((slab, EXTRA), 0)
    lane = iota((slab, EXTRA), 1)
    extra = jnp.zeros((slab, EXTRA), F32)
    for p, part in enumerate(thirds(n_new, 256.0)):
        for h in range(PIECE // EXTRA):
            extra = jnp.where(place == 2 * p + h, part[:, h * EXTRA : (h + 1) * EXTRA], extra)
    for n, x in enumerate((new_m, total, most * 0.25)):
        for p, part in enumerate(thirds(x, 256.0)):
            extra = jnp.where((place == 6) & (lane == 3 * n + p), part, extra)
    z_ref[:, :, PIECE:] = jnp.broadcast_to(extra[None], (count, slab, EXTRA))


def entries_kernel(r_ref, top_ref, low_ref, aux_ref):
    upper = (iota((CHUNK, CHUNK), 0) <= iota((CHUNK, CHUNK), 1)).astype(BF16)
    row = iota((8, CHUNK), 0)
    state = jnp.zeros((PIECE, PIECE), F32)
    normal = jnp.zeros((1, PIECE), F32)
    old_m = jnp.full((1, 1), VERY_NEGATIVE, F32)
    start = jnp.zeros((1, 1), F32)
    steps = top_ref.shape[0]
    for step in range(steps):
        mine = chunk_blocks(r_ref, step)
        top_ref[step], low_ref[step] = halves(state)
        gates = beside(r_ref, mine, GATES, GATES + GATE_ROWS)
        cum = dot(gates, upper, (1, 0))
        cum = cum[0:1] + cum[1:2] + cum[2:3]
        gate = gates.astype(F32)
        gate = gate[3:4] + gate[4:5] + gate[5:6]
        total = cum[:, CHUNK - 1 : CHUNK]
        tail = total - cum + gate
        new_m = jnp.maximum(old_m + total, jnp.max(tail, axis=1, keepdims=True))
        keep = jnp.exp(old_m + total - new_m)
        aux = jnp.where(row == 0, normal, 0.0)
        for p, x in ((1, old_m), (2, start), (3, cum), (4, gate - cum)):
            aux = jnp.where(row == p, x, aux)
        aux_ref[step] = aux
        if step < steps - 1:
            keys = key_rows(r_ref, mine)
            fresh = dot(
                weighted_values(beside(r_ref, mine, 0, PIECE), jnp.exp(tail - new_m)),
                jnp.concatenate([keys, keys], axis=0),
                (1, 0),
            )
            state = keep * state + fresh[0:PIECE]
            normal = keep * normal + fresh[PIECE : PIECE + 1] + fresh[PIECE + 1 : PIECE + 2]
            old_m = new_m
            start = start + total


def prefix_kernel(own_ref, z_ref, y_ref, nin_ref):
    count, slab, _ = z_ref.shape
    own = own_ref[0]
    small = 1.0 / 256.0

    def joined(a, b, c):
        return a + (b + c * small) * small

    scalars = z_ref[:, 6, PIECE:]
    columns = [scalars[:, p : p + 1] for p in range(9)]
    m = joined(*columns[0:3])
    most = joined(*columns[6:9]) * 4.0
    shard = iota((count, EXTRA), 0)
    later = iota((count, EXTRA), 1)
    before = shard < later
    after = (iota((count, count), 1) > iota((count, count), 0)).astype(BF16)
    gap = joined(
        *(dot(after, jnp.where(before, c, 0.0).astype(BF16), (1, 0)) for c in columns[3:6])
    )
    reach = jnp.where(before, m + gap, VERY_NEGATIVE)
    top = jnp.max(reach, axis=0, keepdims=True)
    weight = jnp.where(before, jnp.exp(reach - top), 0.0)
    heavy = weight * most
    bound = jnp.sum(heavy, axis=0, keepdims=True)
    heavy = heavy * jnp.where(bound > 0.0, 1.0 / bound, 0.0)
    size = count * slab
    shift = slab.bit_length() - 1
    down = (iota((size, count), 0) >> shift == iota((size, count), 1)).astype(BF16)
    right = (iota((count, size), 0) == iota((count, size), 1) >> shift).astype(BF16)
    same = (iota((size, size), 0) & (slab - 1)) == (iota((size, size), 1) & (slab - 1))
    turned = heavy.T[0:count, :]
    wide = []
    for x in halves(turned):
        x = dot(dot(down, x, (1, 0)).astype(BF16), right, (1, 0))
        wide.append(jnp.where(same, x, 0.0).astype(BF16))
    x_top, x_low = halves(z_ref[:, :, 0:PIECE].reshape(size, PIECE))
    y = dot(
        jnp.concatenate([wide[0], wide[1], wide[0]], axis=1),
        jnp.concatenate([x_top, x_top, x_low], axis=0),
        (1, 0),
    )
    y_ref[...] = y.reshape(count, slab, PIECE)

    mine = iota((1, EXTRA), 1) == own
    column = jnp.sum(jnp.where(mine, weight, 0.0), axis=1, keepdims=True)
    row = iota((8, EXTRA), 0)
    own_top = jnp.sum(jnp.where(mine, top, 0.0), axis=1, keepdims=True)
    own_bound = jnp.sum(jnp.where(mine, bound, 0.0), axis=1, keepdims=True)
    for h in range(PIECE // EXTRA):
        n = joined(*(z_ref[:, 2 * p + h, PIECE:] for p in range(3)))
        n = jnp.sum(column * n, axis=0, keepdims=True)
        area = jnp.where(row == 3, own_top, jnp.where(row == 4, own_bound, 0.0))
        for p, part in enumerate(thirds(n, 1.0)):
            area = jnp.where(row == p, part, area)
        nin_ref[:, h * EXTRA : (h + 1) * EXTRA] = area


def inside_kernel(r_ref, other_ref, top_ref, low_ref, aux_ref, num_ref, row_ref):
    factor = PIECE**-0.5
    causal = iota((CHUNK, CHUNK), 0) <= iota((CHUNK, CHUNK), 1)
    row = iota((8, CHUNK), 0)
    for step in range(num_ref.shape[0]):
        mine = chunk_blocks(r_ref, step)
        asked = asked_rows(r_ref, other_ref, mine)
        turned = beside(r_ref, mine, 0, PIECE)
        aux = aux_ref[step]
        cum = aux[3:4]
        carried = cum + aux[1:2]
        score = dot(key_rows(r_ref, mine), asked, (1, 0))
        gap = jnp.where(causal, aux.T[:, 4:5] + cum, VERY_NEGATIVE)
        top = jnp.maximum(carried, jnp.max(gap, axis=0, keepdims=True))
        weighted = jnp.exp(gap - top) * score
        outside = jnp.exp(carried - top)
        normal = jnp.zeros((8, CHUNK), F32)
        for p, part in enumerate(thirds(aux[0:1], 1.0)):
            normal = jnp.where(row == p, part, normal)
        reached = jnp.sum(dot(normal.astype(BF16), asked, (1, 0)), axis=0, keepdims=True)
        den = jnp.sum(weighted, axis=0, keepdims=True) + outside * reached
        num = dot(
            jnp.concatenate([turned, turned], axis=1),
            jnp.concatenate(halves(weighted), axis=0),
            (1, 0),
        )
        read = dot(
            jnp.concatenate([top_ref[step], low_ref[step]], axis=1),
            jnp.concatenate([asked, asked], axis=0),
            (1, 0),
        )
        num_ref[step] = num + outside * read
        row_ref[step] = jnp.where(row == 0, top, jnp.where(row == 1, den * factor, cum + aux[2:3]))


def finish_kernel(own_ref, other_ref, num_ref, row_ref, c_ref, nin_ref, out_ref, both_ref):
    factor = PIECE**-0.5
    at = pl.program_id(0)

    @pl.when(at == 0)
    def _():
        both_ref[...] = jnp.concatenate(halves(c_ref[...]), axis=1)

    place = iota((8, PIECE), 0)
    normal = jnp.where(place < 3, nin_ref[...], 0.0).astype(BF16)
    before_m = nin_ref[3:4, 0:1]
    bound = nin_ref[4:5, 0:1]
    for step in range(num_ref.shape[0]):
        blocks = chunk_blocks(own_ref, step)
        asked = jnp.concatenate(
            [beside(own_ref, blocks, 0, HALF), beside(other_ref, blocks, 0, HALF)], axis=0
        )
        rows = row_ref[step]
        m, den, cum = rows[0:1], rows[1:2], rows[2:3]
        reached = jnp.sum(dot(normal, asked, (1, 0)), axis=0, keepdims=True)
        carried = cum + before_m
        new_m = jnp.maximum(m, carried)
        inside = jnp.exp(m - new_m)
        outside = jnp.exp(carried - new_m) * factor
        den = den * inside + outside * reached
        over = 1.0 / jnp.maximum(jnp.abs(den), 1.0)
        read = dot(both_ref[...], jnp.concatenate([asked, asked], axis=0), (1, 0))
        out = num_ref[step] * (inside * over * factor) + read * (outside * bound * over)
        out_ref[step * CHUNK : (step + 1) * CHUNK, :] = out.astype(BF16).T


def whole(shape):
    return pl.BlockSpec(shape, lambda i: (0,) * len(shape))


def stepped(shape, at=0):
    return pl.BlockSpec(shape, lambda i: tuple(i if d == at else 0 for d in range(len(shape))))


def near(x):
    return pltpu.with_memory_space_constraint(x, pltpu.VMEM)


NEAR = pl.BlockSpec(memory_space=pltpu.VMEM)
FAR = pl.BlockSpec()
PARAMS = pltpu.CompilerParams(vmem_limit_bytes=VMEM_LIMIT)


def on_device(queries, keys, values, input_pre, forget_pre):
    rows = queries.shape[0]
    pieces = lax.axis_size("head")
    shards = lax.axis_size("seq")
    tokens = pieces * rows
    steps = tokens // CHUNK
    tall = GATES + GATE_ROWS
    slab = PIECE // shards
    wide = PIECE + EXTRA

    packed = pl.pallas_call(
        pack_kernel,
        in_specs=[FAR] * 5,
        out_specs=NEAR,
        out_shape=pltpu.VMEM((pieces, tall, rows), BF16),
        compiler_params=PARAMS,
        name="pack",
    )(queries, keys, values, input_pre.T, forget_pre.T)

    received = lax.all_to_all(packed, "head", split_axis=0, concat_axis=0, tiled=True)

    summary = pl.pallas_call(
        summary_kernel,
        in_specs=[NEAR],
        out_specs=NEAR,
        out_shape=pltpu.VMEM((shards, slab, wide), F32),
        compiler_params=PARAMS,
        name="summary",
    )(near(received))

    spread = lax.all_to_all(summary.astype(F16), "seq", split_axis=0, concat_axis=0, tiled=True)

    other = lax.ppermute(received[:, ASKED:GATES, :], "head", [(i, i ^ 1) for i in range(pieces)])

    entry_top, entry_low, aux = pl.pallas_call(
        entries_kernel,
        in_specs=[NEAR],
        out_specs=[FAR] * 3,
        out_shape=[
            jax.ShapeDtypeStruct((steps, PIECE, PIECE), BF16),
            jax.ShapeDtypeStruct((steps, PIECE, PIECE), BF16),
            jax.ShapeDtypeStruct((steps, 8, CHUNK), F32),
        ],
        name="entries",
    )(near(received))

    own = lax.axis_index("seq").astype(jnp.int32).reshape(1)
    before, normal = pl.pallas_call(
        prefix_kernel,
        in_specs=[pl.BlockSpec(memory_space=pltpu.SMEM), NEAR],
        out_specs=[NEAR, FAR],
        out_shape=[
            pltpu.VMEM((shards, slab, PIECE), F32),
            jax.ShapeDtypeStruct((8, PIECE), F32),
        ],
        compiler_params=pltpu.CompilerParams(vmem_limit_bytes=60 << 20),
        name="prefix",
    )(own, near(spread.astype(F32)))

    back = lax.all_to_all(before.astype(F16), "seq", split_axis=0, concat_axis=0, tiled=True)

    num, line = pl.pallas_call(
        inside_kernel,
        in_specs=[NEAR, NEAR, FAR, FAR, FAR],
        out_specs=[FAR] * 2,
        out_shape=[
            jax.ShapeDtypeStruct((steps, PIECE, CHUNK), F32),
            jax.ShapeDtypeStruct((steps, 8, CHUNK), F32),
        ],
        name="inside",
    )(near(received), near(other), entry_top, entry_low, aux)

    return pl.pallas_call(
        finish_kernel,
        grid=(FINISH_STEPS,),
        in_specs=[
            pl.BlockSpec((pieces // FINISH_STEPS, HALF, rows), lambda i: (i, ASKED // HALF, 0)),
            stepped((pieces // FINISH_STEPS, HALF, rows)),
            stepped((steps // FINISH_STEPS, PIECE, CHUNK)),
            stepped((steps // FINISH_STEPS, 8, CHUNK)),
            NEAR,
            whole((8, PIECE)),
        ],
        out_specs=stepped((tokens // FINISH_STEPS, PIECE)),
        out_shape=jax.ShapeDtypeStruct((tokens, PIECE), BF16),
        scratch_shapes=[pltpu.VMEM((PIECE, 2 * PIECE), BF16)],
        compiler_params=pltpu.CompilerParams(vmem_limit_bytes=60 << 20),
        name="finish",
    )(received, other, num, line, near(back.reshape(PIECE, PIECE).astype(F32)), normal)


def solution(mesh):
    spec = P(("seq", "head"), None)

    return jax.shard_map(
        on_device, mesh=mesh, in_specs=(spec,) * 5, out_specs=P("seq", "head"), check_vma=False
    )
```

```python
import jax
import jax.numpy as jnp
from jax import lax
from jax.experimental import pallas as pl
from jax.experimental.pallas import tpu as pltpu
from jax.sharding import PartitionSpec as P

VERY_NEGATIVE = -1e30
CHUNK = 256
PIECE = 256
HALF = PIECE // 2
KEYS = PIECE
ASKED = 2 * PIECE
GATES = ASKED + HALF
VMEM_LIMIT = 24 << 20
INSIDE_LIMIT = 48 << 20
EXTRA = 128
GATE_ROWS = 8
F32 = jnp.float32
BF16 = jnp.bfloat16
F16 = jnp.float16


def dot(a, b, contract):
    return lax.dot_general(a, b, ((contract[:1], contract[1:]), ((), ())), preferred_element_type=F32)


def halves(x):
    top = x.astype(BF16)
    return top, (x - top.astype(F32)).astype(BF16)


def thirds(x, scale):
    first = x.astype(BF16).astype(F32)
    rest = (x - first) * scale
    second = rest.astype(BF16).astype(F32)
    third = ((rest - second) * scale).astype(BF16).astype(F32)
    return first, second, third


def iota(shape, dim):
    return lax.broadcasted_iota(jnp.int32, shape, dim)


def pack_kernel(q_in, k_in, v_in, gate_in, forget_in, out_ref, q_ref, k_ref, v_ref, gate_ref, forget_ref, sem):
    rows = k_ref.shape[0]
    pairs = (gate_in, gate_ref), (forget_in, forget_ref), (v_in, v_ref), (k_in, k_ref), (q_in, q_ref)
    copies = [pltpu.make_async_copy(a, b, sem.at[n]) for n, (a, b) in enumerate(pairs)]
    for copy in copies:
        copy.start()
    copies[0].wait()
    copies[1].wait()
    parts = []
    for x in (-jnp.log1p(jnp.exp(-forget_ref[...])), gate_ref[...]):
        parts += thirds(x, 1.0)
    for copy in copies[2:]:
        copy.wait()
    row = iota((GATE_ROWS, rows), 0)
    for h in range(k_ref.shape[1] // PIECE):
        area = jnp.zeros((GATE_ROWS, rows), F32)
        for p in range(6):
            area = jnp.where(row == p, parts[p][h : h + 1], area)
        area = area.astype(BF16)
        for u in range(2):
            n = 2 * h + u
            out_ref[n, 0:PIECE, :] = v_ref[:, n * PIECE : (n + 1) * PIECE].T
            for c in range(2):
                left = h * PIECE + (c ^ u) * HALF
                out_ref[n, KEYS + c * HALF : KEYS + (c + 1) * HALF, :] = k_ref[:, left : left + HALF]
            left = h * PIECE + u * HALF
            out_ref[n, ASKED:GATES, :] = q_ref[:, left : left + HALF].T
            out_ref[n, GATES : GATES + GATE_ROWS, :] = area


def beside(ref, blocks, low, high):
    return jnp.concatenate([ref[b, low:high, :] for b in blocks], axis=1)


def key_rows(ref, blocks):
    return jnp.concatenate(
        [
            jnp.concatenate([ref[b, KEYS + c * HALF : KEYS + (c + 1) * HALF, :] for c in range(2)], axis=1)
            for b in blocks
        ],
        axis=0,
    )


def asked_rows(ref, other_ref, blocks):
    return jnp.concatenate([beside(ref, blocks, ASKED, GATES), beside(other_ref, blocks, 0, HALF)], axis=0)


def chunk_blocks(ref, chunk):
    group = CHUNK // ref.shape[2]
    return range(chunk * group, (chunk + 1) * group)


def weighted_values(turned, weight):
    top, low = halves(turned.astype(F32) * weight)
    first, second, third = thirds(weight, 1.0)
    row = iota((8, weight.shape[1]), 0)
    left = jnp.where(row == 0, first, jnp.where(row == 1, third, 0.0)).astype(BF16)
    right = jnp.where(row == 0, second, 0.0).astype(BF16)
    return jnp.concatenate(
        [jnp.concatenate([top, left], axis=0), jnp.concatenate([low, right], axis=0)], axis=1
    )


def summary_kernel(r_ref, z_ref):
    sources, rows = r_ref.shape[0], r_ref.shape[2]
    decay = [r_ref[:, GATES + p, :] for p in range(3)]
    gate = [r_ref[:, GATES + 3 + p, :].astype(F32) for p in range(3)]
    gate = gate[0] + gate[1] + gate[2]
    after = (iota((rows, rows), 0) > iota((rows, rows), 1)).astype(BF16)
    later = (iota((sources, sources), 1) > iota((sources, sources), 0)).astype(BF16)
    suffix = sum(dot(d, after, (1, 0)) for d in decay)
    rest = sum(dot(later, d, (1, 0)) for d in decay)
    total = sum(jnp.sum(d.astype(F32), axis=0, keepdims=True) for d in decay)
    total = jnp.sum(total, axis=1, keepdims=True)
    tail = suffix + jnp.sum(rest, axis=1, keepdims=True) + gate
    new_m = jnp.max(jnp.max(tail, axis=1, keepdims=True), axis=0, keepdims=True)
    weight = jnp.exp(tail - new_m)
    state = jnp.zeros((PIECE + 8, PIECE), F32)
    for g in range(sources * rows // CHUNK):
        mine = chunk_blocks(r_ref, g)
        turned = beside(r_ref, mine, 0, PIECE)
        share = jnp.concatenate([weight[b : b + 1, :] for b in mine], axis=1)
        keys = key_rows(r_ref, mine)
        state = state + dot(
            weighted_values(turned, share), jnp.concatenate([keys, keys], axis=0), (1, 0)
        )
    c_new = state[0:PIECE]
    n_new = state[PIECE : PIECE + 1] + state[PIECE + 1 : PIECE + 2]

    count, slab = z_ref.shape[0], z_ref.shape[1]
    most = jnp.max(jnp.max(jnp.abs(c_new), axis=1, keepdims=True), axis=0, keepdims=True)
    scaled = c_new * jnp.where(most > 0.0, 1.0 / most, 0.0)
    z_ref[:, :, 0:PIECE] = scaled.reshape(count, slab, PIECE)
    place = iota((slab, EXTRA), 0)
    lane = iota((slab, EXTRA), 1)
    extra = jnp.zeros((slab, EXTRA), F32)
    for p, part in enumerate(thirds(n_new, 256.0)):
        for h in range(PIECE // EXTRA):
            extra = jnp.where(place == 2 * p + h, part[:, h * EXTRA : (h + 1) * EXTRA], extra)
    for n, x in enumerate((new_m, total, most * 0.25)):
        for p, part in enumerate(thirds(x, 256.0)):
            extra = jnp.where((place == 6) & (lane == 3 * n + p), part, extra)
    z_ref[:, :, PIECE:] = jnp.broadcast_to(extra[None], (count, slab, EXTRA))


def entries_kernel(r_ref, top_ref, low_ref, aux_ref):
    upper = (iota((CHUNK, CHUNK), 0) <= iota((CHUNK, CHUNK), 1)).astype(BF16)
    row = iota((8, CHUNK), 0)
    state = jnp.zeros((PIECE, PIECE), F32)
    normal = jnp.zeros((1, PIECE), F32)
    old_m = jnp.full((1, 1), VERY_NEGATIVE, F32)
    start = jnp.zeros((1, 1), F32)
    steps = top_ref.shape[0]
    for step in range(steps):
        mine = chunk_blocks(r_ref, step)
        top_ref[step], low_ref[step] = halves(state)
        gates = beside(r_ref, mine, GATES, GATES + GATE_ROWS)
        cum = dot(gates, upper, (1, 0))
        cum = cum[0:1] + cum[1:2] + cum[2:3]
        gate = gates.astype(F32)
        gate = gate[3:4] + gate[4:5] + gate[5:6]
        total = cum[:, CHUNK - 1 : CHUNK]
        tail = total - cum + gate
        new_m = jnp.maximum(old_m + total, jnp.max(tail, axis=1, keepdims=True))
        keep = jnp.exp(old_m + total - new_m)
        aux = jnp.where(row == 0, normal, 0.0)
        for p, x in ((1, old_m), (2, start), (3, cum), (4, gate - cum)):
            aux = jnp.where(row == p, x, aux)
        aux_ref[step] = aux
        if step < steps - 1:
            keys = key_rows(r_ref, mine)
            fresh = dot(
                weighted_values(beside(r_ref, mine, 0, PIECE), jnp.exp(tail - new_m)),
                jnp.concatenate([keys, keys], axis=0),
                (1, 0),
            )
            state = keep * state + fresh[0:PIECE]
            normal = keep * normal + fresh[PIECE : PIECE + 1] + fresh[PIECE + 1 : PIECE + 2]
            old_m = new_m
            start = start + total


def prefix_kernel(own_ref, z_ref, y_ref, nin_ref):
    count, slab, _ = z_ref.shape
    own = own_ref[0]
    small = 1.0 / 256.0

    def joined(a, b, c):
        return a + (b + c * small) * small

    scalars = z_ref[:, 6, PIECE:]
    columns = [scalars[:, p : p + 1] for p in range(9)]
    m = joined(*columns[0:3])
    most = joined(*columns[6:9]) * 4.0
    shard = iota((count, EXTRA), 0)
    later = iota((count, EXTRA), 1)
    before = shard < later
    after = (iota((count, count), 1) > iota((count, count), 0)).astype(BF16)
    gap = joined(
        *(dot(after, jnp.where(before, c, 0.0).astype(BF16), (1, 0)) for c in columns[3:6])
    )
    reach = jnp.where(before, m + gap, VERY_NEGATIVE)
    top = jnp.max(reach, axis=0, keepdims=True)
    weight = jnp.where(before, jnp.exp(reach - top), 0.0)
    heavy = weight * most
    bound = jnp.sum(heavy, axis=0, keepdims=True)
    heavy = heavy * jnp.where(bound > 0.0, 1.0 / bound, 0.0)
    size = count * slab
    shift = slab.bit_length() - 1
    down = (iota((size, count), 0) >> shift == iota((size, count), 1)).astype(BF16)
    right = (iota((count, size), 0) == iota((count, size), 1) >> shift).astype(BF16)
    same = (iota((size, size), 0) & (slab - 1)) == (iota((size, size), 1) & (slab - 1))
    turned = heavy.T[0:count, :]
    wide = []
    for x in halves(turned):
        x = dot(dot(down, x, (1, 0)).astype(BF16), right, (1, 0))
        wide.append(jnp.where(same, x, 0.0).astype(BF16))
    x_top, x_low = halves(z_ref[:, :, 0:PIECE].reshape(size, PIECE))
    y = dot(
        jnp.concatenate([wide[0], wide[1], wide[0]], axis=1),
        jnp.concatenate([x_top, x_top, x_low], axis=0),
        (1, 0),
    )
    y_ref[...] = y.reshape(count, slab, PIECE)

    mine = iota((1, EXTRA), 1) == own
    column = jnp.sum(jnp.where(mine, weight, 0.0), axis=1, keepdims=True)
    row = iota((8, EXTRA), 0)
    own_top = jnp.sum(jnp.where(mine, top, 0.0), axis=1, keepdims=True)
    own_bound = jnp.sum(jnp.where(mine, bound, 0.0), axis=1, keepdims=True)
    for h in range(PIECE // EXTRA):
        n = joined(*(z_ref[:, 2 * p + h, PIECE:] for p in range(3)))
        n = jnp.sum(column * n, axis=0, keepdims=True)
        area = jnp.where(row == 6, own_top, jnp.where(row == 7, own_bound, 0.0))
        for p, part in enumerate(thirds(n, 1.0)):
            area = jnp.where(row == 3 + p, part, area)
        nin_ref[:, h * EXTRA : (h + 1) * EXTRA] = area


def inside_kernel(r_ref, other_ref, top_ref, low_ref, aux_ref, nin_ref, num_ref, row_ref):
    factor = PIECE**-0.5
    before = nin_ref[...]
    before_m = before[6:7, 0:1]
    bound = before[7:8, 0:1]
    causal = iota((CHUNK, CHUNK), 0) <= iota((CHUNK, CHUNK), 1)
    row = iota((8, CHUNK), 0)
    for step in range(num_ref.shape[0]):
        mine = chunk_blocks(r_ref, step)
        asked = asked_rows(r_ref, other_ref, mine)
        turned = beside(r_ref, mine, 0, PIECE)
        aux = aux_ref[step]
        cum = aux[3:4]
        carried = cum + aux[1:2]
        score = dot(key_rows(r_ref, mine), asked, (1, 0))
        gap = jnp.where(causal, aux.T[:, 4:5] + cum, VERY_NEGATIVE)
        top = jnp.maximum(carried, jnp.max(gap, axis=0, keepdims=True))
        weighted = jnp.exp(gap - top) * score
        outside = jnp.exp(carried - top)
        normal = jnp.where((row >= 3) & (row < 6), before, 0.0)
        for p, part in enumerate(thirds(aux[0:1], 1.0)):
            normal = jnp.where(row == p, part, normal)
        reached = dot(normal.astype(BF16), asked, (1, 0))
        den = jnp.sum(weighted, axis=0, keepdims=True)
        den = factor * (den + outside * (reached[0:1] + reached[1:2] + reached[2:3]))
        carried = cum + aux[2:3] + before_m
        new_m = jnp.maximum(top, carried)
        inside = jnp.exp(top - new_m)
        ahead = jnp.exp(carried - new_m) * factor
        den = den * inside + ahead * (reached[3:4] + reached[4:5] + reached[5:6])
        over = 1.0 / jnp.maximum(jnp.abs(den), 1.0)
        inside = inside * over * factor
        num = dot(
            jnp.concatenate([turned, turned], axis=1),
            jnp.concatenate(halves(weighted), axis=0),
            (1, 0),
        )
        read = dot(
            jnp.concatenate([top_ref[step], low_ref[step]], axis=1),
            jnp.concatenate([asked, asked], axis=0),
            (1, 0),
        )
        num_ref[step] = inside * num + (inside * outside) * read
        row_ref[step] = jnp.broadcast_to(ahead * bound * over, (8, CHUNK))


def finish_kernel(own_ref, other_ref, num_ref, row_ref, c_ref, out_ref, buffer_ref, sem):
    both = jnp.concatenate(halves(c_ref[...]), axis=1)
    copies = []
    for step in range(num_ref.shape[0]):
        blocks = chunk_blocks(own_ref, step)
        asked = jnp.concatenate(
            [beside(own_ref, blocks, 0, HALF), beside(other_ref, blocks, 0, HALF)], axis=0
        )
        read = dot(both, jnp.concatenate([asked, asked], axis=0), (1, 0))
        out = num_ref[step] + read * row_ref[step, 0:1, :]
        here = pl.ds(step * CHUNK, CHUNK)
        buffer_ref[here, :] = out.astype(BF16).T
        copies.append(pltpu.make_async_copy(buffer_ref.at[here], out_ref.at[here], sem.at[step]))
        copies[-1].start()
    for copy in copies:
        copy.wait()


def near(x):
    return pltpu.with_memory_space_constraint(x, pltpu.VMEM)


NEAR = pl.BlockSpec(memory_space=pltpu.VMEM)
FAR = pl.BlockSpec()
PARAMS = pltpu.CompilerParams(vmem_limit_bytes=VMEM_LIMIT)


def on_device(queries, keys, values, input_pre, forget_pre):
    rows = queries.shape[0]
    pieces = lax.axis_size("head")
    shards = lax.axis_size("seq")
    tokens = pieces * rows
    steps = tokens // CHUNK
    tall = GATES + GATE_ROWS
    slab = PIECE // shards
    wide = PIECE + EXTRA

    packed = pl.pallas_call(
        pack_kernel,
        in_specs=[pl.BlockSpec(memory_space=pltpu.HBM)] * 5,
        out_specs=NEAR,
        out_shape=pltpu.VMEM((pieces, tall, rows), BF16),
        scratch_shapes=[
            pltpu.VMEM(queries.shape, BF16),
            pltpu.VMEM(keys.shape, BF16),
            pltpu.VMEM(values.shape, BF16),
            pltpu.VMEM((input_pre.shape[1], rows), F32),
            pltpu.VMEM((input_pre.shape[1], rows), F32),
            pltpu.SemaphoreType.DMA((5,)),
        ],
        compiler_params=PARAMS,
        name="pack",
    )(*(pltpu.with_memory_space_constraint(x, pltpu.HBM) for x in (queries, keys, values, input_pre.T, forget_pre.T)))

    received = lax.all_to_all(packed, "head", split_axis=0, concat_axis=0, tiled=True)

    summary = pl.pallas_call(
        summary_kernel,
        in_specs=[NEAR],
        out_specs=NEAR,
        out_shape=pltpu.VMEM((shards, slab, wide), F32),
        compiler_params=PARAMS,
        name="summary",
    )(near(received))

    spread = lax.all_to_all(summary.astype(F16), "seq", split_axis=0, concat_axis=0, tiled=True)

    ours = received[:, ASKED:GATES, :]
    other = lax.ppermute(ours, "head", [(i, i ^ 1) for i in range(pieces)])

    entry_top, entry_low, aux = pl.pallas_call(
        entries_kernel,
        in_specs=[NEAR],
        out_specs=[FAR] * 3,
        out_shape=[
            jax.ShapeDtypeStruct((steps, PIECE, PIECE), BF16),
            jax.ShapeDtypeStruct((steps, PIECE, PIECE), BF16),
            jax.ShapeDtypeStruct((steps, 8, CHUNK), F32),
        ],
        name="entries",
    )(near(received))

    own = lax.axis_index("seq").astype(jnp.int32).reshape(1)
    before, normal = pl.pallas_call(
        prefix_kernel,
        in_specs=[pl.BlockSpec(memory_space=pltpu.SMEM), NEAR],
        out_specs=[NEAR, FAR],
        out_shape=[
            pltpu.VMEM((shards, slab, PIECE), F32),
            jax.ShapeDtypeStruct((8, PIECE), F32),
        ],
        compiler_params=pltpu.CompilerParams(vmem_limit_bytes=60 << 20),
        name="prefix",
    )(own, near(spread.astype(F32)))

    back = lax.all_to_all(before.astype(F16), "seq", split_axis=0, concat_axis=0, tiled=True)

    num, line = pl.pallas_call(
        inside_kernel,
        in_specs=[NEAR, NEAR, FAR, FAR, FAR, FAR],
        out_specs=[NEAR] * 2,
        out_shape=[
            pltpu.VMEM((steps, PIECE, CHUNK), F32),
            pltpu.VMEM((steps, 8, CHUNK), F32),
        ],
        compiler_params=pltpu.CompilerParams(vmem_limit_bytes=INSIDE_LIMIT),
        name="inside",
    )(near(received), near(other), entry_top, entry_low, aux, normal)

    return pl.pallas_call(
        finish_kernel,
        in_specs=[NEAR] * 5,
        out_specs=pl.BlockSpec(memory_space=pltpu.HBM),
        out_shape=jax.ShapeDtypeStruct((tokens, PIECE), BF16),
        scratch_shapes=[pltpu.VMEM((tokens, PIECE), BF16), pltpu.SemaphoreType.DMA((steps,))],
        compiler_params=PARAMS,
        name="finish",
    )(near(ours), near(other), num, line, near(back.reshape(PIECE, PIECE).astype(F32)))


def solution(mesh):
    spec = P(("seq", "head"), None)

    return jax.shard_map(on_device, mesh=mesh, in_specs=(spec,) * 5, out_specs=P("seq", "head"), check_vma=False)
```

```python
import jax
import jax.numpy as jnp
from jax import lax
from jax.experimental import pallas as pl
from jax.experimental.pallas import tpu as pltpu
from jax.sharding import PartitionSpec as P

VERY_NEGATIVE = -1e30
CHUNK = 256
PIECE = 256
HALF = PIECE // 2
KEYS = PIECE
ASKED = 2 * PIECE
GATES = ASKED + HALF
VMEM_LIMIT = 24 << 20
EXTRA = 128
GATE_ROWS = 8
F32 = jnp.float32
BF16 = jnp.bfloat16
F16 = jnp.float16


def dot(a, b, contract):
    return lax.dot_general(a, b, ((contract[:1], contract[1:]), ((), ())), preferred_element_type=F32)


def halves(x):
    top = x.astype(BF16)
    return top, (x - top.astype(F32)).astype(BF16)


def thirds(x, scale):
    first = x.astype(BF16).astype(F32)
    rest = (x - first) * scale
    second = rest.astype(BF16).astype(F32)
    third = ((rest - second) * scale).astype(BF16).astype(F32)
    return first, second, third


def iota(shape, dim):
    return lax.broadcasted_iota(jnp.int32, shape, dim)


def first_core():
    return lax.rem(lax.axis_index("seq"), 2) == 0


def pack_kernel(q_in, k_in, v_in, gate_in, forget_in, out_ref, q_ref, k_ref, v_ref, gate_ref, forget_ref, sem):
    rows = k_ref.shape[0]
    pairs = (gate_in, gate_ref), (forget_in, forget_ref), (v_in, v_ref), (k_in, k_ref), (q_in, q_ref)
    copies = [pltpu.make_async_copy(a, b, sem.at[n]) for n, (a, b) in enumerate(pairs)]
    for copy in copies:
        copy.start()
    copies[0].wait()
    copies[1].wait()
    parts = []
    for x in (-jnp.log1p(jnp.exp(-forget_ref[...])), gate_ref[...]):
        parts += thirds(x, 1.0)
    for copy in copies[2:]:
        copy.wait()
    row = iota((GATE_ROWS, rows), 0)
    for h in range(k_ref.shape[1] // PIECE):
        area = jnp.zeros((GATE_ROWS, rows), F32)
        for p in range(6):
            area = jnp.where(row == p, parts[p][h : h + 1], area)
        area = area.astype(BF16)
        for u in range(2):
            n = 2 * h + u
            out_ref[n, 0:PIECE, :] = v_ref[:, n * PIECE : (n + 1) * PIECE].T
            for c in range(2):
                left = h * PIECE + (c ^ u) * HALF
                out_ref[n, KEYS + c * HALF : KEYS + (c + 1) * HALF, :] = k_ref[:, left : left + HALF]
            left = h * PIECE + u * HALF
            out_ref[n, ASKED:GATES, :] = q_ref[:, left : left + HALF].T
            out_ref[n, GATES : GATES + GATE_ROWS, :] = area


def beside(ref, blocks, low, high):
    return jnp.concatenate([ref[b, low:high, :] for b in blocks], axis=1)


def key_rows(ref, blocks):
    return jnp.concatenate(
        [
            jnp.concatenate([ref[b, KEYS + c * HALF : KEYS + (c + 1) * HALF, :] for c in range(2)], axis=1)
            for b in blocks
        ],
        axis=0,
    )


def asked_rows(ref, other_ref, blocks):
    return jnp.concatenate([beside(ref, blocks, ASKED, GATES), beside(other_ref, blocks, 0, HALF)], axis=0)


def chunk_blocks(ref, chunk):
    group = CHUNK // ref.shape[2]
    return range(chunk * group, (chunk + 1) * group)


def weighted_values(turned, weight):
    top, low = halves(turned.astype(F32) * weight)
    first, second, third = thirds(weight, 1.0)
    row = iota((8, weight.shape[1]), 0)
    left = jnp.where(row == 0, first, jnp.where(row == 1, third, 0.0)).astype(BF16)
    right = jnp.where(row == 0, second, 0.0).astype(BF16)
    return jnp.concatenate(
        [jnp.concatenate([top, left], axis=0), jnp.concatenate([low, right], axis=0)], axis=1
    )


def summary_kernel(r_ref, mine_ref, send_ref):
    sources, rows = r_ref.shape[0], r_ref.shape[2]
    decay = [r_ref[:, GATES + p, :] for p in range(3)]
    gate = [r_ref[:, GATES + 3 + p, :].astype(F32) for p in range(3)]
    gate = gate[0] + gate[1] + gate[2]
    after = (iota((rows, rows), 0) > iota((rows, rows), 1)).astype(BF16)
    later = (iota((sources, sources), 1) > iota((sources, sources), 0)).astype(BF16)
    suffix = sum(dot(d, after, (1, 0)) for d in decay)
    rest = sum(dot(later, d, (1, 0)) for d in decay)
    total = sum(jnp.sum(d.astype(F32), axis=0, keepdims=True) for d in decay)
    total = jnp.sum(total, axis=1, keepdims=True)
    tail = suffix + jnp.sum(rest, axis=1, keepdims=True) + gate
    new_m = jnp.max(jnp.max(tail, axis=1, keepdims=True), axis=0, keepdims=True)
    weight = jnp.exp(tail - new_m)
    state = jnp.zeros((PIECE + 8, PIECE), F32)
    for g in range(sources * rows // CHUNK):
        mine = chunk_blocks(r_ref, g)
        turned = beside(r_ref, mine, 0, PIECE)
        share = jnp.concatenate([weight[b : b + 1, :] for b in mine], axis=1)
        keys = key_rows(r_ref, mine)
        state = state + dot(
            weighted_values(turned, share), jnp.concatenate([keys, keys], axis=0), (1, 0)
        )
    c_new = state[0:PIECE]
    n_new = state[PIECE : PIECE + 1] + state[PIECE + 1 : PIECE + 2]

    place = iota((8, PIECE), 0)
    rest = jnp.where(place == 0, n_new, jnp.where(place == 1, new_m, total))
    first = first_core()
    low, high = c_new[0:HALF], c_new[HALF:PIECE]
    mine_ref[0:HALF, :] = jnp.where(first, low, high)
    send_ref[0:HALF, :] = jnp.where(first, high, low)
    mine_ref[HALF:, :] = rest
    send_ref[HALF:, :] = rest


def pair_kernel(mine_ref, theirs_ref, z_ref, first_ref):
    first = first_core()
    mine, theirs = mine_ref[...], theirs_ref[...]
    early = jnp.where(first, mine, theirs)
    late = jnp.where(first, theirs, mine)
    first_ref[...] = early
    late_f = late[HALF + 2 : HALF + 3, 0:1]
    moved = early[HALF + 1 : HALF + 2, 0:1] + late_f
    late_m = late[HALF + 1 : HALF + 2, 0:1]
    new_m = jnp.maximum(moved, late_m)
    joined = jnp.exp(moved - new_m) * early + jnp.exp(late_m - new_m) * late
    c_new = joined[0:HALF]
    n_new = joined[HALF : HALF + 1]
    total = early[HALF + 2 : HALF + 3, 0:1] + late_f
    count, slab = z_ref.shape[0], z_ref.shape[1]
    most = jnp.max(jnp.max(jnp.abs(c_new), axis=1, keepdims=True), axis=0, keepdims=True)
    scaled = c_new * jnp.where(most > 0.0, 1.0 / most, 0.0)
    z_ref[:, :, 0:PIECE] = scaled.reshape(count, slab, PIECE)
    place = iota((slab, EXTRA), 0)
    lane = iota((slab, EXTRA), 1)
    extra = jnp.zeros((slab, EXTRA), F32)
    for p, part in enumerate(thirds(n_new, 256.0)):
        for h in range(PIECE // EXTRA):
            extra = jnp.where(place == 2 * p + h, part[:, h * EXTRA : (h + 1) * EXTRA], extra)
    for n, x in enumerate((new_m, total, most * 0.25)):
        for p, part in enumerate(thirds(x, 256.0)):
            extra = jnp.where((place == 6) & (lane == 3 * n + p), part, extra)
    z_ref[:, :, PIECE:] = jnp.broadcast_to(extra[None], (count, slab, EXTRA))


def entries_kernel(r_ref, top_ref, low_ref, aux_ref):
    upper = (iota((CHUNK, CHUNK), 0) <= iota((CHUNK, CHUNK), 1)).astype(BF16)
    row = iota((8, CHUNK), 0)
    state = jnp.zeros((PIECE, PIECE), F32)
    normal = jnp.zeros((1, PIECE), F32)
    old_m = jnp.full((1, 1), VERY_NEGATIVE, F32)
    start = jnp.zeros((1, 1), F32)
    steps = top_ref.shape[0]
    for step in range(steps):
        mine = chunk_blocks(r_ref, step)
        top_ref[step], low_ref[step] = halves(state)
        gates = beside(r_ref, mine, GATES, GATES + GATE_ROWS)
        cum = dot(gates, upper, (1, 0))
        cum = cum[0:1] + cum[1:2] + cum[2:3]
        gate = gates.astype(F32)
        gate = gate[3:4] + gate[4:5] + gate[5:6]
        total = cum[:, CHUNK - 1 : CHUNK]
        tail = total - cum + gate
        new_m = jnp.maximum(old_m + total, jnp.max(tail, axis=1, keepdims=True))
        keep = jnp.exp(old_m + total - new_m)
        aux = jnp.where(row == 0, normal, 0.0)
        for p, x in ((1, old_m), (2, start), (3, cum), (4, gate - cum)):
            aux = jnp.where(row == p, x, aux)
        aux_ref[step] = aux
        if step < steps - 1:
            keys = key_rows(r_ref, mine)
            fresh = dot(
                weighted_values(beside(r_ref, mine, 0, PIECE), jnp.exp(tail - new_m)),
                jnp.concatenate([keys, keys], axis=0),
                (1, 0),
            )
            state = keep * state + fresh[0:PIECE]
            normal = keep * normal + fresh[PIECE : PIECE + 1] + fresh[PIECE + 1 : PIECE + 2]
            old_m = new_m
            start = start + total


def prefix_kernel(z_ref, first_ref, y_ref, nin_ref):
    count, slab, _ = z_ref.shape
    own = lax.axis_index("seq") // 2
    second = jnp.logical_not(first_core())
    small = 1.0 / 256.0

    def joined(a, b, c):
        return a + (b + c * small) * small

    scalars = z_ref[:, 6, PIECE:]
    columns = [scalars[:, p : p + 1] for p in range(9)]
    m = joined(*columns[0:3])
    most = joined(*columns[6:9]) * 4.0
    shard = iota((count, EXTRA), 0)
    later = iota((count, EXTRA), 1)
    before = shard < later
    after = (iota((count, count), 1) > iota((count, count), 0)).astype(BF16)
    gap = joined(
        *(dot(after, jnp.where(before, c, 0.0).astype(BF16), (1, 0)) for c in columns[3:6])
    )
    reach = jnp.where(before, m + gap, VERY_NEGATIVE)
    top = jnp.max(reach, axis=0, keepdims=True)
    weight = jnp.where(before, jnp.exp(reach - top), 0.0)
    heavy = weight * most
    bound = jnp.sum(heavy, axis=0, keepdims=True)
    heavy = heavy * jnp.where(bound > 0.0, 1.0 / bound, 0.0)
    size = count * slab
    shift = slab.bit_length() - 1
    down = (iota((size, count), 0) >> shift == iota((size, count), 1)).astype(BF16)
    right = (iota((count, size), 0) == iota((count, size), 1) >> shift).astype(BF16)
    same = (iota((size, size), 0) & (slab - 1)) == (iota((size, size), 1) & (slab - 1))
    turned = heavy.T[0:count, :]
    wide = []
    for x in halves(turned):
        x = dot(dot(down, x, (1, 0)).astype(BF16), right, (1, 0))
        wide.append(jnp.where(same, x, 0.0).astype(BF16))
    x_top, x_low = halves(z_ref[:, :, 0:PIECE].reshape(size, PIECE))
    y = dot(
        jnp.concatenate([wide[0], wide[1], wide[0]], axis=1),
        jnp.concatenate([x_top, x_top, x_low], axis=0),
        (1, 0),
    )
    y_ref[...] = y.reshape(count, slab, PIECE)

    mine = iota((1, EXTRA), 1) == own
    column = jnp.sum(jnp.where(mine, weight, 0.0), axis=1, keepdims=True)
    row = iota((8, EXTRA), 0)
    own_top = jnp.sum(jnp.where(mine, top, 0.0), axis=1, keepdims=True)
    own_bound = jnp.sum(jnp.where(mine, bound, 0.0), axis=1, keepdims=True)
    first_m = first_ref[HALF + 1 : HALF + 2, 0:1]
    moved = own_top + first_ref[HALF + 2 : HALF + 3, 0:1]
    next_top = jnp.maximum(moved, first_m)
    old_share = jnp.exp(moved - next_top)
    new_share = jnp.exp(first_m - next_top)
    for h in range(PIECE // EXTRA):
        lanes = slice(h * EXTRA, (h + 1) * EXTRA)
        n = joined(*(z_ref[:, 2 * p + h, PIECE:] for p in range(3)))
        n = jnp.sum(column * n, axis=0, keepdims=True)
        n = jnp.where(second, old_share * n + new_share * first_ref[HALF : HALF + 1, lanes], n)
        area = jnp.where(row == 6, jnp.where(second, next_top, own_top), own_bound)
        for p, part in enumerate((old_share, new_share)):
            area = jnp.where(row == p, part, area)
        for p, part in enumerate(thirds(n, 1.0)):
            area = jnp.where(row == 3 + p, part, area)
        nin_ref[:, lanes] = area


def mix_kernel(p_ref, first_ref, nin_ref, keep_ref, send_ref):
    before = p_ref[...] * nin_ref[2:3, 0:1]
    after = before * nin_ref[0:1, 0:1] + first_ref[0:HALF, :] * nin_ref[1:2, 0:1]
    first = first_core()
    keep_ref[...] = jnp.where(first, before, after)
    send_ref[...] = jnp.where(first, after, before)


def inside_kernel(r_ref, other_ref, top_ref, low_ref, aux_ref, nin_ref, num_ref, row_ref):
    factor = PIECE**-0.5
    before = nin_ref[...]
    before_m = before[6:7, 0:1]
    causal = iota((CHUNK, CHUNK), 0) <= iota((CHUNK, CHUNK), 1)
    row = iota((8, CHUNK), 0)
    for step in range(num_ref.shape[0]):
        mine = chunk_blocks(r_ref, step)
        asked = asked_rows(r_ref, other_ref, mine)
        turned = beside(r_ref, mine, 0, PIECE)
        aux = aux_ref[step]
        cum = aux[3:4]
        carried = cum + aux[1:2]
        score = dot(key_rows(r_ref, mine), asked, (1, 0))
        gap = jnp.where(causal, aux.T[:, 4:5] + cum, VERY_NEGATIVE)
        top = jnp.maximum(carried, jnp.max(gap, axis=0, keepdims=True))
        weighted = jnp.exp(gap - top) * score
        outside = jnp.exp(carried - top)
        normal = jnp.where((row >= 3) & (row < 6), before, 0.0)
        for p, part in enumerate(thirds(aux[0:1], 1.0)):
            normal = jnp.where(row == p, part, normal)
        reached = dot(normal.astype(BF16), asked, (1, 0))
        den = jnp.sum(weighted, axis=0, keepdims=True)
        den = factor * (den + outside * (reached[0:1] + reached[1:2] + reached[2:3]))
        carried = cum + aux[2:3] + before_m
        new_m = jnp.maximum(top, carried)
        inside = jnp.exp(top - new_m)
        ahead = jnp.exp(carried - new_m) * factor
        den = den * inside + ahead * (reached[3:4] + reached[4:5] + reached[5:6])
        over = 1.0 / jnp.maximum(jnp.abs(den), 1.0)
        inside = inside * over * factor
        num = dot(
            jnp.concatenate([turned, turned], axis=1),
            jnp.concatenate(halves(weighted), axis=0),
            (1, 0),
        )
        read = dot(
            jnp.concatenate([top_ref[step], low_ref[step]], axis=1),
            jnp.concatenate([asked, asked], axis=0),
            (1, 0),
        )
        num_ref[step] = inside * num + (inside * outside) * read
        row_ref[step] = jnp.broadcast_to(ahead * over, (8, CHUNK))


def finish_kernel(
    own_in, other_in, num_in, row_in, keep_ref, came_ref, out_ref,
    own_ref, other_ref, num_ref, row_ref, buffer_ref, in_sem, out_sem,
):
    steps = num_ref.shape[0]
    group = own_ref.shape[0] // steps
    row_copy = pltpu.make_async_copy(row_in, row_ref, in_sem.at[3 * steps])
    row_copy.start()
    arriving = []
    for step in range(steps):
        blocks = pl.ds(step * group, group)
        pairs = (
            (own_in.at[blocks], own_ref.at[blocks]),
            (other_in.at[blocks], other_ref.at[blocks]),
            (num_in.at[step], num_ref.at[step]),
        )
        arriving.append(
            [pltpu.make_async_copy(a, b, in_sem.at[3 * step + n]) for n, (a, b) in enumerate(pairs)]
        )
        for copy in arriving[-1]:
            copy.start()
    first = first_core()
    keep, came = keep_ref[...], came_ref[...]
    state = jnp.concatenate([jnp.where(first, keep, came), jnp.where(first, came, keep)], axis=0)
    both = jnp.concatenate(halves(state), axis=1)
    row_copy.wait()
    leaving = []
    for step in range(steps):
        for copy in arriving[step]:
            copy.wait()
        blocks = chunk_blocks(own_ref, step)
        asked = jnp.concatenate(
            [beside(own_ref, blocks, 0, HALF), beside(other_ref, blocks, 0, HALF)], axis=0
        )
        read = dot(both, jnp.concatenate([asked, asked], axis=0), (1, 0))
        out = num_ref[step] + read * row_ref[step, 0:1, :]
        here = pl.ds(step * CHUNK, CHUNK)
        buffer_ref[here, :] = out.astype(BF16).T
        leaving.append(pltpu.make_async_copy(buffer_ref.at[here], out_ref.at[here], out_sem.at[step]))
        leaving[-1].start()
    for copy in leaving:
        copy.wait()


def far(x):
    return pltpu.with_memory_space_constraint(x, pltpu.HBM)


def near(x):
    return pltpu.with_memory_space_constraint(x, pltpu.VMEM)


NEAR = pl.BlockSpec(memory_space=pltpu.VMEM)
FAR = pl.BlockSpec()
PARAMS = pltpu.CompilerParams(vmem_limit_bytes=VMEM_LIMIT)


def on_device(queries, keys, values, input_pre, forget_pre):
    rows = queries.shape[0]
    pieces = lax.axis_size("head")
    shards = lax.axis_size("seq")
    tokens = pieces * rows
    steps = tokens // CHUNK
    tall = GATES + GATE_ROWS
    chips = shards // 2
    slab = HALF // chips
    pairs = [(i, i ^ 1) for i in range(shards)]
    columns = [[2 * z + c for z in range(chips)] for c in range(2)]
    wide = PIECE + EXTRA

    packed = pl.pallas_call(
        pack_kernel,
        in_specs=[pl.BlockSpec(memory_space=pltpu.HBM)] * 5,
        out_specs=NEAR,
        out_shape=pltpu.VMEM((pieces, tall, rows), BF16),
        scratch_shapes=[
            pltpu.VMEM(queries.shape, BF16),
            pltpu.VMEM(keys.shape, BF16),
            pltpu.VMEM(values.shape, BF16),
            pltpu.VMEM((input_pre.shape[1], rows), F32),
            pltpu.VMEM((input_pre.shape[1], rows), F32),
            pltpu.SemaphoreType.DMA((5,)),
        ],
        compiler_params=PARAMS,
        name="pack",
    )(*(far(x) for x in (queries, keys, values, input_pre.T, forget_pre.T)))

    received = lax.all_to_all(packed, "head", split_axis=0, concat_axis=0, tiled=True)

    half = pltpu.VMEM((HALF + 8, PIECE), F32)
    mine, send = pl.pallas_call(
        summary_kernel,
        in_specs=[NEAR],
        out_specs=[NEAR] * 2,
        out_shape=[half] * 2,
        compiler_params=PARAMS,
        name="summary",
    )(near(received))

    theirs = lax.ppermute(send, "seq", pairs)

    summary, first = pl.pallas_call(
        pair_kernel,
        in_specs=[NEAR, NEAR],
        out_specs=[NEAR, FAR],
        out_shape=[
            pltpu.VMEM((chips, slab, wide), F32),
            jax.ShapeDtypeStruct((HALF + 8, PIECE), F32),
        ],
        compiler_params=PARAMS,
        name="pair",
    )(mine, near(theirs))

    spread = lax.all_to_all(
        summary.astype(F16),
        "seq",
        split_axis=0,
        concat_axis=0,
        tiled=True,
        axis_index_groups=columns,
    )

    ours = received[:, ASKED:GATES, :]
    other = lax.ppermute(ours, "head", [(i, i ^ 1) for i in range(pieces)])

    entry_top, entry_low, aux = pl.pallas_call(
        entries_kernel,
        in_specs=[NEAR],
        out_specs=[FAR] * 3,
        out_shape=[
            jax.ShapeDtypeStruct((steps, PIECE, PIECE), BF16),
            jax.ShapeDtypeStruct((steps, PIECE, PIECE), BF16),
            jax.ShapeDtypeStruct((steps, 8, CHUNK), F32),
        ],
        name="entries",
    )(near(received))

    before, normal = pl.pallas_call(
        prefix_kernel,
        in_specs=[NEAR, NEAR],
        out_specs=[NEAR, FAR],
        out_shape=[
            pltpu.VMEM((chips, slab, PIECE), F32),
            jax.ShapeDtypeStruct((8, PIECE), F32),
        ],
        compiler_params=pltpu.CompilerParams(vmem_limit_bytes=60 << 20),
        name="prefix",
    )(near(spread.astype(F32)), near(first))

    back = lax.all_to_all(before.astype(F16), "seq", split_axis=0, concat_axis=0, tiled=True, axis_index_groups=columns)

    keep, lend = pl.pallas_call(
        mix_kernel,
        in_specs=[NEAR] * 3,
        out_specs=[NEAR] * 2,
        out_shape=[pltpu.VMEM((HALF, PIECE), F32)] * 2,
        compiler_params=PARAMS,
        name="mix",
    )(near(back.reshape(HALF, PIECE).astype(F32)), near(first), near(normal))
    came = lax.ppermute(lend, "seq", pairs)

    num, line = pl.pallas_call(
        inside_kernel,
        in_specs=[NEAR, NEAR, FAR, FAR, FAR, FAR],
        out_specs=[FAR] * 2,
        out_shape=[
            jax.ShapeDtypeStruct((steps, PIECE, CHUNK), F32),
            jax.ShapeDtypeStruct((steps, 8, CHUNK), F32),
        ],
        name="inside",
    )(near(received), near(other), entry_top, entry_low, aux, normal)

    return pl.pallas_call(
        finish_kernel,
        in_specs=[pl.BlockSpec(memory_space=pltpu.HBM)] * 4 + [NEAR] * 2,
        out_specs=pl.BlockSpec(memory_space=pltpu.HBM),
        out_shape=jax.ShapeDtypeStruct((tokens, PIECE), BF16),
        scratch_shapes=[
            pltpu.VMEM(ours.shape, BF16),
            pltpu.VMEM(ours.shape, BF16),
            pltpu.VMEM(num.shape, F32),
            pltpu.VMEM(line.shape, F32),
            pltpu.VMEM((tokens, PIECE), BF16),
            pltpu.SemaphoreType.DMA((3 * steps + 1,)),
            pltpu.SemaphoreType.DMA((steps,)),
        ],
        compiler_params=PARAMS,
        name="finish",
    )(far(ours), far(other), far(num), far(line), keep, near(came))


def solution(mesh):
    spec = P(("seq", "head"), None)

    return jax.shard_map(on_device, mesh=mesh, in_specs=(spec,) * 5, out_specs=P("seq", "head"), check_vma=False)
```

```python
import jax
import jax.numpy as jnp
from jax import lax
from jax.experimental import pallas as pl
from jax.experimental.pallas import tpu as pltpu
from jax.sharding import PartitionSpec as P

VERY_NEGATIVE = -1e30
CHUNK = 256
PIECE = 256
HALF = PIECE // 2
KEYS = PIECE
ASKED = 2 * PIECE
GATES = ASKED + HALF
VMEM_LIMIT = 24 << 20
INSIDE_LIMIT = 56 << 20
FAR_LIMIT = 59 << 20
NEAR_CHIPS = 4
GATE_ROWS = 8
F32 = jnp.float32
BF16 = jnp.bfloat16


def dot(a, b, contract):
    return lax.dot_general(a, b, ((contract[:1], contract[1:]), ((), ())), preferred_element_type=F32)


def halves(x):
    top = x.astype(BF16)
    return top, (x - top.astype(F32)).astype(BF16)


def thirds(x, scale):
    first = x.astype(BF16).astype(F32)
    rest = (x - first) * scale
    second = rest.astype(BF16).astype(F32)
    third = ((rest - second) * scale).astype(BF16).astype(F32)
    return first, second, third


def iota(shape, dim):
    return lax.broadcasted_iota(jnp.int32, shape, dim)


def first_core():
    return lax.rem(lax.axis_index("seq"), 2) == 0


def pack_kernel(q_in, k_in, v_in, gate_in, forget_in, out_ref, q_ref, k_ref, v_ref, gate_ref, forget_ref, sem):
    rows = k_ref.shape[0]
    pairs = (gate_in, gate_ref), (forget_in, forget_ref), (v_in, v_ref), (k_in, k_ref), (q_in, q_ref)
    copies = [pltpu.make_async_copy(a, b, sem.at[n]) for n, (a, b) in enumerate(pairs)]
    for copy in copies:
        copy.start()
    copies[0].wait()
    copies[1].wait()
    parts = []
    for x in (-jnp.log1p(jnp.exp(-forget_ref[...])), gate_ref[...]):
        parts += thirds(x, 1.0)
    for copy in copies[2:]:
        copy.wait()
    row = iota((GATE_ROWS, rows), 0)
    for h in range(k_ref.shape[1] // PIECE):
        area = jnp.zeros((GATE_ROWS, rows), F32)
        for p in range(6):
            area = jnp.where(row == p, parts[p][h : h + 1], area)
        area = area.astype(BF16)
        for u in range(2):
            n = 2 * h + u
            out_ref[n, 0:PIECE, :] = v_ref[:, n * PIECE : (n + 1) * PIECE].T
            for c in range(2):
                left = h * PIECE + (c ^ u) * HALF
                out_ref[n, KEYS + c * HALF : KEYS + (c + 1) * HALF, :] = k_ref[:, left : left + HALF]
            left = h * PIECE + u * HALF
            out_ref[n, ASKED:GATES, :] = q_ref[:, left : left + HALF].T
            out_ref[n, GATES : GATES + GATE_ROWS, :] = area


def beside(ref, blocks, low, high):
    return jnp.concatenate([ref[b, low:high, :] for b in blocks], axis=1)


def key_rows(ref, blocks):
    return jnp.concatenate(
        [
            jnp.concatenate([ref[b, KEYS + c * HALF : KEYS + (c + 1) * HALF, :] for c in range(2)], axis=1)
            for b in blocks
        ],
        axis=0,
    )


def asked_rows(ref, other_ref, blocks):
    return jnp.concatenate([beside(ref, blocks, ASKED, GATES), beside(other_ref, blocks, 0, HALF)], axis=0)


def chunk_blocks(ref, chunk):
    group = CHUNK // ref.shape[2]
    return range(chunk * group, (chunk + 1) * group)


def weighted_values(turned, weight):
    top, low = halves(turned.astype(F32) * weight)
    first, second, third = thirds(weight, 1.0)
    row = iota((8, weight.shape[1]), 0)
    left = jnp.where(row == 0, first, jnp.where(row == 1, third, 0.0)).astype(BF16)
    right = jnp.where(row == 0, second, 0.0).astype(BF16)
    return jnp.concatenate(
        [jnp.concatenate([top, left], axis=0), jnp.concatenate([low, right], axis=0)], axis=1
    )


def summary_kernel(r_ref, mine_ref, send_ref):
    sources, rows = r_ref.shape[0], r_ref.shape[2]
    decay = [r_ref[:, GATES + p, :] for p in range(3)]
    gate = [r_ref[:, GATES + 3 + p, :].astype(F32) for p in range(3)]
    gate = gate[0] + gate[1] + gate[2]
    after = (iota((rows, rows), 0) > iota((rows, rows), 1)).astype(BF16)
    later = (iota((sources, sources), 1) > iota((sources, sources), 0)).astype(BF16)
    suffix = sum(dot(d, after, (1, 0)) for d in decay)
    rest = sum(dot(later, d, (1, 0)) for d in decay)
    total = sum(jnp.sum(d.astype(F32), axis=0, keepdims=True) for d in decay)
    total = jnp.sum(total, axis=1, keepdims=True)
    tail = suffix + jnp.sum(rest, axis=1, keepdims=True) + gate
    new_m = jnp.max(jnp.max(tail, axis=1, keepdims=True), axis=0, keepdims=True)
    weight = jnp.exp(tail - new_m)
    state = jnp.zeros((PIECE + 8, PIECE), F32)
    for g in range(sources * rows // CHUNK):
        mine = chunk_blocks(r_ref, g)
        turned = beside(r_ref, mine, 0, PIECE)
        share = jnp.concatenate([weight[b : b + 1, :] for b in mine], axis=1)
        keys = key_rows(r_ref, mine)
        state = state + dot(
            weighted_values(turned, share), jnp.concatenate([keys, keys], axis=0), (1, 0)
        )
    c_new = state[0:PIECE]
    n_new = state[PIECE : PIECE + 1] + state[PIECE + 1 : PIECE + 2]

    place = iota((8, PIECE), 0)
    rest = jnp.where(place == 0, n_new, jnp.where(place == 1, new_m, total))
    first = first_core()
    low, high = c_new[0:HALF], c_new[HALF:PIECE]
    mine_ref[0:HALF, :] = jnp.where(first, low, high)
    send_ref[0:HALF, :] = jnp.where(first, high, low)
    mine_ref[HALF:, :] = rest
    send_ref[HALF:, :] = rest


def scalar(rows, n):
    return rows[n : n + 1, 0:1]


def pair_kernel(mine_ref, theirs_ref, z_ref, first_ref):
    first = first_core()
    mine, theirs = mine_ref[...], theirs_ref[...]
    early = jnp.where(first, mine, theirs)
    late = jnp.where(first, theirs, mine)
    first_ref[...] = early
    late_f = scalar(late, HALF + 2)
    moved = scalar(early, HALF + 1) + late_f
    late_m = scalar(late, HALF + 1)
    new_m = jnp.maximum(moved, late_m)
    joined = jnp.exp(moved - new_m) * early + jnp.exp(late_m - new_m) * late
    count, slab = z_ref.shape[0], z_ref.shape[1] - 8
    place = iota((8, PIECE), 0)
    rest = jnp.where(place == 1, new_m, scalar(early, HALF + 2) + late_f)
    rest = jnp.where(place == 0, joined[HALF : HALF + 1], rest)
    for i in range(count):
        z_ref[i, 0:slab, :] = joined[i * slab : (i + 1) * slab]
        z_ref[i, slab:, :] = rest


def entries_kernel(r_ref, top_ref, low_ref, aux_ref):
    upper = (iota((CHUNK, CHUNK), 0) <= iota((CHUNK, CHUNK), 1)).astype(BF16)
    row = iota((8, CHUNK), 0)
    state = jnp.zeros((PIECE, PIECE), F32)
    normal = jnp.zeros((1, PIECE), F32)
    old_m = jnp.full((1, 1), VERY_NEGATIVE, F32)
    start = jnp.zeros((1, 1), F32)
    steps = top_ref.shape[0]
    for step in range(steps):
        mine = chunk_blocks(r_ref, step)
        top_ref[step], low_ref[step] = halves(state)
        gates = beside(r_ref, mine, GATES, GATES + GATE_ROWS)
        cum = dot(gates, upper, (1, 0))
        cum = cum[0:1] + cum[1:2] + cum[2:3]
        gate = gates.astype(F32)
        gate = gate[3:4] + gate[4:5] + gate[5:6]
        total = cum[:, CHUNK - 1 : CHUNK]
        tail = total - cum + gate
        new_m = jnp.maximum(old_m + total, jnp.max(tail, axis=1, keepdims=True))
        keep = jnp.exp(old_m + total - new_m)
        aux = jnp.where(row == 0, normal, 0.0)
        for p, x in ((1, old_m), (2, start), (3, cum), (4, gate - cum)):
            aux = jnp.where(row == p, x, aux)
        aux_ref[step] = aux
        if step < steps - 1:
            keys = key_rows(r_ref, mine)
            fresh = dot(
                weighted_values(beside(r_ref, mine, 0, PIECE), jnp.exp(tail - new_m)),
                jnp.concatenate([keys, keys], axis=0),
                (1, 0),
            )
            state = keep * state + fresh[0:PIECE]
            normal = keep * normal + fresh[PIECE : PIECE + 1] + fresh[PIECE + 1 : PIECE + 2]
            old_m = new_m
            start = start + total


def near_kernel(z_ref, sum_ref, y_ref, meta_ref):
    count, slab = z_ref.shape[0], z_ref.shape[1] - 8
    state = jnp.zeros((slab, PIECE), F32)
    normal = jnp.zeros((1, PIECE), F32)
    old_m = jnp.full((1, 1), VERY_NEGATIVE, F32)
    total = jnp.zeros((1, 1), F32)
    for i in range(count):
        y_ref[i] = state
        for n, x in enumerate((old_m, total, normal)):
            meta_ref[n * count + i : n * count + i + 1, :] = jnp.broadcast_to(x, (1, PIECE))
        rest = z_ref[i, slab:, :]
        m, f = scalar(rest, 1), scalar(rest, 2)
        new_m = jnp.maximum(old_m + f, m)
        keep, take = jnp.exp(old_m + f - new_m), jnp.exp(m - new_m)
        state = keep * state + take * z_ref[i, 0:slab, :]
        normal = keep * normal + take * rest[0:1]
        old_m = new_m
        total = total + f
    place = iota((8, PIECE), 0)
    sum_ref[0:slab, :] = state
    sum_ref[slab:, :] = jnp.where(place == 0, normal, jnp.where(place == 1, old_m, total))


def far_kernel(*refs):
    y_ref, meta_ref, first_ref, *ahead, out_ref, nin_ref = refs
    count, slab = y_ref.shape[0], y_ref.shape[1]
    chip = lax.axis_index("seq") // 2
    near_at, group = lax.rem(chip, count), chip // count
    second = jnp.logical_not(first_core())
    state = jnp.zeros((slab, PIECE), F32)
    normal = jnp.zeros((1, PIECE), F32)
    old_m = jnp.full((1, 1), VERY_NEGATIVE, F32)
    for d in range(len(ahead), 0, -1):
        there = group >= d
        rest = ahead[d - 1][slab:, :]
        m = jnp.where(there, scalar(rest, 1), VERY_NEGATIVE)
        f = jnp.where(there, scalar(rest, 2), 0.0)
        new_m = jnp.maximum(old_m + f, m)
        keep, take = jnp.exp(old_m + f - new_m), jnp.exp(m - new_m)
        state = keep * state + take * ahead[d - 1][0:slab, :]
        normal = keep * normal + take * rest[0:1]
        old_m = new_m
    meta = meta_ref[...]
    own_m = jnp.full((1, 1), VERY_NEGATIVE, F32)
    own_n = jnp.zeros((1, PIECE), F32)
    for i in range(count):
        m, f = scalar(meta, i), scalar(meta, count + i)
        new_m = jnp.maximum(old_m + f, m)
        keep, take = jnp.exp(old_m + f - new_m), jnp.exp(m - new_m)
        out_ref[i] = keep * state + take * y_ref[i]
        n = keep * normal + take * meta[2 * count + i : 2 * count + i + 1]
        own_m = jnp.where(near_at == i, new_m, own_m)
        own_n = jnp.where(near_at == i, n, own_n)
    first_m = scalar(first_ref, HALF + 1)
    moved = own_m + scalar(first_ref, HALF + 2)
    next_m = jnp.maximum(moved, first_m)
    old_share, new_share = jnp.exp(moved - next_m), jnp.exp(first_m - next_m)
    next_n = old_share * own_n + new_share * first_ref[HALF : HALF + 1, :]
    place = iota((8, PIECE), 0)
    area = jnp.where(place == 0, old_share, new_share)
    area = jnp.where(place == 6, jnp.where(second, next_m, own_m), area)
    for p, part in enumerate(thirds(jnp.where(second, next_n, own_n), 1.0)):
        area = jnp.where(place == 3 + p, part, area)
    nin_ref[...] = area


def mix_kernel(p_ref, first_ref, nin_ref, keep_ref, send_ref):
    before = p_ref[...]
    after = before * nin_ref[0:1, 0:1] + first_ref[0:HALF, :] * nin_ref[1:2, 0:1]
    first = first_core()
    keep_ref[...] = jnp.where(first, before, after)
    send_ref[...] = jnp.where(first, after, before)


def inside_kernel(r_ref, other_ref, top_ref, low_ref, aux_ref, nin_ref, num_ref, row_ref):
    factor = PIECE**-0.5
    before = nin_ref[...]
    before_m = before[6:7, 0:1]
    causal = iota((CHUNK, CHUNK), 0) <= iota((CHUNK, CHUNK), 1)
    row = iota((8, CHUNK), 0)
    for step in range(num_ref.shape[0]):
        mine = chunk_blocks(r_ref, step)
        asked = asked_rows(r_ref, other_ref, mine)
        turned = beside(r_ref, mine, 0, PIECE)
        aux = aux_ref[step]
        cum = aux[3:4]
        carried = cum + aux[1:2]
        score = dot(key_rows(r_ref, mine), asked, (1, 0))
        gap = jnp.where(causal, aux.T[:, 4:5] + cum, VERY_NEGATIVE)
        top = jnp.maximum(carried, jnp.max(gap, axis=0, keepdims=True))
        weighted = jnp.exp(gap - top) * score
        outside = jnp.exp(carried - top)
        normal = jnp.where((row >= 3) & (row < 6), before, 0.0)
        for p, part in enumerate(thirds(aux[0:1], 1.0)):
            normal = jnp.where(row == p, part, normal)
        reached = dot(normal.astype(BF16), asked, (1, 0))
        den = jnp.sum(weighted, axis=0, keepdims=True)
        den = factor * (den + outside * (reached[0:1] + reached[1:2] + reached[2:3]))
        carried = cum + aux[2:3] + before_m
        new_m = jnp.maximum(top, carried)
        inside = jnp.exp(top - new_m)
        ahead = jnp.exp(carried - new_m) * factor
        den = den * inside + ahead * (reached[3:4] + reached[4:5] + reached[5:6])
        over = 1.0 / jnp.maximum(jnp.abs(den), 1.0)
        inside = inside * over * factor
        num = dot(
            jnp.concatenate([turned, turned], axis=1),
            jnp.concatenate(halves(weighted), axis=0),
            (1, 0),
        )
        read = dot(
            jnp.concatenate([top_ref[step], low_ref[step]], axis=1),
            jnp.concatenate([asked, asked], axis=0),
            (1, 0),
        )
        num_ref[step] = inside * num + (inside * outside) * read
        row_ref[step] = jnp.broadcast_to(ahead * over, (8, CHUNK))


def finish_kernel(
    own_in, other_in, num_ref, row_ref, keep_ref, came_ref, out_ref,
    own_ref, other_ref, buffer_ref, in_sem, out_sem,
):
    steps = num_ref.shape[0]
    group = own_ref.shape[0] // steps
    arriving = []
    for step in range(steps):
        blocks = pl.ds(step * group, group)
        pairs = (
            (own_in.at[blocks], own_ref.at[blocks]),
            (other_in.at[blocks], other_ref.at[blocks]),
        )
        arriving.append(
            [pltpu.make_async_copy(a, b, in_sem.at[2 * step + n]) for n, (a, b) in enumerate(pairs)]
        )
        for copy in arriving[-1]:
            copy.start()
    first = first_core()
    keep, came = keep_ref[...], came_ref[...]
    state = jnp.concatenate([jnp.where(first, keep, came), jnp.where(first, came, keep)], axis=0)
    both = jnp.concatenate(halves(state), axis=1)
    leaving = []
    for step in range(steps):
        for copy in arriving[step]:
            copy.wait()
        blocks = chunk_blocks(own_ref, step)
        asked = jnp.concatenate(
            [beside(own_ref, blocks, 0, HALF), beside(other_ref, blocks, 0, HALF)], axis=0
        )
        read = dot(both, jnp.concatenate([asked, asked], axis=0), (1, 0))
        out = num_ref[step] + read * row_ref[step, 0:1, :]
        here = pl.ds(step * CHUNK, CHUNK)
        buffer_ref[here, :] = out.astype(BF16).T
        leaving.append(pltpu.make_async_copy(buffer_ref.at[here], out_ref.at[here], out_sem.at[step]))
        leaving[-1].start()
    for copy in leaving:
        copy.wait()


def far(x):
    return pltpu.with_memory_space_constraint(x, pltpu.HBM)


def near(x):
    return pltpu.with_memory_space_constraint(x, pltpu.VMEM)


NEAR = pl.BlockSpec(memory_space=pltpu.VMEM)
FAR = pl.BlockSpec()
PARAMS = pltpu.CompilerParams(vmem_limit_bytes=VMEM_LIMIT)


def on_device(queries, keys, values, input_pre, forget_pre):
    rows = queries.shape[0]
    pieces = lax.axis_size("head")
    shards = lax.axis_size("seq")
    tokens = pieces * rows
    steps = tokens // CHUNK
    tall = GATES + GATE_ROWS
    chips = shards // 2
    close = NEAR_CHIPS
    slab = HALF // close
    pairs = [(i, i ^ 1) for i in range(shards)]
    groups = [
        [2 * (g + z) + c for z in range(close)] for g in range(0, chips, close) for c in range(2)
    ]

    packed = pl.pallas_call(
        pack_kernel,
        in_specs=[pl.BlockSpec(memory_space=pltpu.HBM)] * 5,
        out_specs=NEAR,
        out_shape=pltpu.VMEM((pieces, tall, rows), BF16),
        scratch_shapes=[
            pltpu.VMEM(queries.shape, BF16),
            pltpu.VMEM(keys.shape, BF16),
            pltpu.VMEM(values.shape, BF16),
            pltpu.VMEM((input_pre.shape[1], rows), F32),
            pltpu.VMEM((input_pre.shape[1], rows), F32),
            pltpu.SemaphoreType.DMA((5,)),
        ],
        compiler_params=PARAMS,
        name="pack",
    )(*(far(x) for x in (queries, keys, values, input_pre.T, forget_pre.T)))

    received = lax.all_to_all(packed, "head", split_axis=0, concat_axis=0, tiled=True)

    half = pltpu.VMEM((HALF + 8, PIECE), F32)
    mine, send = pl.pallas_call(
        summary_kernel,
        in_specs=[NEAR],
        out_specs=[NEAR] * 2,
        out_shape=[half] * 2,
        compiler_params=PARAMS,
        name="summary",
    )(near(received))

    theirs = lax.ppermute(send, "seq", pairs)

    summary, first = pl.pallas_call(
        pair_kernel,
        in_specs=[NEAR, NEAR],
        out_specs=[NEAR, FAR],
        out_shape=[
            pltpu.VMEM((close, slab + 8, PIECE), F32),
            jax.ShapeDtypeStruct((HALF + 8, PIECE), F32),
        ],
        compiler_params=PARAMS,
        name="pair",
    )(mine, near(theirs))

    spread = lax.all_to_all(
        summary, "seq", split_axis=0, concat_axis=0, tiled=True, axis_index_groups=groups
    )

    ours = received[:, ASKED:GATES, :]
    other = lax.ppermute(ours, "head", [(i, i ^ 1) for i in range(pieces)])

    entry_top, entry_low, aux = pl.pallas_call(
        entries_kernel,
        in_specs=[NEAR],
        out_specs=[FAR] * 3,
        out_shape=[
            jax.ShapeDtypeStruct((steps, PIECE, PIECE), BF16),
            jax.ShapeDtypeStruct((steps, PIECE, PIECE), BF16),
            jax.ShapeDtypeStruct((steps, 8, CHUNK), F32),
        ],
        name="entries",
    )(near(received))

    group_sum, local, meta = pl.pallas_call(
        near_kernel,
        in_specs=[NEAR],
        out_specs=[NEAR, FAR, FAR],
        out_shape=[
            pltpu.VMEM((slab + 8, PIECE), F32),
            jax.ShapeDtypeStruct((close, slab, PIECE), F32),
            jax.ShapeDtypeStruct((16, PIECE), F32),
        ],
        compiler_params=pltpu.CompilerParams(vmem_limit_bytes=FAR_LIMIT),
        name="near",
    )(near(spread))

    ahead = []
    for d in range(1, chips // close):
        step = 2 * close * d
        ahead.append(lax.ppermute(group_sum, "seq", [(i, i + step) for i in range(shards - step)]))

    before, normal = pl.pallas_call(
        far_kernel,
        in_specs=[FAR, FAR] + [NEAR] * (1 + len(ahead)),
        out_specs=[FAR] * 2,
        out_shape=[
            jax.ShapeDtypeStruct((close, slab, PIECE), F32),
            jax.ShapeDtypeStruct((8, PIECE), F32),
        ],
        compiler_params=pltpu.CompilerParams(vmem_limit_bytes=FAR_LIMIT),
        name="far",
    )(local, meta, near(first), *(near(a) for a in ahead))

    back = lax.all_to_all(
        before, "seq", split_axis=0, concat_axis=0, tiled=True, axis_index_groups=groups
    )

    keep, lend = pl.pallas_call(
        mix_kernel,
        in_specs=[NEAR] * 3,
        out_specs=[NEAR] * 2,
        out_shape=[pltpu.VMEM((HALF, PIECE), F32)] * 2,
        compiler_params=PARAMS,
        name="mix",
    )(near(back.reshape(HALF, PIECE)), near(first), near(normal))
    came = lax.ppermute(lend, "seq", pairs)

    num, line = pl.pallas_call(
        inside_kernel,
        in_specs=[FAR] * 6,
        out_specs=[NEAR] * 2,
        out_shape=[
            pltpu.VMEM((steps, PIECE, CHUNK), F32),
            pltpu.VMEM((steps, 8, CHUNK), F32),
        ],
        compiler_params=pltpu.CompilerParams(vmem_limit_bytes=INSIDE_LIMIT),
        name="inside",
    )(far(received), far(other), entry_top, entry_low, aux, normal)

    return pl.pallas_call(
        finish_kernel,
        in_specs=[pl.BlockSpec(memory_space=pltpu.HBM)] * 2 + [NEAR] * 4,
        out_specs=pl.BlockSpec(memory_space=pltpu.HBM),
        out_shape=jax.ShapeDtypeStruct((tokens, PIECE), BF16),
        scratch_shapes=[
            pltpu.VMEM(ours.shape, BF16),
            pltpu.VMEM(ours.shape, BF16),
            pltpu.VMEM((tokens, PIECE), BF16),
            pltpu.SemaphoreType.DMA((2 * steps,)),
            pltpu.SemaphoreType.DMA((steps,)),
        ],
        compiler_params=PARAMS,
        name="finish",
    )(far(ours), far(other), num, line, keep, near(came))


def solution(mesh):
    spec = P(("seq", "head"), None)

    return jax.shard_map(on_device, mesh=mesh, in_specs=(spec,) * 5, out_specs=P("seq", "head"), check_vma=False)
```

```python
import jax
import jax.numpy as jnp
from jax import lax
from jax.experimental import pallas as pl
from jax.experimental.pallas import tpu as pltpu
from jax.sharding import PartitionSpec as P

VERY_NEGATIVE = -1e30
CHUNK = 256
PIECE = 256
HALF = PIECE // 2
KEYS = PIECE
GATES = 2 * PIECE
VMEM_LIMIT = 24 << 20
INSIDE_LIMIT = 56 << 20
FAR_LIMIT = 59 << 20
NEAR_CHIPS = 4
GATE_ROWS = 8
F32 = jnp.float32
BF16 = jnp.bfloat16


def dot(a, b, contract):
    return lax.dot_general(a, b, ((contract[:1], contract[1:]), ((), ())), preferred_element_type=F32)


def halves(x):
    top = x.astype(BF16)
    return top, (x - top.astype(F32)).astype(BF16)


def thirds(x, scale):
    first = x.astype(BF16).astype(F32)
    rest = (x - first) * scale
    second = rest.astype(BF16).astype(F32)
    third = ((rest - second) * scale).astype(BF16).astype(F32)
    return first, second, third


def iota(shape, dim):
    return lax.broadcasted_iota(jnp.int32, shape, dim)


def first_core():
    return lax.rem(lax.axis_index("seq"), 2) == 0


def pack_kernel(k_in, v_in, gate_in, forget_in, out_ref, k_ref, v_ref, gate_ref, forget_ref, sem):
    rows = k_ref.shape[0]
    pairs = (gate_in, gate_ref), (forget_in, forget_ref), (v_in, v_ref), (k_in, k_ref)
    copies = [pltpu.make_async_copy(a, b, sem.at[n]) for n, (a, b) in enumerate(pairs)]
    for copy in copies:
        copy.start()
    copies[0].wait()
    copies[1].wait()
    parts = []
    for x in (-jnp.log1p(jnp.exp(-forget_ref[...])), gate_ref[...]):
        parts += thirds(x, 1.0)
    for copy in copies[2:]:
        copy.wait()
    row = iota((GATE_ROWS, rows), 0)
    for h in range(k_ref.shape[1] // PIECE):
        area = jnp.zeros((GATE_ROWS, rows), F32)
        for p in range(6):
            area = jnp.where(row == p, parts[p][h : h + 1], area)
        area = area.astype(BF16)
        for u in range(2):
            n = 2 * h + u
            out_ref[n, 0:PIECE, :] = v_ref[:, n * PIECE : (n + 1) * PIECE].T
            for c in range(2):
                left = h * PIECE + c * HALF
                out_ref[n, KEYS + c * HALF : KEYS + (c + 1) * HALF, :] = k_ref[:, left : left + HALF]
            out_ref[n, GATES : GATES + GATE_ROWS, :] = area


def turn_kernel(q_ref, out_ref):
    for h in range(q_ref.shape[1] // PIECE):
        turned = q_ref[:, h * PIECE : (h + 1) * PIECE].T
        out_ref[2 * h] = turned
        out_ref[2 * h + 1] = turned


def beside(ref, blocks, low, high):
    return jnp.concatenate([ref[b, low:high, :] for b in blocks], axis=1)


def key_rows(ref, blocks):
    return jnp.concatenate(
        [
            jnp.concatenate([ref[b, KEYS + c * HALF : KEYS + (c + 1) * HALF, :] for c in range(2)], axis=1)
            for b in blocks
        ],
        axis=0,
    )


def chunk_blocks(ref, chunk):
    group = CHUNK // ref.shape[2]
    return range(chunk * group, (chunk + 1) * group)


def weighted_values(turned, weight):
    top, low = halves(turned.astype(F32) * weight)
    first, second, third = thirds(weight, 1.0)
    row = iota((8, weight.shape[1]), 0)
    left = jnp.where(row == 0, first, jnp.where(row == 1, third, 0.0)).astype(BF16)
    right = jnp.where(row == 0, second, 0.0).astype(BF16)
    return jnp.concatenate(
        [jnp.concatenate([top, left], axis=0), jnp.concatenate([low, right], axis=0)], axis=1
    )


def summary_kernel(r_ref, mine_ref, send_ref):
    sources, rows = r_ref.shape[0], r_ref.shape[2]
    decay = [r_ref[:, GATES + p, :] for p in range(3)]
    gate = [r_ref[:, GATES + 3 + p, :].astype(F32) for p in range(3)]
    gate = gate[0] + gate[1] + gate[2]
    after = (iota((rows, rows), 0) > iota((rows, rows), 1)).astype(BF16)
    later = (iota((sources, sources), 1) > iota((sources, sources), 0)).astype(BF16)
    suffix = sum(dot(d, after, (1, 0)) for d in decay)
    rest = sum(dot(later, d, (1, 0)) for d in decay)
    total = sum(jnp.sum(d.astype(F32), axis=0, keepdims=True) for d in decay)
    total = jnp.sum(total, axis=1, keepdims=True)
    tail = suffix + jnp.sum(rest, axis=1, keepdims=True) + gate
    new_m = jnp.max(jnp.max(tail, axis=1, keepdims=True), axis=0, keepdims=True)
    weight = jnp.exp(tail - new_m)
    state = jnp.zeros((PIECE + 8, PIECE), F32)
    for g in range(sources * rows // CHUNK):
        mine = chunk_blocks(r_ref, g)
        turned = beside(r_ref, mine, 0, PIECE)
        share = jnp.concatenate([weight[b : b + 1, :] for b in mine], axis=1)
        keys = key_rows(r_ref, mine)
        state = state + dot(
            weighted_values(turned, share), jnp.concatenate([keys, keys], axis=0), (1, 0)
        )
    c_new = state[0:PIECE]
    n_new = state[PIECE : PIECE + 1] + state[PIECE + 1 : PIECE + 2]

    place = iota((8, PIECE), 0)
    rest = jnp.where(place == 0, n_new, jnp.where(place == 1, new_m, total))
    first = first_core()
    low, high = c_new[0:HALF], c_new[HALF:PIECE]
    mine_ref[0:HALF, :] = jnp.where(first, low, high)
    send_ref[0:HALF, :] = jnp.where(first, high, low)
    mine_ref[HALF:, :] = rest
    send_ref[HALF:, :] = rest


def scalar(rows, n):
    return rows[n : n + 1, 0:1]


def pair_kernel(mine_ref, theirs_ref, z_ref, first_ref):
    first = first_core()
    mine, theirs = mine_ref[...], theirs_ref[...]
    early = jnp.where(first, mine, theirs)
    late = jnp.where(first, theirs, mine)
    first_ref[...] = early
    late_f = scalar(late, HALF + 2)
    moved = scalar(early, HALF + 1) + late_f
    late_m = scalar(late, HALF + 1)
    new_m = jnp.maximum(moved, late_m)
    joined = jnp.exp(moved - new_m) * early + jnp.exp(late_m - new_m) * late
    count, slab = z_ref.shape[0], z_ref.shape[1] - 8
    place = iota((8, PIECE), 0)
    rest = jnp.where(place == 1, new_m, scalar(early, HALF + 2) + late_f)
    rest = jnp.where(place == 0, joined[HALF : HALF + 1], rest)
    for i in range(count):
        z_ref[i, 0:slab, :] = joined[i * slab : (i + 1) * slab]
        z_ref[i, slab:, :] = rest


def entries_kernel(r_ref, top_ref, low_ref, aux_ref):
    upper = (iota((CHUNK, CHUNK), 0) <= iota((CHUNK, CHUNK), 1)).astype(BF16)
    row = iota((8, CHUNK), 0)
    state = jnp.zeros((PIECE, PIECE), F32)
    normal = jnp.zeros((1, PIECE), F32)
    old_m = jnp.full((1, 1), VERY_NEGATIVE, F32)
    start = jnp.zeros((1, 1), F32)
    steps = top_ref.shape[0]
    for step in range(steps):
        mine = chunk_blocks(r_ref, step)
        top_ref[step], low_ref[step] = halves(state)
        gates = beside(r_ref, mine, GATES, GATES + GATE_ROWS)
        cum = dot(gates, upper, (1, 0))
        cum = cum[0:1] + cum[1:2] + cum[2:3]
        gate = gates.astype(F32)
        gate = gate[3:4] + gate[4:5] + gate[5:6]
        total = cum[:, CHUNK - 1 : CHUNK]
        tail = total - cum + gate
        new_m = jnp.maximum(old_m + total, jnp.max(tail, axis=1, keepdims=True))
        keep = jnp.exp(old_m + total - new_m)
        aux = jnp.where(row == 0, normal, 0.0)
        for p, x in ((1, old_m), (2, start), (3, cum), (4, gate - cum)):
            aux = jnp.where(row == p, x, aux)
        aux_ref[step] = aux
        if step < steps - 1:
            keys = key_rows(r_ref, mine)
            fresh = dot(
                weighted_values(beside(r_ref, mine, 0, PIECE), jnp.exp(tail - new_m)),
                jnp.concatenate([keys, keys], axis=0),
                (1, 0),
            )
            state = keep * state + fresh[0:PIECE]
            normal = keep * normal + fresh[PIECE : PIECE + 1] + fresh[PIECE + 1 : PIECE + 2]
            old_m = new_m
            start = start + total


def near_kernel(z_ref, sum_ref, y_ref, meta_ref):
    count, slab = z_ref.shape[0], z_ref.shape[1] - 8
    state = jnp.zeros((slab, PIECE), F32)
    normal = jnp.zeros((1, PIECE), F32)
    old_m = jnp.full((1, 1), VERY_NEGATIVE, F32)
    total = jnp.zeros((1, 1), F32)
    for i in range(count):
        y_ref[i] = state
        for n, x in enumerate((old_m, total, normal)):
            meta_ref[n * count + i : n * count + i + 1, :] = jnp.broadcast_to(x, (1, PIECE))
        rest = z_ref[i, slab:, :]
        m, f = scalar(rest, 1), scalar(rest, 2)
        new_m = jnp.maximum(old_m + f, m)
        keep, take = jnp.exp(old_m + f - new_m), jnp.exp(m - new_m)
        state = keep * state + take * z_ref[i, 0:slab, :]
        normal = keep * normal + take * rest[0:1]
        old_m = new_m
        total = total + f
    place = iota((8, PIECE), 0)
    sum_ref[0:slab, :] = state
    sum_ref[slab:, :] = jnp.where(place == 0, normal, jnp.where(place == 1, old_m, total))


def far_kernel(*refs):
    y_ref, meta_ref, first_ref, *ahead, out_ref, nin_ref = refs
    count, slab = y_ref.shape[0], y_ref.shape[1]
    chip = lax.axis_index("seq") // 2
    near_at, group = lax.rem(chip, count), chip // count
    second = jnp.logical_not(first_core())
    state = jnp.zeros((slab, PIECE), F32)
    normal = jnp.zeros((1, PIECE), F32)
    old_m = jnp.full((1, 1), VERY_NEGATIVE, F32)
    for d in range(len(ahead), 0, -1):
        there = group >= d
        rest = ahead[d - 1][slab:, :]
        m = jnp.where(there, scalar(rest, 1), VERY_NEGATIVE)
        f = jnp.where(there, scalar(rest, 2), 0.0)
        new_m = jnp.maximum(old_m + f, m)
        keep, take = jnp.exp(old_m + f - new_m), jnp.exp(m - new_m)
        state = keep * state + take * ahead[d - 1][0:slab, :]
        normal = keep * normal + take * rest[0:1]
        old_m = new_m
    meta = meta_ref[...]
    own_m = jnp.full((1, 1), VERY_NEGATIVE, F32)
    own_n = jnp.zeros((1, PIECE), F32)
    for i in range(count):
        m, f = scalar(meta, i), scalar(meta, count + i)
        new_m = jnp.maximum(old_m + f, m)
        keep, take = jnp.exp(old_m + f - new_m), jnp.exp(m - new_m)
        out_ref[i] = keep * state + take * y_ref[i]
        n = keep * normal + take * meta[2 * count + i : 2 * count + i + 1]
        own_m = jnp.where(near_at == i, new_m, own_m)
        own_n = jnp.where(near_at == i, n, own_n)
    first_m = scalar(first_ref, HALF + 1)
    moved = own_m + scalar(first_ref, HALF + 2)
    next_m = jnp.maximum(moved, first_m)
    old_share, new_share = jnp.exp(moved - next_m), jnp.exp(first_m - next_m)
    next_n = old_share * own_n + new_share * first_ref[HALF : HALF + 1, :]
    place = iota((8, PIECE), 0)
    area = jnp.where(place == 0, old_share, new_share)
    area = jnp.where(place == 6, jnp.where(second, next_m, own_m), area)
    for p, part in enumerate(thirds(jnp.where(second, next_n, own_n), 1.0)):
        area = jnp.where(place == 3 + p, part, area)
    nin_ref[...] = area


def mix_kernel(p_ref, first_ref, nin_ref, keep_ref, send_ref):
    before = p_ref[...]
    after = before * nin_ref[0:1, 0:1] + first_ref[0:HALF, :] * nin_ref[1:2, 0:1]
    first = first_core()
    keep_ref[...] = jnp.where(first, before, after)
    send_ref[...] = jnp.where(first, after, before)


def inside_kernel(r_ref, asked_ref, top_ref, low_ref, aux_ref, nin_ref, num_ref, row_ref):
    factor = PIECE**-0.5
    before = nin_ref[...]
    before_m = before[6:7, 0:1]
    causal = iota((CHUNK, CHUNK), 0) <= iota((CHUNK, CHUNK), 1)
    row = iota((8, CHUNK), 0)
    for step in range(num_ref.shape[0]):
        mine = chunk_blocks(r_ref, step)
        asked = beside(asked_ref, mine, 0, PIECE)
        turned = beside(r_ref, mine, 0, PIECE)
        aux = aux_ref[step]
        cum = aux[3:4]
        carried = cum + aux[1:2]
        score = dot(key_rows(r_ref, mine), asked, (1, 0))
        gap = jnp.where(causal, aux.T[:, 4:5] + cum, VERY_NEGATIVE)
        top = jnp.maximum(carried, jnp.max(gap, axis=0, keepdims=True))
        weighted = jnp.exp(gap - top) * score
        outside = jnp.exp(carried - top)
        normal = jnp.where((row >= 3) & (row < 6), before, 0.0)
        for p, part in enumerate(thirds(aux[0:1], 1.0)):
            normal = jnp.where(row == p, part, normal)
        reached = dot(normal.astype(BF16), asked, (1, 0))
        den = jnp.sum(weighted, axis=0, keepdims=True)
        den = factor * (den + outside * (reached[0:1] + reached[1:2] + reached[2:3]))
        carried = cum + aux[2:3] + before_m
        new_m = jnp.maximum(top, carried)
        inside = jnp.exp(top - new_m)
        ahead = jnp.exp(carried - new_m) * factor
        den = den * inside + ahead * (reached[3:4] + reached[4:5] + reached[5:6])
        over = 1.0 / jnp.maximum(jnp.abs(den), 1.0)
        inside = inside * over * factor
        num = dot(
            jnp.concatenate([turned, turned], axis=1),
            jnp.concatenate(halves(weighted), axis=0),
            (1, 0),
        )
        read = dot(
            jnp.concatenate([top_ref[step], low_ref[step]], axis=1),
            jnp.concatenate([asked, asked], axis=0),
            (1, 0),
        )
        num_ref[step] = inside * num + (inside * outside) * read
        row_ref[step] = jnp.broadcast_to(ahead * over, (8, CHUNK))


def finish_kernel(
    asked_in, num_ref, row_ref, keep_ref, came_ref, out_ref, asked_ref, buffer_ref, in_sem, out_sem,
):
    steps = num_ref.shape[0]
    parts = in_sem.shape[0]
    share = asked_ref.shape[0] // parts
    arriving = []
    for p in range(parts):
        blocks = pl.ds(p * share, share)
        arriving.append(pltpu.make_async_copy(asked_in.at[blocks], asked_ref.at[blocks], in_sem.at[p]))
        arriving[-1].start()
    first = first_core()
    keep, came = keep_ref[...], came_ref[...]
    state = jnp.concatenate([jnp.where(first, keep, came), jnp.where(first, came, keep)], axis=0)
    both = jnp.concatenate(halves(state), axis=1)
    each = steps // out_sem.shape[0]
    leaving = []
    for step in range(steps):
        if step % (steps // parts) == 0:
            arriving[step // (steps // parts)].wait()
        asked = beside(asked_ref, chunk_blocks(asked_ref, step), 0, PIECE)
        read = dot(both, jnp.concatenate([asked, asked], axis=0), (1, 0))
        out = num_ref[step] + read * row_ref[step, 0:1, :]
        buffer_ref[pl.ds(step * CHUNK, CHUNK), :] = out.astype(BF16).T
        if step % each == each - 1:
            here = pl.ds((step - each + 1) * CHUNK, each * CHUNK)
            leaving.append(
                pltpu.make_async_copy(buffer_ref.at[here], out_ref.at[here], out_sem.at[step // each])
            )
            leaving[-1].start()
    for copy in leaving:
        copy.wait()


def far(x):
    return pltpu.with_memory_space_constraint(x, pltpu.HBM)


def near(x):
    return pltpu.with_memory_space_constraint(x, pltpu.VMEM)


NEAR = pl.BlockSpec(memory_space=pltpu.VMEM)
FAR = pl.BlockSpec()
PARAMS = pltpu.CompilerParams(vmem_limit_bytes=VMEM_LIMIT)


def on_device(queries, keys, values, input_pre, forget_pre):
    rows = queries.shape[0]
    pieces = lax.axis_size("head")
    shards = lax.axis_size("seq")
    tokens = pieces * rows
    steps = tokens // CHUNK
    tall = GATES + GATE_ROWS
    chips = shards // 2
    close = NEAR_CHIPS
    slab = HALF // close
    pairs = [(i, i ^ 1) for i in range(shards)]
    groups = [
        [2 * (g + z) + c for z in range(close)] for g in range(0, chips, close) for c in range(2)
    ]

    packed = pl.pallas_call(
        pack_kernel,
        in_specs=[pl.BlockSpec(memory_space=pltpu.HBM)] * 4,
        out_specs=NEAR,
        out_shape=pltpu.VMEM((pieces, tall, rows), BF16),
        scratch_shapes=[
            pltpu.VMEM(keys.shape, BF16),
            pltpu.VMEM(values.shape, BF16),
            pltpu.VMEM((input_pre.shape[1], rows), F32),
            pltpu.VMEM((input_pre.shape[1], rows), F32),
            pltpu.SemaphoreType.DMA((4,)),
        ],
        compiler_params=PARAMS,
        name="pack",
    )(*(far(x) for x in (keys, values, input_pre.T, forget_pre.T)))

    received = lax.all_to_all(packed, "head", split_axis=0, concat_axis=0, tiled=True)

    half = pltpu.VMEM((HALF + 8, PIECE), F32)
    mine, send = pl.pallas_call(
        summary_kernel,
        in_specs=[NEAR],
        out_specs=[NEAR] * 2,
        out_shape=[half] * 2,
        compiler_params=PARAMS,
        name="summary",
    )(near(received))

    theirs = lax.ppermute(send, "seq", pairs)

    summary, first = pl.pallas_call(
        pair_kernel,
        in_specs=[NEAR, NEAR],
        out_specs=[NEAR, FAR],
        out_shape=[
            pltpu.VMEM((close, slab + 8, PIECE), F32),
            jax.ShapeDtypeStruct((HALF + 8, PIECE), F32),
        ],
        compiler_params=PARAMS,
        name="pair",
    )(mine, near(theirs))

    spread = lax.all_to_all(
        summary, "seq", split_axis=0, concat_axis=0, tiled=True, axis_index_groups=groups
    )

    turned = pl.pallas_call(
        turn_kernel,
        in_specs=[FAR],
        out_specs=FAR,
        out_shape=jax.ShapeDtypeStruct((pieces, PIECE, rows), BF16),
        name="turn",
    )(far(queries))
    asked = lax.all_to_all(turned, "head", split_axis=0, concat_axis=0, tiled=True)

    entry_top, entry_low, aux = pl.pallas_call(
        entries_kernel,
        in_specs=[FAR],
        out_specs=[FAR] * 3,
        out_shape=[
            jax.ShapeDtypeStruct((steps, PIECE, PIECE), BF16),
            jax.ShapeDtypeStruct((steps, PIECE, PIECE), BF16),
            jax.ShapeDtypeStruct((steps, 8, CHUNK), F32),
        ],
        name="entries",
    )(far(received))

    group_sum, local, meta = pl.pallas_call(
        near_kernel,
        in_specs=[NEAR],
        out_specs=[NEAR, FAR, FAR],
        out_shape=[
            pltpu.VMEM((slab + 8, PIECE), F32),
            jax.ShapeDtypeStruct((close, slab, PIECE), F32),
            jax.ShapeDtypeStruct((16, PIECE), F32),
        ],
        compiler_params=pltpu.CompilerParams(vmem_limit_bytes=FAR_LIMIT),
        name="near",
    )(near(spread))

    ahead = []
    for d in range(1, chips // close):
        step = 2 * close * d
        ahead.append(lax.ppermute(group_sum, "seq", [(i, i + step) for i in range(shards - step)]))

    before, normal = pl.pallas_call(
        far_kernel,
        in_specs=[FAR, FAR] + [NEAR] * (1 + len(ahead)),
        out_specs=[FAR] * 2,
        out_shape=[
            jax.ShapeDtypeStruct((close, slab, PIECE), F32),
            jax.ShapeDtypeStruct((8, PIECE), F32),
        ],
        compiler_params=pltpu.CompilerParams(vmem_limit_bytes=FAR_LIMIT),
        name="far",
    )(local, meta, near(first), *(near(a) for a in ahead))

    back = lax.all_to_all(
        before, "seq", split_axis=0, concat_axis=0, tiled=True, axis_index_groups=groups
    )

    keep, lend = pl.pallas_call(
        mix_kernel,
        in_specs=[NEAR] * 3,
        out_specs=[NEAR] * 2,
        out_shape=[pltpu.VMEM((HALF, PIECE), F32)] * 2,
        compiler_params=PARAMS,
        name="mix",
    )(near(back.reshape(HALF, PIECE)), near(first), near(normal))
    came = lax.ppermute(lend, "seq", pairs)

    num, line = pl.pallas_call(
        inside_kernel,
        in_specs=[FAR] * 6,
        out_specs=[NEAR] * 2,
        out_shape=[
            pltpu.VMEM((steps, PIECE, CHUNK), F32),
            pltpu.VMEM((steps, 8, CHUNK), F32),
        ],
        compiler_params=pltpu.CompilerParams(vmem_limit_bytes=INSIDE_LIMIT),
        name="inside",
    )(far(received), far(asked), entry_top, entry_low, aux, normal)

    return pl.pallas_call(
        finish_kernel,
        in_specs=[pl.BlockSpec(memory_space=pltpu.HBM)] + [NEAR] * 4,
        out_specs=pl.BlockSpec(memory_space=pltpu.HBM),
        out_shape=jax.ShapeDtypeStruct((tokens, PIECE), BF16),
        scratch_shapes=[
            pltpu.VMEM(asked.shape, BF16),
            pltpu.VMEM((tokens, PIECE), BF16),
            pltpu.SemaphoreType.DMA((2,)),
            pltpu.SemaphoreType.DMA((steps // 2,)),
        ],
        compiler_params=PARAMS,
        name="finish",
    )(far(asked), num, line, keep, near(came))


def solution(mesh):
    spec = P(("seq", "head"), None)

    return jax.shard_map(on_device, mesh=mesh, in_specs=(spec,) * 5, out_specs=P("seq", "head"), check_vma=False)
```

```python
import jax
import jax.numpy as jnp
from jax import lax
from jax.experimental import pallas as pl
from jax.experimental.pallas import tpu as pltpu
from jax.sharding import PartitionSpec as P

VERY_NEGATIVE = -1e30
CHUNK = 256
PIECE = 256
HALF = PIECE // 2
KEYS = PIECE
GATES = 2 * PIECE
VMEM_LIMIT = 24 << 20
INSIDE_LIMIT = 56 << 20
FAR_LIMIT = 59 << 20
NEAR_CHIPS = 4
PARTS = 2
GATE_ROWS = 8
F32 = jnp.float32
BF16 = jnp.bfloat16


def dot(a, b, contract):
    return lax.dot_general(a, b, ((contract[:1], contract[1:]), ((), ())), preferred_element_type=F32)


def halves(x):
    top = x.astype(BF16)
    return top, (x - top.astype(F32)).astype(BF16)


def thirds(x, scale):
    first = x.astype(BF16).astype(F32)
    rest = (x - first) * scale
    second = rest.astype(BF16).astype(F32)
    third = ((rest - second) * scale).astype(BF16).astype(F32)
    return first, second, third


def iota(shape, dim):
    return lax.broadcasted_iota(jnp.int32, shape, dim)


def first_core():
    return lax.rem(lax.axis_index("seq"), 2) == 0


def pack_kernel(k_in, v_in, gate_in, forget_in, out_ref, k_ref, v_ref, gate_ref, forget_ref, sem):
    rows = k_ref.shape[0]
    pairs = (gate_in, gate_ref), (forget_in, forget_ref), (v_in, v_ref), (k_in, k_ref)
    copies = [pltpu.make_async_copy(a, b, sem.at[n]) for n, (a, b) in enumerate(pairs)]
    for copy in copies:
        copy.start()
    copies[0].wait()
    copies[1].wait()
    parts = []
    for x in (-jnp.log1p(jnp.exp(-forget_ref[...])), gate_ref[...]):
        parts += thirds(x, 1.0)
    for copy in copies[2:]:
        copy.wait()
    row = iota((GATE_ROWS, rows), 0)
    for h in range(k_ref.shape[1] // PIECE):
        area = jnp.zeros((GATE_ROWS, rows), F32)
        for p in range(6):
            area = jnp.where(row == p, parts[p][h : h + 1], area)
        area = area.astype(BF16)
        for u in range(2):
            n = 2 * h + u
            out_ref[n, 0:PIECE, :] = v_ref[:, n * PIECE : (n + 1) * PIECE].T
            for c in range(2):
                left = h * PIECE + c * HALF
                out_ref[n, KEYS + c * HALF : KEYS + (c + 1) * HALF, :] = k_ref[:, left : left + HALF]
            out_ref[n, GATES : GATES + GATE_ROWS, :] = area


def turn_kernel(q_ref, out_ref):
    for h in range(q_ref.shape[1] // PIECE):
        turned = q_ref[:, h * PIECE : (h + 1) * PIECE].T
        out_ref[2 * h] = turned
        out_ref[2 * h + 1] = turned


def beside(ref, blocks, low, high):
    return jnp.concatenate([ref[b, low:high, :] for b in blocks], axis=1)


def key_rows(ref, blocks):
    return jnp.concatenate(
        [
            jnp.concatenate([ref[b, KEYS + c * HALF : KEYS + (c + 1) * HALF, :] for c in range(2)], axis=1)
            for b in blocks
        ],
        axis=0,
    )


def chunk_blocks(ref, chunk):
    group = CHUNK // ref.shape[2]
    return range(chunk * group, (chunk + 1) * group)


def weighted_values(turned, weight):
    top, low = halves(turned.astype(F32) * weight)
    first, second, third = thirds(weight, 1.0)
    row = iota((8, weight.shape[1]), 0)
    left = jnp.where(row == 0, first, jnp.where(row == 1, third, 0.0)).astype(BF16)
    right = jnp.where(row == 0, second, 0.0).astype(BF16)
    return jnp.concatenate(
        [jnp.concatenate([top, left], axis=0), jnp.concatenate([low, right], axis=0)], axis=1
    )


def summary_kernel(r_ref, mine_ref, send_ref):
    sources, rows = r_ref.shape[0], r_ref.shape[2]
    decay = [r_ref[:, GATES + p, :] for p in range(3)]
    gate = [r_ref[:, GATES + 3 + p, :].astype(F32) for p in range(3)]
    gate = gate[0] + gate[1] + gate[2]
    after = (iota((rows, rows), 0) > iota((rows, rows), 1)).astype(BF16)
    later = (iota((sources, sources), 1) > iota((sources, sources), 0)).astype(BF16)
    suffix = sum(dot(d, after, (1, 0)) for d in decay)
    rest = sum(dot(later, d, (1, 0)) for d in decay)
    total = sum(jnp.sum(d.astype(F32), axis=0, keepdims=True) for d in decay)
    total = jnp.sum(total, axis=1, keepdims=True)
    tail = suffix + jnp.sum(rest, axis=1, keepdims=True) + gate
    new_m = jnp.max(jnp.max(tail, axis=1, keepdims=True), axis=0, keepdims=True)
    weight = jnp.exp(tail - new_m)
    state = jnp.zeros((PIECE + 8, PIECE), F32)
    for g in range(sources * rows // CHUNK):
        mine = chunk_blocks(r_ref, g)
        turned = beside(r_ref, mine, 0, PIECE)
        share = jnp.concatenate([weight[b : b + 1, :] for b in mine], axis=1)
        keys = key_rows(r_ref, mine)
        state = state + dot(
            weighted_values(turned, share), jnp.concatenate([keys, keys], axis=0), (1, 0)
        )
    c_new = state[0:PIECE]
    n_new = state[PIECE : PIECE + 1] + state[PIECE + 1 : PIECE + 2]

    place = iota((8, PIECE), 0)
    rest = jnp.where(place == 0, n_new, jnp.where(place == 1, new_m, total))
    first = first_core()
    low, high = c_new[0:HALF], c_new[HALF:PIECE]
    mine_ref[0:HALF, :] = jnp.where(first, low, high)
    send_ref[0:HALF, :] = jnp.where(first, high, low)
    mine_ref[HALF:, :] = rest
    send_ref[HALF:, :] = rest


def scalar(rows, n):
    return rows[n : n + 1, 0:1]


def pair_kernel(mine_ref, theirs_ref, z_ref, first_ref):
    first = first_core()
    mine, theirs = mine_ref[...], theirs_ref[...]
    early = jnp.where(first, mine, theirs)
    late = jnp.where(first, theirs, mine)
    first_ref[...] = early
    late_f = scalar(late, HALF + 2)
    moved = scalar(early, HALF + 1) + late_f
    late_m = scalar(late, HALF + 1)
    new_m = jnp.maximum(moved, late_m)
    joined = jnp.exp(moved - new_m) * early + jnp.exp(late_m - new_m) * late
    count, slab = z_ref.shape[0], z_ref.shape[1] - 8
    place = iota((8, PIECE), 0)
    rest = jnp.where(place == 1, new_m, scalar(early, HALF + 2) + late_f)
    rest = jnp.where(place == 0, joined[HALF : HALF + 1], rest)
    for i in range(count):
        z_ref[i, 0:slab, :] = joined[i * slab : (i + 1) * slab]
        z_ref[i, slab:, :] = rest


def in_parts(pairs, sem, parts):
    started = []
    for p in range(parts):
        copies = []
        for n, (a, b) in enumerate(pairs):
            share = a.shape[0] // parts
            here = pl.ds(p * share, share)
            copies.append(pltpu.make_async_copy(a.at[here], b.at[here], sem.at[len(pairs) * p + n]))
            copies[-1].start()
        started.append(copies)
    return started


def entries_kernel(r_in, entry_out, aux_ref, r_ref, entry_ref, in_sem, out_sem):
    upper = (iota((CHUNK, CHUNK), 0) <= iota((CHUNK, CHUNK), 1)).astype(BF16)
    row = iota((8, CHUNK), 0)
    state = jnp.zeros((PIECE, PIECE), F32)
    normal = jnp.zeros((1, PIECE), F32)
    old_m = jnp.full((1, 1), VERY_NEGATIVE, F32)
    start = jnp.zeros((1, 1), F32)
    steps = entry_ref.shape[0]
    arriving = in_parts([(r_in, r_ref)], in_sem, PARTS)
    leaving = []
    for step in range(steps):
        if step % (steps // PARTS) == 0:
            arriving[step // (steps // PARTS)][0].wait()
        mine = chunk_blocks(r_ref, step)
        entry_ref[step] = jnp.concatenate(halves(state), axis=1)
        if (step + 1) % (steps // PARTS) == 0:
            part = step // (steps // PARTS)
            here = pl.ds(part * (steps // PARTS), steps // PARTS)
            leaving.append(
                pltpu.make_async_copy(entry_ref.at[here], entry_out.at[here], out_sem.at[part])
            )
            leaving[-1].start()
        gates = beside(r_ref, mine, GATES, GATES + GATE_ROWS)
        cum = dot(gates, upper, (1, 0))
        cum = cum[0:1] + cum[1:2] + cum[2:3]
        gate = gates.astype(F32)
        gate = gate[3:4] + gate[4:5] + gate[5:6]
        total = cum[:, CHUNK - 1 : CHUNK]
        tail = total - cum + gate
        new_m = jnp.maximum(old_m + total, jnp.max(tail, axis=1, keepdims=True))
        keep = jnp.exp(old_m + total - new_m)
        aux = jnp.where(row == 0, normal, 0.0)
        for p, x in ((1, old_m), (2, start), (3, cum), (4, gate - cum)):
            aux = jnp.where(row == p, x, aux)
        aux_ref[step] = aux
        if step < steps - 1:
            keys = key_rows(r_ref, mine)
            fresh = dot(
                weighted_values(beside(r_ref, mine, 0, PIECE), jnp.exp(tail - new_m)),
                jnp.concatenate([keys, keys], axis=0),
                (1, 0),
            )
            state = keep * state + fresh[0:PIECE]
            normal = keep * normal + fresh[PIECE : PIECE + 1] + fresh[PIECE + 1 : PIECE + 2]
            old_m = new_m
            start = start + total
    for copy in leaving:
        copy.wait()


def near_kernel(z_ref, sum_ref, y_ref, meta_ref):
    count, slab = z_ref.shape[0], z_ref.shape[1] - 8
    state = jnp.zeros((slab, PIECE), F32)
    normal = jnp.zeros((1, PIECE), F32)
    old_m = jnp.full((1, 1), VERY_NEGATIVE, F32)
    total = jnp.zeros((1, 1), F32)
    for i in range(count):
        y_ref[i] = state
        for n, x in enumerate((old_m, total, normal)):
            meta_ref[n * count + i : n * count + i + 1, :] = jnp.broadcast_to(x, (1, PIECE))
        rest = z_ref[i, slab:, :]
        m, f = scalar(rest, 1), scalar(rest, 2)
        new_m = jnp.maximum(old_m + f, m)
        keep, take = jnp.exp(old_m + f - new_m), jnp.exp(m - new_m)
        state = keep * state + take * z_ref[i, 0:slab, :]
        normal = keep * normal + take * rest[0:1]
        old_m = new_m
        total = total + f
    place = iota((8, PIECE), 0)
    sum_ref[0:slab, :] = state
    sum_ref[slab:, :] = jnp.where(place == 0, normal, jnp.where(place == 1, old_m, total))


def far_kernel(*refs):
    y_ref, meta_ref, first_ref, *ahead, out_ref, nin_ref = refs
    count, slab = y_ref.shape[0], y_ref.shape[1]
    chip = lax.axis_index("seq") // 2
    near_at, group = lax.rem(chip, count), chip // count
    second = jnp.logical_not(first_core())
    state = jnp.zeros((slab, PIECE), F32)
    normal = jnp.zeros((1, PIECE), F32)
    old_m = jnp.full((1, 1), VERY_NEGATIVE, F32)
    for d in range(len(ahead), 0, -1):
        there = group >= d
        rest = ahead[d - 1][slab:, :]
        m = jnp.where(there, scalar(rest, 1), VERY_NEGATIVE)
        f = jnp.where(there, scalar(rest, 2), 0.0)
        new_m = jnp.maximum(old_m + f, m)
        keep, take = jnp.exp(old_m + f - new_m), jnp.exp(m - new_m)
        state = keep * state + take * ahead[d - 1][0:slab, :]
        normal = keep * normal + take * rest[0:1]
        old_m = new_m
    meta = meta_ref[...]
    own_m = jnp.full((1, 1), VERY_NEGATIVE, F32)
    own_n = jnp.zeros((1, PIECE), F32)
    for i in range(count):
        m, f = scalar(meta, i), scalar(meta, count + i)
        new_m = jnp.maximum(old_m + f, m)
        keep, take = jnp.exp(old_m + f - new_m), jnp.exp(m - new_m)
        out_ref[i] = keep * state + take * y_ref[i]
        n = keep * normal + take * meta[2 * count + i : 2 * count + i + 1]
        own_m = jnp.where(near_at == i, new_m, own_m)
        own_n = jnp.where(near_at == i, n, own_n)
    first_m = scalar(first_ref, HALF + 1)
    moved = own_m + scalar(first_ref, HALF + 2)
    next_m = jnp.maximum(moved, first_m)
    old_share, new_share = jnp.exp(moved - next_m), jnp.exp(first_m - next_m)
    next_n = old_share * own_n + new_share * first_ref[HALF : HALF + 1, :]
    place = iota((8, PIECE), 0)
    area = jnp.where(place == 0, old_share, new_share)
    area = jnp.where(place == 6, jnp.where(second, next_m, own_m), area)
    for p, part in enumerate(thirds(jnp.where(second, next_n, own_n), 1.0)):
        area = jnp.where(place == 3 + p, part, area)
    nin_ref[...] = area


def mix_kernel(p_ref, first_ref, nin_ref, keep_ref, send_ref):
    before = p_ref[...]
    after = before * nin_ref[0:1, 0:1] + first_ref[0:HALF, :] * nin_ref[1:2, 0:1]
    first = first_core()
    keep_ref[...] = jnp.where(first, before, after)
    send_ref[...] = jnp.where(first, after, before)


def inside_kernel(
    r_in, asked_in, entry_in, aux_ref, nin_ref, num_ref, row_ref, r_ref, asked_ref, entry_ref, in_sem
):
    factor = PIECE**-0.5
    before = nin_ref[...]
    before_m = before[6:7, 0:1]
    causal = iota((CHUNK, CHUNK), 0) <= iota((CHUNK, CHUNK), 1)
    row = iota((8, CHUNK), 0)
    steps = num_ref.shape[0]
    pairs = [(r_in, r_ref), (asked_in, asked_ref), (entry_in, entry_ref)]
    arriving = in_parts(pairs, in_sem, PARTS)
    for step in range(steps):
        if step % (steps // PARTS) == 0:
            for copy in arriving[step // (steps // PARTS)]:
                copy.wait()
        mine = chunk_blocks(r_ref, step)
        asked = beside(asked_ref, mine, 0, PIECE)
        turned = beside(r_ref, mine, 0, PIECE)
        aux = aux_ref[step]
        cum = aux[3:4]
        carried = cum + aux[1:2]
        score = dot(key_rows(r_ref, mine), asked, (1, 0))
        gap = jnp.where(causal, aux.T[:, 4:5] + cum, VERY_NEGATIVE)
        top = jnp.maximum(carried, jnp.max(gap, axis=0, keepdims=True))
        weighted = jnp.exp(gap - top) * score
        outside = jnp.exp(carried - top)
        normal = jnp.where((row >= 3) & (row < 6), before, 0.0)
        for p, part in enumerate(thirds(aux[0:1], 1.0)):
            normal = jnp.where(row == p, part, normal)
        reached = dot(normal.astype(BF16), asked, (1, 0))
        den = jnp.sum(weighted, axis=0, keepdims=True)
        den = factor * (den + outside * (reached[0:1] + reached[1:2] + reached[2:3]))
        carried = cum + aux[2:3] + before_m
        new_m = jnp.maximum(top, carried)
        inside = jnp.exp(top - new_m)
        ahead = jnp.exp(carried - new_m) * factor
        den = den * inside + ahead * (reached[3:4] + reached[4:5] + reached[5:6])
        over = 1.0 / jnp.maximum(jnp.abs(den), 1.0)
        inside = inside * over * factor
        num = dot(
            jnp.concatenate([turned, turned], axis=1),
            jnp.concatenate(halves(weighted), axis=0),
            (1, 0),
        )
        read = dot(
            entry_ref[step],
            jnp.concatenate([asked, asked], axis=0),
            (1, 0),
        )
        num_ref[step] = inside * num + (inside * outside) * read
        row_ref[step] = jnp.broadcast_to(ahead * over, (8, CHUNK))


def finish_kernel(
    asked_in, num_ref, row_ref, keep_ref, came_ref, out_ref, asked_ref, buffer_ref, in_sem, out_sem,
):
    steps = num_ref.shape[0]
    parts = in_sem.shape[0]
    share = asked_ref.shape[0] // parts
    arriving = []
    for p in range(parts):
        blocks = pl.ds(p * share, share)
        arriving.append(pltpu.make_async_copy(asked_in.at[blocks], asked_ref.at[blocks], in_sem.at[p]))
        arriving[-1].start()
    first = first_core()
    keep, came = keep_ref[...], came_ref[...]
    state = jnp.concatenate([jnp.where(first, keep, came), jnp.where(first, came, keep)], axis=0)
    both = jnp.concatenate(halves(state), axis=1)
    each = steps // out_sem.shape[0]
    leaving = []
    for step in range(steps):
        if step % (steps // parts) == 0:
            arriving[step // (steps // parts)].wait()
        asked = beside(asked_ref, chunk_blocks(asked_ref, step), 0, PIECE)
        read = dot(both, jnp.concatenate([asked, asked], axis=0), (1, 0))
        out = num_ref[step] + read * row_ref[step, 0:1, :]
        buffer_ref[pl.ds(step * CHUNK, CHUNK), :] = out.astype(BF16).T
        if step % each == each - 1:
            here = pl.ds((step - each + 1) * CHUNK, each * CHUNK)
            leaving.append(
                pltpu.make_async_copy(buffer_ref.at[here], out_ref.at[here], out_sem.at[step // each])
            )
            leaving[-1].start()
    for copy in leaving:
        copy.wait()


def far(x):
    return pltpu.with_memory_space_constraint(x, pltpu.HBM)


def near(x):
    return pltpu.with_memory_space_constraint(x, pltpu.VMEM)


NEAR = pl.BlockSpec(memory_space=pltpu.VMEM)
FAR = pl.BlockSpec()
PARAMS = pltpu.CompilerParams(vmem_limit_bytes=VMEM_LIMIT)


def on_device(queries, keys, values, input_pre, forget_pre):
    rows = queries.shape[0]
    pieces = lax.axis_size("head")
    shards = lax.axis_size("seq")
    tokens = pieces * rows
    steps = tokens // CHUNK
    tall = GATES + GATE_ROWS
    chips = shards // 2
    close = NEAR_CHIPS
    slab = HALF // close
    pairs = [(i, i ^ 1) for i in range(shards)]
    groups = [
        [2 * (g + z) + c for z in range(close)] for g in range(0, chips, close) for c in range(2)
    ]

    packed = pl.pallas_call(
        pack_kernel,
        in_specs=[pl.BlockSpec(memory_space=pltpu.HBM)] * 4,
        out_specs=NEAR,
        out_shape=pltpu.VMEM((pieces, tall, rows), BF16),
        scratch_shapes=[
            pltpu.VMEM(keys.shape, BF16),
            pltpu.VMEM(values.shape, BF16),
            pltpu.VMEM((input_pre.shape[1], rows), F32),
            pltpu.VMEM((input_pre.shape[1], rows), F32),
            pltpu.SemaphoreType.DMA((4,)),
        ],
        compiler_params=PARAMS,
        name="pack",
    )(*(far(x) for x in (keys, values, input_pre.T, forget_pre.T)))

    received = lax.all_to_all(packed, "head", split_axis=0, concat_axis=0, tiled=True)

    half = pltpu.VMEM((HALF + 8, PIECE), F32)
    mine, send = pl.pallas_call(
        summary_kernel,
        in_specs=[NEAR],
        out_specs=[NEAR] * 2,
        out_shape=[half] * 2,
        compiler_params=PARAMS,
        name="summary",
    )(near(received))

    theirs = lax.ppermute(send, "seq", pairs)

    summary, first = pl.pallas_call(
        pair_kernel,
        in_specs=[NEAR, NEAR],
        out_specs=[NEAR, FAR],
        out_shape=[
            pltpu.VMEM((close, slab + 8, PIECE), F32),
            jax.ShapeDtypeStruct((HALF + 8, PIECE), F32),
        ],
        compiler_params=PARAMS,
        name="pair",
    )(mine, near(theirs))

    spread = lax.all_to_all(
        summary, "seq", split_axis=0, concat_axis=0, tiled=True, axis_index_groups=groups
    )

    turned = pl.pallas_call(
        turn_kernel,
        in_specs=[FAR],
        out_specs=FAR,
        out_shape=jax.ShapeDtypeStruct((pieces, PIECE, rows), BF16),
        name="turn",
    )(far(queries))
    asked = lax.all_to_all(turned, "head", split_axis=0, concat_axis=0, tiled=True)

    far_spec = pl.BlockSpec(memory_space=pltpu.HBM)
    entries = (steps, PIECE, 2 * PIECE)
    entry, aux = pl.pallas_call(
        entries_kernel,
        in_specs=[far_spec],
        out_specs=[far_spec, FAR],
        out_shape=[
            jax.ShapeDtypeStruct(entries, BF16),
            jax.ShapeDtypeStruct((steps, 8, CHUNK), F32),
        ],
        scratch_shapes=[
            pltpu.VMEM(received.shape, BF16),
            pltpu.VMEM(entries, BF16),
            pltpu.SemaphoreType.DMA((PARTS,)),
            pltpu.SemaphoreType.DMA((PARTS,)),
        ],
        name="entries",
    )(far(received))

    group_sum, local, meta = pl.pallas_call(
        near_kernel,
        in_specs=[NEAR],
        out_specs=[NEAR, FAR, FAR],
        out_shape=[
            pltpu.VMEM((slab + 8, PIECE), F32),
            jax.ShapeDtypeStruct((close, slab, PIECE), F32),
            jax.ShapeDtypeStruct((16, PIECE), F32),
        ],
        compiler_params=pltpu.CompilerParams(vmem_limit_bytes=FAR_LIMIT),
        name="near",
    )(near(spread))

    ahead = []
    for d in range(1, chips // close):
        step = 2 * close * d
        ahead.append(lax.ppermute(group_sum, "seq", [(i, i + step) for i in range(shards - step)]))

    before, normal = pl.pallas_call(
        far_kernel,
        in_specs=[FAR, FAR] + [NEAR] * (1 + len(ahead)),
        out_specs=[FAR] * 2,
        out_shape=[
            jax.ShapeDtypeStruct((close, slab, PIECE), F32),
            jax.ShapeDtypeStruct((8, PIECE), F32),
        ],
        compiler_params=pltpu.CompilerParams(vmem_limit_bytes=FAR_LIMIT),
        name="far",
    )(local, meta, near(first), *(near(a) for a in ahead))

    back = lax.all_to_all(
        before, "seq", split_axis=0, concat_axis=0, tiled=True, axis_index_groups=groups
    )

    keep, lend = pl.pallas_call(
        mix_kernel,
        in_specs=[NEAR] * 3,
        out_specs=[NEAR] * 2,
        out_shape=[pltpu.VMEM((HALF, PIECE), F32)] * 2,
        compiler_params=PARAMS,
        name="mix",
    )(near(back.reshape(HALF, PIECE)), near(first), near(normal))
    came = lax.ppermute(lend, "seq", pairs)

    num, line = pl.pallas_call(
        inside_kernel,
        in_specs=[far_spec] * 3 + [FAR] * 2,
        out_specs=[NEAR] * 2,
        out_shape=[
            pltpu.VMEM((steps, PIECE, CHUNK), F32),
            pltpu.VMEM((steps, 8, CHUNK), F32),
        ],
        scratch_shapes=[
            pltpu.VMEM(received.shape, BF16),
            pltpu.VMEM(asked.shape, BF16),
            pltpu.VMEM(entries, BF16),
            pltpu.SemaphoreType.DMA((3 * PARTS,)),
        ],
        compiler_params=pltpu.CompilerParams(vmem_limit_bytes=INSIDE_LIMIT),
        name="inside",
    )(far(received), far(asked), far(entry), aux, normal)

    return pl.pallas_call(
        finish_kernel,
        in_specs=[pl.BlockSpec(memory_space=pltpu.HBM)] + [NEAR] * 4,
        out_specs=pl.BlockSpec(memory_space=pltpu.HBM),
        out_shape=jax.ShapeDtypeStruct((tokens, PIECE), BF16),
        scratch_shapes=[
            pltpu.VMEM(asked.shape, BF16),
            pltpu.VMEM((tokens, PIECE), BF16),
            pltpu.SemaphoreType.DMA((2,)),
            pltpu.SemaphoreType.DMA((steps // 2,)),
        ],
        compiler_params=PARAMS,
        name="finish",
    )(far(asked), num, line, keep, near(came))


def solution(mesh):
    spec = P(("seq", "head"), None)

    return jax.shard_map(on_device, mesh=mesh, in_specs=(spec,) * 5, out_specs=P("seq", "head"), check_vma=False)
```

```python
import jax
import jax.numpy as jnp
from jax import lax
from jax.experimental import pallas as pl
from jax.experimental.pallas import tpu as pltpu
from jax.sharding import PartitionSpec as P

VERY_NEGATIVE = -1e30
CHUNK = 256
PIECE = 256
HALF = PIECE // 2
KEYS = PIECE
GATES = 2 * PIECE
VMEM_LIMIT = 24 << 20
INSIDE_LIMIT = 56 << 20
FAR_LIMIT = 59 << 20
NEAR_CHIPS = 4
PARTS = 2
GATE_ROWS = 8
F32 = jnp.float32
BF16 = jnp.bfloat16


def dot(a, b, contract):
    return lax.dot_general(a, b, ((contract[:1], contract[1:]), ((), ())), preferred_element_type=F32)


def halves(x):
    top = x.astype(BF16)
    return top, (x - top.astype(F32)).astype(BF16)


def thirds(x, scale):
    first = x.astype(BF16).astype(F32)
    rest = (x - first) * scale
    second = rest.astype(BF16).astype(F32)
    third = ((rest - second) * scale).astype(BF16).astype(F32)
    return first, second, third


def iota(shape, dim):
    return lax.broadcasted_iota(jnp.int32, shape, dim)


def first_core():
    return lax.rem(lax.axis_index("seq"), 2) == 0


def pack_kernel(k_in, v_in, gate_in, forget_in, out_ref, k_ref, v_ref, gate_ref, forget_ref, sem):
    rows = k_ref.shape[0]
    pairs = (gate_in, gate_ref), (forget_in, forget_ref), (v_in, v_ref), (k_in, k_ref)
    copies = [pltpu.make_async_copy(a, b, sem.at[n]) for n, (a, b) in enumerate(pairs)]
    for copy in copies:
        copy.start()
    copies[0].wait()
    copies[1].wait()
    parts = []
    for x in (-jnp.log1p(jnp.exp(-forget_ref[...])), gate_ref[...]):
        parts += thirds(x, 1.0)
    for copy in copies[2:]:
        copy.wait()
    row = iota((GATE_ROWS, rows), 0)
    for h in range(k_ref.shape[1] // PIECE):
        area = jnp.zeros((GATE_ROWS, rows), F32)
        for p in range(6):
            area = jnp.where(row == p, parts[p][h : h + 1], area)
        area = area.astype(BF16)
        for u in range(2):
            n = 2 * h + u
            out_ref[n, 0:PIECE, :] = v_ref[:, n * PIECE : (n + 1) * PIECE].T
            for c in range(2):
                left = h * PIECE + c * HALF
                out_ref[n, KEYS + c * HALF : KEYS + (c + 1) * HALF, :] = k_ref[:, left : left + HALF]
            out_ref[n, GATES : GATES + GATE_ROWS, :] = area


def turn_kernel(q_ref, out_ref):
    for h in range(q_ref.shape[1] // PIECE):
        turned = q_ref[:, h * PIECE : (h + 1) * PIECE].T
        out_ref[2 * h] = turned
        out_ref[2 * h + 1] = turned


def beside(ref, blocks, low, high):
    return jnp.concatenate([ref[b, low:high, :] for b in blocks], axis=1)


def key_rows(ref, blocks):
    return jnp.concatenate(
        [
            jnp.concatenate([ref[b, KEYS + c * HALF : KEYS + (c + 1) * HALF, :] for c in range(2)], axis=1)
            for b in blocks
        ],
        axis=0,
    )


def chunk_blocks(ref, chunk):
    group = CHUNK // ref.shape[2]
    return range(chunk * group, (chunk + 1) * group)


def weighted_values(turned, weight):
    top, low = halves(turned.astype(F32) * weight)
    first, second, third = thirds(weight, 1.0)
    row = iota((8, weight.shape[1]), 0)
    left = jnp.where(row == 0, first, jnp.where(row == 1, third, 0.0)).astype(BF16)
    right = jnp.where(row == 0, second, 0.0).astype(BF16)
    return jnp.concatenate(
        [jnp.concatenate([top, left], axis=0), jnp.concatenate([low, right], axis=0)], axis=1
    )


def summary_kernel(r_ref, mine_ref, send_ref):
    sources, rows = r_ref.shape[0], r_ref.shape[2]
    decay = [r_ref[:, GATES + p, :] for p in range(3)]
    gate = [r_ref[:, GATES + 3 + p, :].astype(F32) for p in range(3)]
    gate = gate[0] + gate[1] + gate[2]
    after = (iota((rows, rows), 0) > iota((rows, rows), 1)).astype(BF16)
    later = (iota((sources, sources), 1) > iota((sources, sources), 0)).astype(BF16)
    suffix = sum(dot(d, after, (1, 0)) for d in decay)
    rest = sum(dot(later, d, (1, 0)) for d in decay)
    total = sum(jnp.sum(d.astype(F32), axis=0, keepdims=True) for d in decay)
    total = jnp.sum(total, axis=1, keepdims=True)
    tail = suffix + jnp.sum(rest, axis=1, keepdims=True) + gate
    new_m = jnp.max(jnp.max(tail, axis=1, keepdims=True), axis=0, keepdims=True)
    weight = jnp.exp(tail - new_m)
    state = jnp.zeros((PIECE + 8, PIECE), F32)
    for g in range(sources * rows // CHUNK):
        mine = chunk_blocks(r_ref, g)
        turned = beside(r_ref, mine, 0, PIECE)
        share = jnp.concatenate([weight[b : b + 1, :] for b in mine], axis=1)
        keys = key_rows(r_ref, mine)
        state = state + dot(
            weighted_values(turned, share), jnp.concatenate([keys, keys], axis=0), (1, 0)
        )
    c_new = state[0:PIECE]
    n_new = state[PIECE : PIECE + 1] + state[PIECE + 1 : PIECE + 2]

    place = iota((8, PIECE), 0)
    rest = jnp.where(place == 0, n_new, jnp.where(place == 1, new_m, total))
    first = first_core()
    low, high = c_new[0:HALF], c_new[HALF:PIECE]
    mine_ref[0:HALF, :] = jnp.where(first, low, high)
    send_ref[0:HALF, :] = jnp.where(first, high, low)
    mine_ref[HALF:, :] = rest
    send_ref[HALF:, :] = rest


def scalar(rows, n):
    return rows[n : n + 1, 0:1]


def pair_kernel(mine_ref, theirs_ref, z_ref, first_ref):
    first = first_core()
    mine, theirs = mine_ref[...], theirs_ref[...]
    early = jnp.where(first, mine, theirs)
    late = jnp.where(first, theirs, mine)
    first_ref[...] = early
    late_f = scalar(late, HALF + 2)
    moved = scalar(early, HALF + 1) + late_f
    late_m = scalar(late, HALF + 1)
    new_m = jnp.maximum(moved, late_m)
    joined = jnp.exp(moved - new_m) * early + jnp.exp(late_m - new_m) * late
    count, slab = z_ref.shape[0], z_ref.shape[1] - 8
    place = iota((8, PIECE), 0)
    rest = jnp.where(place == 1, new_m, scalar(early, HALF + 2) + late_f)
    rest = jnp.where(place == 0, joined[HALF : HALF + 1], rest)
    for i in range(count):
        z_ref[i, 0:slab, :] = joined[i * slab : (i + 1) * slab]
        z_ref[i, slab:, :] = rest


def in_parts(pairs, sem, parts):
    started = []
    for p in range(parts):
        copies = []
        for n, (a, b) in enumerate(pairs):
            share = a.shape[0] // parts
            here = pl.ds(p * share, share)
            copies.append(pltpu.make_async_copy(a.at[here], b.at[here], sem.at[len(pairs) * p + n]))
            copies[-1].start()
        started.append(copies)
    return started


def entries_kernel(r_in, entry_out, aux_ref, r_ref, entry_ref, in_sem, out_sem):
    upper = (iota((CHUNK, CHUNK), 0) <= iota((CHUNK, CHUNK), 1)).astype(BF16)
    row = iota((8, CHUNK), 0)
    state = jnp.zeros((PIECE, PIECE), F32)
    normal = jnp.zeros((1, PIECE), F32)
    old_m = jnp.full((1, 1), VERY_NEGATIVE, F32)
    start = jnp.zeros((1, 1), F32)
    steps = entry_ref.shape[0]
    arriving = in_parts([(r_in, r_ref)], in_sem, PARTS)
    leaving = []
    for step in range(steps):
        if step % (steps // PARTS) == 0:
            arriving[step // (steps // PARTS)][0].wait()
        mine = chunk_blocks(r_ref, step)
        entry_ref[step] = jnp.concatenate(halves(state), axis=1)
        if (step + 1) % (steps // PARTS) == 0:
            part = step // (steps // PARTS)
            here = pl.ds(part * (steps // PARTS), steps // PARTS)
            leaving.append(
                pltpu.make_async_copy(entry_ref.at[here], entry_out.at[here], out_sem.at[part])
            )
            leaving[-1].start()
        gates = beside(r_ref, mine, GATES, GATES + GATE_ROWS)
        cum = dot(gates, upper, (1, 0))
        cum = cum[0:1] + cum[1:2] + cum[2:3]
        gate = gates.astype(F32)
        gate = gate[3:4] + gate[4:5] + gate[5:6]
        total = cum[:, CHUNK - 1 : CHUNK]
        tail = total - cum + gate
        new_m = jnp.maximum(old_m + total, jnp.max(tail, axis=1, keepdims=True))
        keep = jnp.exp(old_m + total - new_m)
        aux = jnp.where(row == 0, normal, 0.0)
        for p, x in ((1, old_m), (2, start), (3, cum), (4, gate - cum)):
            aux = jnp.where(row == p, x, aux)
        aux_ref[step] = aux
        if step < steps - 1:
            keys = key_rows(r_ref, mine)
            fresh = dot(
                weighted_values(beside(r_ref, mine, 0, PIECE), jnp.exp(tail - new_m)),
                jnp.concatenate([keys, keys], axis=0),
                (1, 0),
            )
            state = keep * state + fresh[0:PIECE]
            normal = keep * normal + fresh[PIECE : PIECE + 1] + fresh[PIECE + 1 : PIECE + 2]
            old_m = new_m
            start = start + total
    for copy in leaving:
        copy.wait()


def near_kernel(z_ref, sum_ref, y_ref, meta_ref):
    count, slab = z_ref.shape[0], z_ref.shape[1] - 8
    state = jnp.zeros((slab, PIECE), F32)
    normal = jnp.zeros((1, PIECE), F32)
    old_m = jnp.full((1, 1), VERY_NEGATIVE, F32)
    total = jnp.zeros((1, 1), F32)
    for i in range(count):
        y_ref[i] = state
        for n, x in enumerate((old_m, total, normal)):
            meta_ref[n * count + i : n * count + i + 1, :] = jnp.broadcast_to(x, (1, PIECE))
        rest = z_ref[i, slab:, :]
        m, f = scalar(rest, 1), scalar(rest, 2)
        new_m = jnp.maximum(old_m + f, m)
        keep, take = jnp.exp(old_m + f - new_m), jnp.exp(m - new_m)
        state = keep * state + take * z_ref[i, 0:slab, :]
        normal = keep * normal + take * rest[0:1]
        old_m = new_m
        total = total + f
    place = iota((8, PIECE), 0)
    sum_ref[0:slab, :] = state
    sum_ref[slab:, :] = jnp.where(place == 0, normal, jnp.where(place == 1, old_m, total))


def far_kernel(*refs):
    y_ref, meta_ref, first_ref, *ahead, out_ref, nin_ref = refs
    count, slab = y_ref.shape[0], y_ref.shape[1]
    chip = lax.axis_index("seq") // 2
    near_at, group = lax.rem(chip, count), chip // count
    second = jnp.logical_not(first_core())
    state = jnp.zeros((slab, PIECE), F32)
    normal = jnp.zeros((1, PIECE), F32)
    old_m = jnp.full((1, 1), VERY_NEGATIVE, F32)
    for d in range(len(ahead), 0, -1):
        there = group >= d
        rest = ahead[d - 1][slab:, :]
        m = jnp.where(there, scalar(rest, 1), VERY_NEGATIVE)
        f = jnp.where(there, scalar(rest, 2), 0.0)
        new_m = jnp.maximum(old_m + f, m)
        keep, take = jnp.exp(old_m + f - new_m), jnp.exp(m - new_m)
        state = keep * state + take * ahead[d - 1][0:slab, :]
        normal = keep * normal + take * rest[0:1]
        old_m = new_m
    meta = meta_ref[...]
    own_m = jnp.full((1, 1), VERY_NEGATIVE, F32)
    own_n = jnp.zeros((1, PIECE), F32)
    for i in range(count):
        m, f = scalar(meta, i), scalar(meta, count + i)
        new_m = jnp.maximum(old_m + f, m)
        keep, take = jnp.exp(old_m + f - new_m), jnp.exp(m - new_m)
        out_ref[i] = keep * state + take * y_ref[i]
        n = keep * normal + take * meta[2 * count + i : 2 * count + i + 1]
        own_m = jnp.where(near_at == i, new_m, own_m)
        own_n = jnp.where(near_at == i, n, own_n)
    first_m = scalar(first_ref, HALF + 1)
    moved = own_m + scalar(first_ref, HALF + 2)
    next_m = jnp.maximum(moved, first_m)
    old_share, new_share = jnp.exp(moved - next_m), jnp.exp(first_m - next_m)
    next_n = old_share * own_n + new_share * first_ref[HALF : HALF + 1, :]
    place = iota((8, PIECE), 0)
    area = jnp.where(place == 0, old_share, new_share)
    area = jnp.where(place == 6, jnp.where(second, next_m, own_m), area)
    for p, part in enumerate(thirds(jnp.where(second, next_n, own_n), 1.0)):
        area = jnp.where(place == 3 + p, part, area)
    nin_ref[...] = area


def mix_kernel(p_ref, first_ref, nin_ref, keep_ref, send_ref):
    before = p_ref[...]
    after = before * nin_ref[0:1, 0:1] + first_ref[0:HALF, :] * nin_ref[1:2, 0:1]
    first = first_core()
    keep_ref[...] = jnp.where(first, before, after)
    send_ref[...] = jnp.where(first, after, before)


def inside_kernel(
    r_in, asked_ref, entry_in, aux_ref, nin_ref, num_ref, row_ref, r_ref, entry_ref, in_sem
):
    factor = PIECE**-0.5
    before = nin_ref[...]
    before_m = before[6:7, 0:1]
    causal = iota((CHUNK, CHUNK), 0) <= iota((CHUNK, CHUNK), 1)
    row = iota((8, CHUNK), 0)
    steps = num_ref.shape[0]
    pairs = [(r_in, r_ref), (entry_in, entry_ref)]
    arriving = in_parts(pairs, in_sem, PARTS)
    for step in range(steps):
        if step % (steps // PARTS) == 0:
            for copy in arriving[step // (steps // PARTS)]:
                copy.wait()
        mine = chunk_blocks(r_ref, step)
        asked = beside(asked_ref, mine, 0, PIECE)
        turned = beside(r_ref, mine, 0, PIECE)
        aux = aux_ref[step]
        cum = aux[3:4]
        carried = cum + aux[1:2]
        score = dot(key_rows(r_ref, mine), asked, (1, 0))
        gap = jnp.where(causal, aux.T[:, 4:5] + cum, VERY_NEGATIVE)
        top = jnp.maximum(carried, jnp.max(gap, axis=0, keepdims=True))
        weighted = jnp.exp(gap - top) * score
        outside = jnp.exp(carried - top)
        normal = jnp.where((row >= 3) & (row < 6), before, 0.0)
        for p, part in enumerate(thirds(aux[0:1], 1.0)):
            normal = jnp.where(row == p, part, normal)
        reached = dot(normal.astype(BF16), asked, (1, 0))
        den = jnp.sum(weighted, axis=0, keepdims=True)
        den = factor * (den + outside * (reached[0:1] + reached[1:2] + reached[2:3]))
        carried = cum + aux[2:3] + before_m
        new_m = jnp.maximum(top, carried)
        inside = jnp.exp(top - new_m)
        ahead = jnp.exp(carried - new_m) * factor
        den = den * inside + ahead * (reached[3:4] + reached[4:5] + reached[5:6])
        over = 1.0 / jnp.maximum(jnp.abs(den), 1.0)
        inside = inside * over * factor
        num = dot(
            jnp.concatenate([turned, turned], axis=1),
            jnp.concatenate(halves(weighted), axis=0),
            (1, 0),
        )
        read = dot(
            entry_ref[step],
            jnp.concatenate([asked, asked], axis=0),
            (1, 0),
        )
        num_ref[step] = inside * num + (inside * outside) * read
        row_ref[step] = jnp.broadcast_to(ahead * over, (8, CHUNK))


def finish_kernel(
    asked_in, num_ref, row_ref, keep_ref, came_ref, out_ref, asked_ref, buffer_ref, in_sem, out_sem,
):
    steps = num_ref.shape[0]
    parts = in_sem.shape[0]
    share = asked_ref.shape[0] // parts
    arriving = []
    for p in range(parts):
        blocks = pl.ds(p * share, share)
        arriving.append(pltpu.make_async_copy(asked_in.at[blocks], asked_ref.at[blocks], in_sem.at[p]))
        arriving[-1].start()
    first = first_core()
    keep, came = keep_ref[...], came_ref[...]
    state = jnp.concatenate([jnp.where(first, keep, came), jnp.where(first, came, keep)], axis=0)
    both = jnp.concatenate(halves(state), axis=1)
    each = steps // out_sem.shape[0]
    leaving = []
    for step in range(steps):
        if step % (steps // parts) == 0:
            arriving[step // (steps // parts)].wait()
        asked = beside(asked_ref, chunk_blocks(asked_ref, step), 0, PIECE)
        read = dot(both, jnp.concatenate([asked, asked], axis=0), (1, 0))
        out = num_ref[step] + read * row_ref[step, 0:1, :]
        buffer_ref[pl.ds(step * CHUNK, CHUNK), :] = out.astype(BF16).T
        if step % each == each - 1:
            here = pl.ds((step - each + 1) * CHUNK, each * CHUNK)
            leaving.append(
                pltpu.make_async_copy(buffer_ref.at[here], out_ref.at[here], out_sem.at[step // each])
            )
            leaving[-1].start()
    for copy in leaving:
        copy.wait()


def far(x):
    return pltpu.with_memory_space_constraint(x, pltpu.HBM)


def near(x):
    return pltpu.with_memory_space_constraint(x, pltpu.VMEM)


NEAR = pl.BlockSpec(memory_space=pltpu.VMEM)
FAR = pl.BlockSpec()
PARAMS = pltpu.CompilerParams(vmem_limit_bytes=VMEM_LIMIT)


def on_device(queries, keys, values, input_pre, forget_pre):
    rows = queries.shape[0]
    pieces = lax.axis_size("head")
    shards = lax.axis_size("seq")
    tokens = pieces * rows
    steps = tokens // CHUNK
    tall = GATES + GATE_ROWS
    chips = shards // 2
    close = NEAR_CHIPS
    slab = HALF // close
    pairs = [(i, i ^ 1) for i in range(shards)]
    groups = [
        [2 * (g + z) + c for z in range(close)] for g in range(0, chips, close) for c in range(2)
    ]

    packed = pl.pallas_call(
        pack_kernel,
        in_specs=[pl.BlockSpec(memory_space=pltpu.HBM)] * 4,
        out_specs=NEAR,
        out_shape=pltpu.VMEM((pieces, tall, rows), BF16),
        scratch_shapes=[
            pltpu.VMEM(keys.shape, BF16),
            pltpu.VMEM(values.shape, BF16),
            pltpu.VMEM((input_pre.shape[1], rows), F32),
            pltpu.VMEM((input_pre.shape[1], rows), F32),
            pltpu.SemaphoreType.DMA((4,)),
        ],
        compiler_params=PARAMS,
        name="pack",
    )(*(far(x) for x in (keys, values, input_pre.T, forget_pre.T)))

    received = lax.all_to_all(packed, "head", split_axis=0, concat_axis=0, tiled=True)

    half = pltpu.VMEM((HALF + 8, PIECE), F32)
    mine, send = pl.pallas_call(
        summary_kernel,
        in_specs=[NEAR],
        out_specs=[NEAR] * 2,
        out_shape=[half] * 2,
        compiler_params=PARAMS,
        name="summary",
    )(near(received))

    theirs = lax.ppermute(send, "seq", pairs)

    summary, first = pl.pallas_call(
        pair_kernel,
        in_specs=[NEAR, NEAR],
        out_specs=[NEAR, FAR],
        out_shape=[
            pltpu.VMEM((close, slab + 8, PIECE), F32),
            jax.ShapeDtypeStruct((HALF + 8, PIECE), F32),
        ],
        compiler_params=PARAMS,
        name="pair",
    )(mine, near(theirs))

    spread = lax.all_to_all(
        summary, "seq", split_axis=0, concat_axis=0, tiled=True, axis_index_groups=groups
    )

    turned = pl.pallas_call(
        turn_kernel,
        in_specs=[FAR],
        out_specs=FAR,
        out_shape=jax.ShapeDtypeStruct((pieces, PIECE, rows), BF16),
        name="turn",
    )(far(queries))
    asked = lax.all_to_all(turned, "head", split_axis=0, concat_axis=0, tiled=True)

    far_spec = pl.BlockSpec(memory_space=pltpu.HBM)
    entries = (steps, PIECE, 2 * PIECE)
    entry, aux = pl.pallas_call(
        entries_kernel,
        in_specs=[far_spec],
        out_specs=[far_spec, FAR],
        out_shape=[
            jax.ShapeDtypeStruct(entries, BF16),
            jax.ShapeDtypeStruct((steps, 8, CHUNK), F32),
        ],
        scratch_shapes=[
            pltpu.VMEM(received.shape, BF16),
            pltpu.VMEM(entries, BF16),
            pltpu.SemaphoreType.DMA((PARTS,)),
            pltpu.SemaphoreType.DMA((PARTS,)),
        ],
        name="entries",
    )(far(received))

    group_sum, local, meta = pl.pallas_call(
        near_kernel,
        in_specs=[NEAR],
        out_specs=[NEAR, FAR, FAR],
        out_shape=[
            pltpu.VMEM((slab + 8, PIECE), F32),
            jax.ShapeDtypeStruct((close, slab, PIECE), F32),
            jax.ShapeDtypeStruct((16, PIECE), F32),
        ],
        compiler_params=pltpu.CompilerParams(vmem_limit_bytes=FAR_LIMIT),
        name="near",
    )(near(spread))

    ahead = []
    for d in range(1, chips // close):
        step = 2 * close * d
        ahead.append(lax.ppermute(group_sum, "seq", [(i, i + step) for i in range(shards - step)]))

    before, normal = pl.pallas_call(
        far_kernel,
        in_specs=[FAR, FAR] + [NEAR] * (1 + len(ahead)),
        out_specs=[FAR] * 2,
        out_shape=[
            jax.ShapeDtypeStruct((close, slab, PIECE), F32),
            jax.ShapeDtypeStruct((8, PIECE), F32),
        ],
        compiler_params=pltpu.CompilerParams(vmem_limit_bytes=FAR_LIMIT),
        name="far",
    )(local, meta, near(first), *(near(a) for a in ahead))

    back = lax.all_to_all(
        before, "seq", split_axis=0, concat_axis=0, tiled=True, axis_index_groups=groups
    )

    keep, lend = pl.pallas_call(
        mix_kernel,
        in_specs=[NEAR] * 3,
        out_specs=[NEAR] * 2,
        out_shape=[pltpu.VMEM((HALF, PIECE), F32)] * 2,
        compiler_params=PARAMS,
        name="mix",
    )(near(back.reshape(HALF, PIECE)), near(first), near(normal))
    came = lax.ppermute(lend, "seq", pairs)

    num, line = pl.pallas_call(
        inside_kernel,
        in_specs=[far_spec, NEAR, far_spec, FAR, FAR],
        out_specs=[NEAR] * 2,
        out_shape=[
            pltpu.VMEM((steps, PIECE, CHUNK), F32),
            pltpu.VMEM((steps, 8, CHUNK), F32),
        ],
        scratch_shapes=[
            pltpu.VMEM(received.shape, BF16),
            pltpu.VMEM(entries, BF16),
            pltpu.SemaphoreType.DMA((2 * PARTS,)),
        ],
        compiler_params=pltpu.CompilerParams(vmem_limit_bytes=INSIDE_LIMIT),
        name="inside",
    )(far(received), near(asked), far(entry), aux, normal)

    return pl.pallas_call(
        finish_kernel,
        in_specs=[pl.BlockSpec(memory_space=pltpu.HBM)] + [NEAR] * 4,
        out_specs=pl.BlockSpec(memory_space=pltpu.HBM),
        out_shape=jax.ShapeDtypeStruct((tokens, PIECE), BF16),
        scratch_shapes=[
            pltpu.VMEM(asked.shape, BF16),
            pltpu.VMEM((tokens, PIECE), BF16),
            pltpu.SemaphoreType.DMA((2,)),
            pltpu.SemaphoreType.DMA((steps // 2,)),
        ],
        compiler_params=PARAMS,
        name="finish",
    )(far(asked), num, line, keep, near(came))


def solution(mesh):
    spec = P(("seq", "head"), None)

    return jax.shard_map(on_device, mesh=mesh, in_specs=(spec,) * 5, out_specs=P("seq", "head"), check_vma=False)
```

```python
import jax
import jax.numpy as jnp
from jax import lax
from jax.experimental import pallas as pl
from jax.experimental.pallas import tpu as pltpu
from jax.sharding import PartitionSpec as P

VERY_NEGATIVE = -1e30
CHUNK = 256
PIECE = 256
HALF = PIECE // 2
KEYS = PIECE
GATES = 2 * PIECE
VMEM_LIMIT = 24 << 20
INSIDE_LIMIT = 56 << 20
FAR_LIMIT = 59 << 20
NEAR_CHIPS = 4
PARTS = 2
GATE_ROWS = 8
F32 = jnp.float32
BF16 = jnp.bfloat16


def dot(a, b, contract):
    return lax.dot_general(a, b, ((contract[:1], contract[1:]), ((), ())), preferred_element_type=F32)


def halves(x):
    top = x.astype(BF16)
    return top, (x - top.astype(F32)).astype(BF16)


def thirds(x, scale):
    first = x.astype(BF16).astype(F32)
    rest = (x - first) * scale
    second = rest.astype(BF16).astype(F32)
    third = ((rest - second) * scale).astype(BF16).astype(F32)
    return first, second, third


def iota(shape, dim):
    return lax.broadcasted_iota(jnp.int32, shape, dim)


def first_core():
    return lax.rem(lax.axis_index("seq"), 2) == 0


def pack_kernel(k_in, v_in, gate_in, forget_in, out_ref, k_ref, v_ref, gate_ref, forget_ref, sem):
    rows = k_ref.shape[0]
    pairs = (gate_in, gate_ref), (forget_in, forget_ref), (v_in, v_ref), (k_in, k_ref)
    copies = [pltpu.make_async_copy(a, b, sem.at[n]) for n, (a, b) in enumerate(pairs)]
    for copy in copies:
        copy.start()
    copies[0].wait()
    copies[1].wait()
    parts = []
    for x in (-jnp.log1p(jnp.exp(-forget_ref[...])), gate_ref[...]):
        parts += thirds(x, 1.0)
    for copy in copies[2:]:
        copy.wait()
    row = iota((GATE_ROWS, rows), 0)
    for h in range(k_ref.shape[1] // PIECE):
        area = jnp.zeros((GATE_ROWS, rows), F32)
        for p in range(6):
            area = jnp.where(row == p, parts[p][h : h + 1], area)
        area = area.astype(BF16)
        for u in range(2):
            n = 2 * h + u
            out_ref[n, 0:PIECE, :] = v_ref[:, n * PIECE : (n + 1) * PIECE].T
            for c in range(2):
                left = h * PIECE + c * HALF
                out_ref[n, KEYS + c * HALF : KEYS + (c + 1) * HALF, :] = k_ref[:, left : left + HALF]
            out_ref[n, GATES : GATES + GATE_ROWS, :] = area


def turn_kernel(q_ref, out_ref):
    for h in range(q_ref.shape[1] // PIECE):
        turned = q_ref[:, h * PIECE : (h + 1) * PIECE].T
        out_ref[2 * h] = turned
        out_ref[2 * h + 1] = turned


def beside(ref, blocks, low, high):
    return jnp.concatenate([ref[b, low:high, :] for b in blocks], axis=1)


def key_rows(ref, blocks):
    return jnp.concatenate(
        [
            jnp.concatenate([ref[b, KEYS + c * HALF : KEYS + (c + 1) * HALF, :] for c in range(2)], axis=1)
            for b in blocks
        ],
        axis=0,
    )


def chunk_blocks(ref, chunk):
    group = CHUNK // ref.shape[2]
    return range(chunk * group, (chunk + 1) * group)


def weighted_values(turned, weight):
    top, low = halves(turned.astype(F32) * weight)
    first, second, third = thirds(weight, 1.0)
    row = iota((8, weight.shape[1]), 0)
    left = jnp.where(row == 0, first, jnp.where(row == 1, third, 0.0)).astype(BF16)
    right = jnp.where(row == 0, second, 0.0).astype(BF16)
    return jnp.concatenate(
        [jnp.concatenate([top, left], axis=0), jnp.concatenate([low, right], axis=0)], axis=1
    )


def summary_kernel(r_ref, mine_ref, send_ref):
    sources, rows = r_ref.shape[0], r_ref.shape[2]
    decay = [r_ref[:, GATES + p, :] for p in range(3)]
    gate = [r_ref[:, GATES + 3 + p, :].astype(F32) for p in range(3)]
    gate = gate[0] + gate[1] + gate[2]
    after = (iota((rows, rows), 0) > iota((rows, rows), 1)).astype(BF16)
    later = (iota((sources, sources), 1) > iota((sources, sources), 0)).astype(BF16)
    suffix = sum(dot(d, after, (1, 0)) for d in decay)
    rest = sum(dot(later, d, (1, 0)) for d in decay)
    total = sum(jnp.sum(d.astype(F32), axis=0, keepdims=True) for d in decay)
    total = jnp.sum(total, axis=1, keepdims=True)
    tail = suffix + jnp.sum(rest, axis=1, keepdims=True) + gate
    new_m = jnp.max(jnp.max(tail, axis=1, keepdims=True), axis=0, keepdims=True)
    weight = jnp.exp(tail - new_m)
    state = jnp.zeros((PIECE + 8, PIECE), F32)
    for g in range(sources * rows // CHUNK):
        mine = chunk_blocks(r_ref, g)
        turned = beside(r_ref, mine, 0, PIECE)
        share = jnp.concatenate([weight[b : b + 1, :] for b in mine], axis=1)
        keys = key_rows(r_ref, mine)
        state = state + dot(
            weighted_values(turned, share), jnp.concatenate([keys, keys], axis=0), (1, 0)
        )
    c_new = state[0:PIECE]
    n_new = state[PIECE : PIECE + 1] + state[PIECE + 1 : PIECE + 2]

    place = iota((8, PIECE), 0)
    rest = jnp.where(place == 0, n_new, jnp.where(place == 1, new_m, total))
    first = first_core()
    low, high = c_new[0:HALF], c_new[HALF:PIECE]
    mine_ref[0:HALF, :] = jnp.where(first, low, high)
    send_ref[0:HALF, :] = jnp.where(first, high, low)
    mine_ref[HALF:, :] = rest
    send_ref[HALF:, :] = rest


def scalar(rows, n):
    return rows[n : n + 1, 0:1]


def pair_kernel(mine_ref, theirs_ref, z_ref, first_ref):
    first = first_core()
    mine, theirs = mine_ref[...], theirs_ref[...]
    early = jnp.where(first, mine, theirs)
    late = jnp.where(first, theirs, mine)
    first_ref[...] = early
    late_f = scalar(late, HALF + 2)
    moved = scalar(early, HALF + 1) + late_f
    late_m = scalar(late, HALF + 1)
    new_m = jnp.maximum(moved, late_m)
    joined = jnp.exp(moved - new_m) * early + jnp.exp(late_m - new_m) * late
    count, slab = z_ref.shape[0], z_ref.shape[1] - 8
    place = iota((8, PIECE), 0)
    rest = jnp.where(place == 1, new_m, scalar(early, HALF + 2) + late_f)
    rest = jnp.where(place == 0, joined[HALF : HALF + 1], rest)
    for i in range(count):
        z_ref[i, 0:slab, :] = joined[i * slab : (i + 1) * slab]
        z_ref[i, slab:, :] = rest


def in_parts(pairs, sem, parts):
    started = []
    for p in range(parts):
        copies = []
        for n, (a, b) in enumerate(pairs):
            share = a.shape[0] // parts
            here = pl.ds(p * share, share)
            copies.append(pltpu.make_async_copy(a.at[here], b.at[here], sem.at[len(pairs) * p + n]))
            copies[-1].start()
        started.append(copies)
    return started


def entries_kernel(r_in, entry_out, aux_ref, r_ref, entry_ref, in_sem, out_sem):
    upper = (iota((CHUNK, CHUNK), 0) <= iota((CHUNK, CHUNK), 1)).astype(BF16)
    row = iota((8, CHUNK), 0)
    state = jnp.zeros((PIECE, PIECE), F32)
    normal = jnp.zeros((1, PIECE), F32)
    old_m = jnp.full((1, 1), VERY_NEGATIVE, F32)
    start = jnp.zeros((1, 1), F32)
    steps = entry_ref.shape[0]
    arriving = in_parts([(r_in, r_ref)], in_sem, PARTS)
    leaving = []
    for step in range(steps):
        if step % (steps // PARTS) == 0:
            arriving[step // (steps // PARTS)][0].wait()
        mine = chunk_blocks(r_ref, step)
        entry_ref[step] = jnp.concatenate(halves(state), axis=1)
        if (step + 1) % (steps // PARTS) == 0:
            part = step // (steps // PARTS)
            here = pl.ds(part * (steps // PARTS), steps // PARTS)
            leaving.append(
                pltpu.make_async_copy(entry_ref.at[here], entry_out.at[here], out_sem.at[part])
            )
            leaving[-1].start()
        gates = beside(r_ref, mine, GATES, GATES + GATE_ROWS)
        cum = dot(gates, upper, (1, 0))
        cum = cum[0:1] + cum[1:2] + cum[2:3]
        gate = gates.astype(F32)
        gate = gate[3:4] + gate[4:5] + gate[5:6]
        total = cum[:, CHUNK - 1 : CHUNK]
        tail = total - cum + gate
        new_m = jnp.maximum(old_m + total, jnp.max(tail, axis=1, keepdims=True))
        keep = jnp.exp(old_m + total - new_m)
        aux = jnp.where(row == 0, normal, 0.0)
        for p, x in ((1, old_m), (2, start), (3, cum), (4, gate - cum)):
            aux = jnp.where(row == p, x, aux)
        aux_ref[step] = aux
        if step < steps - 1:
            keys = key_rows(r_ref, mine)
            fresh = dot(
                weighted_values(beside(r_ref, mine, 0, PIECE), jnp.exp(tail - new_m)),
                jnp.concatenate([keys, keys], axis=0),
                (1, 0),
            )
            state = keep * state + fresh[0:PIECE]
            normal = keep * normal + fresh[PIECE : PIECE + 1] + fresh[PIECE + 1 : PIECE + 2]
            old_m = new_m
            start = start + total
    for copy in leaving:
        copy.wait()


def near_states(z_ref):
    count, slab = z_ref.shape[0], z_ref.shape[1] - 8
    state = jnp.zeros((slab, PIECE), F32)
    normal = jnp.zeros((1, PIECE), F32)
    old_m = jnp.full((1, 1), VERY_NEGATIVE, F32)
    total = jnp.zeros((1, 1), F32)
    states = [(state, normal, old_m, total)]
    for i in range(count):
        rest = z_ref[i, slab:, :]
        m, f = scalar(rest, 1), scalar(rest, 2)
        new_m = jnp.maximum(old_m + f, m)
        keep, take = jnp.exp(old_m + f - new_m), jnp.exp(m - new_m)
        state = keep * state + take * z_ref[i, 0:slab, :]
        normal = keep * normal + take * rest[0:1]
        old_m = new_m
        total = total + f
        states.append((state, normal, old_m, total))
    return states


def near_kernel(z_ref, sum_ref):
    slab = z_ref.shape[1] - 8
    state, normal, m, total = near_states(z_ref)[-1]
    place = iota((8, PIECE), 0)
    sum_ref[0:slab, :] = state
    sum_ref[slab:, :] = jnp.where(place == 0, normal, jnp.where(place == 1, m, total))


def far_kernel(*refs):
    z_ref, first_ref, *ahead, out_ref, nin_ref = refs
    count, slab = z_ref.shape[0], z_ref.shape[1] - 8
    chip = lax.axis_index("seq") // 2
    near_at, group = lax.rem(chip, count), chip // count
    second = jnp.logical_not(first_core())
    state = jnp.zeros((slab, PIECE), F32)
    normal = jnp.zeros((1, PIECE), F32)
    old_m = jnp.full((1, 1), VERY_NEGATIVE, F32)
    for d in range(len(ahead), 0, -1):
        there = group >= d
        rest = ahead[d - 1][slab:, :]
        m = jnp.where(there, scalar(rest, 1), VERY_NEGATIVE)
        f = jnp.where(there, scalar(rest, 2), 0.0)
        new_m = jnp.maximum(old_m + f, m)
        keep, take = jnp.exp(old_m + f - new_m), jnp.exp(m - new_m)
        state = keep * state + take * ahead[d - 1][0:slab, :]
        normal = keep * normal + take * rest[0:1]
        old_m = new_m
    local = near_states(z_ref)
    own_m = jnp.full((1, 1), VERY_NEGATIVE, F32)
    own_n = jnp.zeros((1, PIECE), F32)
    for i in range(count):
        near_state, near_normal, m, f = local[i]
        new_m = jnp.maximum(old_m + f, m)
        keep, take = jnp.exp(old_m + f - new_m), jnp.exp(m - new_m)
        out_ref[i] = keep * state + take * near_state
        n = keep * normal + take * near_normal
        own_m = jnp.where(near_at == i, new_m, own_m)
        own_n = jnp.where(near_at == i, n, own_n)
    first_m = scalar(first_ref, HALF + 1)
    moved = own_m + scalar(first_ref, HALF + 2)
    next_m = jnp.maximum(moved, first_m)
    old_share, new_share = jnp.exp(moved - next_m), jnp.exp(first_m - next_m)
    next_n = old_share * own_n + new_share * first_ref[HALF : HALF + 1, :]
    place = iota((8, PIECE), 0)
    area = jnp.where(place == 0, old_share, new_share)
    area = jnp.where(place == 6, jnp.where(second, next_m, own_m), area)
    for p, part in enumerate(thirds(jnp.where(second, next_n, own_n), 1.0)):
        area = jnp.where(place == 3 + p, part, area)
    nin_ref[...] = area


def mix_kernel(p_ref, first_ref, nin_ref, keep_ref, send_ref):
    before = p_ref[...]
    after = before * nin_ref[0:1, 0:1] + first_ref[0:HALF, :] * nin_ref[1:2, 0:1]
    first = first_core()
    keep_ref[...] = jnp.where(first, before, after)
    send_ref[...] = jnp.where(first, after, before)


def inside_kernel(
    r_in, asked_ref, entry_in, aux_ref, nin_ref, num_ref, row_ref, r_ref, entry_ref, in_sem
):
    factor = PIECE**-0.5
    before = nin_ref[...]
    before_m = before[6:7, 0:1]
    causal = iota((CHUNK, CHUNK), 0) <= iota((CHUNK, CHUNK), 1)
    row = iota((8, CHUNK), 0)
    steps = num_ref.shape[0]
    pairs = [(r_in, r_ref), (entry_in, entry_ref)]
    arriving = in_parts(pairs, in_sem, PARTS)
    for step in range(steps):
        if step % (steps // PARTS) == 0:
            for copy in arriving[step // (steps // PARTS)]:
                copy.wait()
        mine = chunk_blocks(r_ref, step)
        asked = beside(asked_ref, mine, 0, PIECE)
        turned = beside(r_ref, mine, 0, PIECE)
        aux = aux_ref[step]
        cum = aux[3:4]
        carried = cum + aux[1:2]
        score = dot(key_rows(r_ref, mine), asked, (1, 0))
        gap = jnp.where(causal, aux.T[:, 4:5] + cum, VERY_NEGATIVE)
        top = jnp.maximum(carried, jnp.max(gap, axis=0, keepdims=True))
        weighted = jnp.exp(gap - top) * score
        outside = jnp.exp(carried - top)
        normal = jnp.where((row >= 3) & (row < 6), before, 0.0)
        for p, part in enumerate(thirds(aux[0:1], 1.0)):
            normal = jnp.where(row == p, part, normal)
        reached = dot(normal.astype(BF16), asked, (1, 0))
        den = jnp.sum(weighted, axis=0, keepdims=True)
        den = factor * (den + outside * (reached[0:1] + reached[1:2] + reached[2:3]))
        carried = cum + aux[2:3] + before_m
        new_m = jnp.maximum(top, carried)
        inside = jnp.exp(top - new_m)
        ahead = jnp.exp(carried - new_m) * factor
        den = den * inside + ahead * (reached[3:4] + reached[4:5] + reached[5:6])
        over = 1.0 / jnp.maximum(jnp.abs(den), 1.0)
        inside = inside * over * factor
        num = dot(
            jnp.concatenate([turned, turned], axis=1),
            jnp.concatenate(halves(weighted), axis=0),
            (1, 0),
        )
        read = dot(
            entry_ref[step],
            jnp.concatenate([asked, asked], axis=0),
            (1, 0),
        )
        num_ref[step] = inside * num + (inside * outside) * read
        row_ref[step] = jnp.broadcast_to(ahead * over, (8, CHUNK))


def finish_kernel(
    asked_in, num_ref, row_ref, keep_ref, came_ref, out_ref, asked_ref, buffer_ref, in_sem, out_sem,
):
    steps = num_ref.shape[0]
    parts = in_sem.shape[0]
    share = asked_ref.shape[0] // parts
    arriving = []
    for p in range(parts):
        blocks = pl.ds(p * share, share)
        arriving.append(pltpu.make_async_copy(asked_in.at[blocks], asked_ref.at[blocks], in_sem.at[p]))
        arriving[-1].start()
    first = first_core()
    keep, came = keep_ref[...], came_ref[...]
    state = jnp.concatenate([jnp.where(first, keep, came), jnp.where(first, came, keep)], axis=0)
    both = jnp.concatenate(halves(state), axis=1)
    each = steps // out_sem.shape[0]
    leaving = []
    for step in range(steps):
        if step % (steps // parts) == 0:
            arriving[step // (steps // parts)].wait()
        asked = beside(asked_ref, chunk_blocks(asked_ref, step), 0, PIECE)
        read = dot(both, jnp.concatenate([asked, asked], axis=0), (1, 0))
        out = num_ref[step] + read * row_ref[step, 0:1, :]
        buffer_ref[pl.ds(step * CHUNK, CHUNK), :] = out.astype(BF16).T
        if step % each == each - 1:
            here = pl.ds((step - each + 1) * CHUNK, each * CHUNK)
            leaving.append(
                pltpu.make_async_copy(buffer_ref.at[here], out_ref.at[here], out_sem.at[step // each])
            )
            leaving[-1].start()
    for copy in leaving:
        copy.wait()


def far(x):
    return pltpu.with_memory_space_constraint(x, pltpu.HBM)


def near(x):
    return pltpu.with_memory_space_constraint(x, pltpu.VMEM)


NEAR = pl.BlockSpec(memory_space=pltpu.VMEM)
FAR = pl.BlockSpec()
PARAMS = pltpu.CompilerParams(vmem_limit_bytes=VMEM_LIMIT)


def on_device(queries, keys, values, input_pre, forget_pre):
    rows = queries.shape[0]
    pieces = lax.axis_size("head")
    shards = lax.axis_size("seq")
    tokens = pieces * rows
    steps = tokens // CHUNK
    tall = GATES + GATE_ROWS
    chips = shards // 2
    close = NEAR_CHIPS
    slab = HALF // close
    pairs = [(i, i ^ 1) for i in range(shards)]
    groups = [
        [2 * (g + z) + c for z in range(close)] for g in range(0, chips, close) for c in range(2)
    ]

    packed = pl.pallas_call(
        pack_kernel,
        in_specs=[pl.BlockSpec(memory_space=pltpu.HBM)] * 4,
        out_specs=NEAR,
        out_shape=pltpu.VMEM((pieces, tall, rows), BF16),
        scratch_shapes=[
            pltpu.VMEM(keys.shape, BF16),
            pltpu.VMEM(values.shape, BF16),
            pltpu.VMEM((input_pre.shape[1], rows), F32),
            pltpu.VMEM((input_pre.shape[1], rows), F32),
            pltpu.SemaphoreType.DMA((4,)),
        ],
        compiler_params=PARAMS,
        name="pack",
    )(*(far(x) for x in (keys, values, input_pre.T, forget_pre.T)))

    received = lax.all_to_all(packed, "head", split_axis=0, concat_axis=0, tiled=True)

    half = pltpu.VMEM((HALF + 8, PIECE), F32)
    mine, send = pl.pallas_call(
        summary_kernel,
        in_specs=[NEAR],
        out_specs=[NEAR] * 2,
        out_shape=[half] * 2,
        compiler_params=PARAMS,
        name="summary",
    )(near(received))

    theirs = lax.ppermute(send, "seq", pairs)

    summary, first = pl.pallas_call(
        pair_kernel,
        in_specs=[NEAR, NEAR],
        out_specs=[NEAR, FAR],
        out_shape=[
            pltpu.VMEM((close, slab + 8, PIECE), F32),
            jax.ShapeDtypeStruct((HALF + 8, PIECE), F32),
        ],
        compiler_params=PARAMS,
        name="pair",
    )(mine, near(theirs))

    spread = lax.all_to_all(
        summary, "seq", split_axis=0, concat_axis=0, tiled=True, axis_index_groups=groups
    )

    turned = pl.pallas_call(
        turn_kernel,
        in_specs=[FAR],
        out_specs=FAR,
        out_shape=jax.ShapeDtypeStruct((pieces, PIECE, rows), BF16),
        name="turn",
    )(far(queries))
    asked = lax.all_to_all(turned, "head", split_axis=0, concat_axis=0, tiled=True)

    far_spec = pl.BlockSpec(memory_space=pltpu.HBM)
    entries = (steps, PIECE, 2 * PIECE)
    entry, aux = pl.pallas_call(
        entries_kernel,
        in_specs=[far_spec],
        out_specs=[far_spec, FAR],
        out_shape=[
            jax.ShapeDtypeStruct(entries, BF16),
            jax.ShapeDtypeStruct((steps, 8, CHUNK), F32),
        ],
        scratch_shapes=[
            pltpu.VMEM(received.shape, BF16),
            pltpu.VMEM(entries, BF16),
            pltpu.SemaphoreType.DMA((PARTS,)),
            pltpu.SemaphoreType.DMA((PARTS,)),
        ],
        name="entries",
    )(far(received))

    group_sum = pl.pallas_call(
        near_kernel,
        in_specs=[NEAR],
        out_specs=NEAR,
        out_shape=pltpu.VMEM((slab + 8, PIECE), F32),
        compiler_params=PARAMS,
        name="near",
    )(near(spread))

    ahead = []
    for d in range(1, chips // close):
        step = 2 * close * d
        ahead.append(lax.ppermute(group_sum, "seq", [(i, i + step) for i in range(shards - step)]))

    before, normal = pl.pallas_call(
        far_kernel,
        in_specs=[FAR] + [NEAR] * (1 + len(ahead)),
        out_specs=[FAR] * 2,
        out_shape=[
            jax.ShapeDtypeStruct((close, slab, PIECE), F32),
            jax.ShapeDtypeStruct((8, PIECE), F32),
        ],
        compiler_params=pltpu.CompilerParams(vmem_limit_bytes=FAR_LIMIT),
        name="far",
    )(spread, near(first), *(near(a) for a in ahead))

    back = lax.all_to_all(
        before, "seq", split_axis=0, concat_axis=0, tiled=True, axis_index_groups=groups
    )

    keep, lend = pl.pallas_call(
        mix_kernel,
        in_specs=[NEAR] * 3,
        out_specs=[NEAR] * 2,
        out_shape=[pltpu.VMEM((HALF, PIECE), F32)] * 2,
        compiler_params=PARAMS,
        name="mix",
    )(near(back.reshape(HALF, PIECE)), near(first), near(normal))
    came = lax.ppermute(lend, "seq", pairs)

    num, line = pl.pallas_call(
        inside_kernel,
        in_specs=[far_spec, NEAR, far_spec, FAR, FAR],
        out_specs=[NEAR] * 2,
        out_shape=[
            pltpu.VMEM((steps, PIECE, CHUNK), F32),
            pltpu.VMEM((steps, 8, CHUNK), F32),
        ],
        scratch_shapes=[
            pltpu.VMEM(received.shape, BF16),
            pltpu.VMEM(entries, BF16),
            pltpu.SemaphoreType.DMA((2 * PARTS,)),
        ],
        compiler_params=pltpu.CompilerParams(vmem_limit_bytes=INSIDE_LIMIT),
        name="inside",
    )(far(received), near(asked), far(entry), aux, normal)

    return pl.pallas_call(
        finish_kernel,
        in_specs=[pl.BlockSpec(memory_space=pltpu.HBM)] + [NEAR] * 4,
        out_specs=pl.BlockSpec(memory_space=pltpu.HBM),
        out_shape=jax.ShapeDtypeStruct((tokens, PIECE), BF16),
        scratch_shapes=[
            pltpu.VMEM(asked.shape, BF16),
            pltpu.VMEM((tokens, PIECE), BF16),
            pltpu.SemaphoreType.DMA((2,)),
            pltpu.SemaphoreType.DMA((steps // 2,)),
        ],
        compiler_params=PARAMS,
        name="finish",
    )(far(asked), num, line, keep, near(came))


def solution(mesh):
    spec = P(("seq", "head"), None)

    return jax.shard_map(on_device, mesh=mesh, in_specs=(spec,) * 5, out_specs=P("seq", "head"), check_vma=False)
```
